32 devices in a mesh: grp: 2 (over y), band: 4 (over z), sect: 4 (over x, core).
Axes of the slice: x: 2, y: 2, z: 4, core: 2. Of those that a mesh axis runs over, the one named last changes fastest.
Arguments:
- features: bfloat16 [4, 24, 96, 2048], P('grp', 'band', None, 'sect'), parts along dimension 0, may hold values from -16 to 16
- low_level: bfloat16 [4, 24, 96, 256], P('grp', 'band'), parts along dimension 0, may hold values from -6 to 6
- land_mask: int32 [4, 24], P('grp', 'band'), parts along dimension 0, may hold values from 0 to 1, as said below
- weight_one: bfloat16 [2048, 256], P('sect'), may hold values from -0.125 to 0.125
- weight_dilated: bfloat16 [3, 3, 3, 2048, 256], P(None, None, None, 'sect'), may hold values from -0.046875 to 0.046875
- bias_branch: float32 [4, 256], replicated, may hold values from -3 to 3
- weight_pool: bfloat16 [2048, 256], P('sect'), may hold values from -0.125 to 0.125
- bias_pool: float32 [256], replicated, may hold values from -3 to 3
- weight_project: bfloat16 [1280, 256], replicated, may hold values from -0.15625 to 0.15625
- bias_project: float32 [256], replicated, may hold values from -3 to 3
- weight_reduce: bfloat16 [256, 48], replicated, may hold values from -0.375 to 0.375
- bias_reduce: float32 [48], replicated, may hold values from -3 to 3
- weight_merging: bfloat16 [3, 3, 304, 256], replicated, may hold values from -0.109375 to 0.109375
- bias_merging: float32 [256], replicated, may hold values from -3 to 3
Outputs:
- merged_map: bfloat16 [4, 24, 96, 256], P('grp', 'band'), parts along dimension 0
The draws below stay inside these ranges and needn't reach their ends.
There are 2 independent parts, one for each index of `grp`. The reference program is written for one: setup_inputs(seed, part) draws one part's arguments, and reference() takes and returns one part's arrays. A program takes and returns all parts, laid end to end along the dimension named above; an argument that names none is the same for every part. Nothing has to cross between parts.
Inputs may be any that keep to these rules, and one draw needn't show every extreme that they name: `land_mask`: in every image each aligned block of 6 rows holds at most 4 ones and at least 2 ones, its first and last rows always being ones; in every image some block holds exactly 4.
All inputs are finite; a program needn't handle non-finite values.
Results may differ from the reference program's by a relative error of at most 0.012.
Values may be sent and summed in bfloat16 or wider, within the bound.
A program may use at most 64 MiB of HBM per device.

```python
import jax
import jax.numpy as jnp
from jax import lax

C = 2048
BR = 256
LOW = 256
LOWP = 48
DEC = 256
W = 96
MB = 2
R_DEV = 6
ACT_DEV = 4
H = 24
N_SECT = 4


def draw_features(key, part):
    base = jax.random.fold_in(key, 11)
    key_noise, key_mean, key_rows = jax.random.split(base, 3)
    rough = jax.random.normal(key_noise, (MB, H, W, C), jnp.float32)
    channel_mean = jax.random.normal(key_mean, (C,), jnp.float32) * 0.7
    row_ramp = 1.0 + 2.0 * jnp.arange(H, dtype=jnp.float32) / H
    row_factor = row_ramp[None, :] * jax.random.uniform(key_rows, (MB, H), jnp.float32, 0.5, 1.5)
    values = rough + channel_mean[None, None, None, :] * row_factor[:, :, None, None]
    return jnp.clip(values, -16.0, 16.0).astype(jnp.bfloat16)


def draw_land_mask(key, part):
    base = jax.random.fold_in(key, 7)
    key_count, key_full, key_order = jax.random.split(base, 3)
    band_count = H // R_DEV
    counts = jax.random.randint(key_count, (MB, band_count), ACT_DEV - ACT_DEV // 2, ACT_DEV + 1)
    full_band = jax.random.randint(key_full, (MB, 1), 0, band_count)
    counts = jnp.where(jnp.arange(band_count)[None, :] == full_band, ACT_DEV, counts)
    row_index = jnp.arange(R_DEV, dtype=jnp.int32)
    edge_row = (row_index == 0) | (row_index == R_DEV - 1)
    random_part = (jax.random.randint(key_order, (MB, band_count, R_DEV), 0, 2 ** 20) + 1) * R_DEV + row_index[None, None, :]
    scores = jnp.where(edge_row[None, None, :], row_index[None, None, :], random_part)
    rank_of = jnp.argsort(jnp.argsort(scores, axis=2), axis=2)
    land_rows = (rank_of < counts[:, :, None]).astype(jnp.int32)
    return land_rows.reshape(MB, H)


def shard_levels(key, shape, cuts, smallest, top_value):
    def one(position, parts):
        heights = jax.random.uniform(jax.random.fold_in(jax.random.fold_in(key, 6), position), (parts,), jnp.float32, smallest / len(cuts), top_value / len(cuts))
        return jnp.repeat(jnp.exp(heights), shape[position] // parts).reshape((-1,) + (1,) * (len(shape) - position - 1))

    gain = one(*cuts[0])
    for cut in cuts[1:]:
        gain = gain * one(*cut)
    return gain


def gaussian(own_key, shape, width, limit, cuts=(), held_as=jnp.bfloat16):
    array = width * jax.random.normal(own_key, shape, jnp.float32)
    if cuts:
        array = array * shard_levels(own_key, shape, cuts, -0.22, 0.18)
    return jnp.clip(array, -limit, limit).astype(held_as)


def setup_inputs(seed: int = 0, part: int = 0) -> dict:
    key_list = jax.random.split(jax.random.key(seed), 15)
    part_keys = jax.random.split(jax.random.fold_in(key_list[14], part), 15)
    return {
        "features": draw_features(jax.random.fold_in(jax.random.fold_in(key_list[14], part), 71), part),
        "low_level": gaussian(part_keys[1], (MB, H, W, LOW), 1.0, 6.0, ((1, 4),)),
        "land_mask": draw_land_mask(jax.random.fold_in(jax.random.fold_in(key_list[14], part), 71), part),
        "weight_one": gaussian(key_list[3], (C, BR), C ** -0.5, 0.125, ((0, 4),)),
        "weight_dilated": gaussian(key_list[4], (3, 3, 3, C, BR), (9 * C) ** -0.5, 0.046875, ((3, 4),)),
        "bias_branch": gaussian(key_list[5], (4, BR), 0.5, 3.0, (), jnp.float32),
        "weight_pool": gaussian(key_list[6], (C, BR), C ** -0.5, 0.125, ((0, 4),)),
        "bias_pool": gaussian(key_list[7], (BR,), 0.5, 3.0, (), jnp.float32),
        "weight_project": gaussian(key_list[8], (5 * BR, BR), (5 * BR) ** -0.5, 0.15625),
        "bias_project": gaussian(key_list[9], (BR,), 0.5, 3.0, (), jnp.float32),
        "weight_reduce": gaussian(key_list[10], (LOW, LOWP), LOW ** -0.5, 0.375),
        "bias_reduce": gaussian(key_list[11], (LOWP,), 0.5, 3.0, (), jnp.float32),
        "weight_merging": gaussian(key_list[12], (3, 3, BR + LOWP, DEC), (9 * (BR + LOWP)) ** -0.5, 0.109375),
        "bias_merging": gaussian(key_list[13], (DEC,), 0.5, 3.0, (), jnp.float32),
    }


DILATIONS = (12, 24, 36)
PADDING = 36
PRECISE = lax.Precision.HIGHEST


def group_partial(sample_map, weight_one, weight_dilated, first_channel, group_width):
    height, breadth = sample_map.shape[0], sample_map.shape[1]
    section = sample_map[:, :, first_channel:first_channel + group_width]
    padded = jnp.pad(section, ((PADDING, PADDING), (PADDING, PADDING), (0, 0)))
    partials = [jnp.dot(section.reshape(-1, group_width), weight_one[first_channel:first_channel + group_width], preferred_element_type=jnp.float32)]
    for branch_index, dilation in enumerate(DILATIONS):
        running = jnp.zeros((height * breadth, weight_one.shape[1]), jnp.float32)
        for row_tap in range(3):
            for col_tap in range(3):
                top = PADDING + dilation * (row_tap - 1)
                left = PADDING + dilation * (col_tap - 1)
                tap_rows = padded[top:top + height, left:left + breadth].reshape(-1, group_width)
                running = running + jnp.dot(tap_rows, weight_dilated[branch_index, row_tap, col_tap, first_channel:first_channel + group_width], preferred_element_type=jnp.float32)
        partials.append(running)
    return jnp.concatenate(partials, axis=1).astype(jnp.bfloat16)


def reference(features, low_level, land_mask, weight_one, weight_dilated, bias_branch, weight_pool, bias_pool, weight_project, bias_project, weight_reduce, bias_reduce, weight_merging, bias_merging):
    group_width = C // N_SECT
    results = []
    for sample in range(MB):
        sample_map = features[sample]
        pre_branch = jnp.zeros((H * W, 4 * BR), jnp.float32)
        for group_index in range(N_SECT):
            pre_branch = pre_branch + group_partial(sample_map, weight_one, weight_dilated, group_index * group_width, group_width).astype(jnp.float32)
        branch = jax.nn.relu(pre_branch + bias_branch.reshape(-1)).astype(jnp.bfloat16)
        average = jnp.sum(sample_map, axis=(0, 1), dtype=jnp.float32) / (H * W)
        pooled = jax.nn.relu(jnp.dot(average, weight_pool.astype(jnp.float32), precision=PRECISE) + bias_pool)
        context = jnp.dot(pooled, weight_project[4 * BR:].astype(jnp.float32), precision=PRECISE)
        row_keep = land_mask[sample].astype(jnp.float32)
        projected = jnp.dot(branch, weight_project[:4 * BR], preferred_element_type=jnp.float32) + context + bias_project
        project_out = (jax.nn.relu(projected).reshape(H, W, BR) * row_keep[:, None, None]).astype(jnp.bfloat16)
        low_reduced = jax.nn.relu(jnp.dot(low_level[sample].reshape(-1, LOW), weight_reduce, preferred_element_type=jnp.float32) + bias_reduce).astype(jnp.bfloat16).reshape(H, W, LOWP)
        joined = jnp.concatenate([project_out, low_reduced], axis=2)
        framed = jnp.pad(joined, ((1, 1), (1, 1), (0, 0)))
        running = jnp.zeros((H * W, DEC), jnp.float32)
        for row_tap in range(3):
            for col_tap in range(3):
                running = running + jnp.dot(framed[row_tap:row_tap + H, col_tap:col_tap + W].reshape(-1, BR + LOWP), weight_merging[row_tap, col_tap], preferred_element_type=jnp.float32)
        merged_map = (jax.nn.relu(running + bias_merging).reshape(H, W, DEC) * row_keep[:, None, None]).astype(jnp.bfloat16)
        results.append(merged_map)
    return jnp.stack(results)
```

```python
import functools
import types

import jax
import jax.numpy as jnp
from jax import lax
from jax.experimental import pallas as pl
from jax.experimental.pallas import tpu as pltpu
from jax.sharding import PartitionSpec as P

DILATIONS = (12, 24, 36)
LAND_BLOCK = 6
LAND_MOST = 4
MESH = pl.DeviceIdType.MESH
F32 = jnp.float32
BF16 = jnp.bfloat16
ORDER = (3, 2, 0, 1)


def offsets(rows, bands):
    off = []
    for k in (1, 2, 3):
        d = DILATIONS[k - 1]
        assert d % rows == 0
        hop = d // rows
        if hop < bands:
            off.append((k, 0, hop))
            off.append((k, 2, hop))
    return off


def pieces(live):
    inner = live - 2
    cuts = [(0, 2)]
    if inner > 1:
        cuts += [(2, inner - inner // 2), (live - inner // 2, inner // 2)]
    elif inner:
        cuts.append((2, inner))
    return cuts


def kernel(dims, names, *refs):
    r = types.SimpleNamespace(**dict(zip(names, refs, strict=True)))
    mb, rows, cols, ch, br_w, live, nb, ns, low_w, lowp = dims
    nx = ns // 2
    cs = cols // nx
    off = offsets(rows, nb)
    n_off = len(off)
    cuts = pieces(live)
    n_cut = len(cuts)
    off_cuts = [(0, 2), (2, rows - 2)]
    need = [(k, 1) for k in ORDER if k] + [(k, i) for k, i, _ in off]
    pad = (r.m_l.shape[1] - cols) // 2
    scope = jax.named_scope

    band = lax.axis_index("band")
    sect = lax.axis_index("sect")
    core = lax.rem(sect, 2)
    xi = lax.div(sect, 2)
    mine, theirs = core, 1 - core
    peer = xi * 2 + 1 - core

    waits = {}

    def fetch(name, *copies, whole):
        sem = r.loc_sem.at[len(waits)]
        for src, dst in copies:
            pltpu.make_async_copy(src, dst, sem).start()
        waits[name] = pltpu.make_async_copy(whole, whole, sem)

    def need_now(*which):
        for name in which:
            waits[name].wait()

    def taps_of(k, i):
        return r.wd_h.at[k - 1, i], r.wd.at[need.index((k, i))]

    fetch("mask", (r.mask_h, r.mask), whole=r.mask)
    fetch("theirs", (r.feat_h.at[theirs], r.feat.at[0]), whole=r.feat.at[0])
    fetch("first", taps_of(*need[0]), whole=r.wd.at[0])
    fetch("mine", (r.feat_h.at[mine], r.feat_own), whole=r.feat_own)
    fetch(
        "wide", (r.wpool_h, r.wide.at[0]), (r.w1_h, r.wide.at[1]), whole=r.wide
    )
    if n_off:
        fetch("off", *[taps_of(*n) for n in need[3:]], whole=r.wd.at[pl.ds(3, n_off)])
    fetch("rest", *[taps_of(*n) for n in need[1:3]], whole=r.wd.at[pl.ds(1, 2)])
    fetch("low", (r.low_h.at[mine], r.low), whole=r.low)
    fetch("wr", (r.wr_h, r.wr), whole=r.wr)
    fetch("br", (r.br_h, r.br), whole=r.br)
    fetch("wml", (r.wm_h.at[:, :, pl.ds(br_w, lowp)], r.wml), whole=r.wml)
    fetch(
        "vec", (r.bm_h, r.vec.at[0]), (r.bpool_h, r.vec.at[1]), (r.bproj_h, r.vec.at[2]),
        whole=r.vec,
    )
    fetch("wproj", (r.wproj_h, r.wproj), whole=r.wproj)
    fetch("bbr", (r.bbr_h, r.bbr), whole=r.bbr)
    fetch(
        "wmp",
        *[
            (r.wm_h.at[i, j, pl.ds(0, br_w)], r.wmp.at[j, pl.ds(i * br_w, br_w)])
            for i in range(3) for j in range(3)
        ],
        whole=r.wmp,
    )

    bar = pltpu.get_barrier_semaphore()
    up_ok = band >= 1
    dn_ok = band + 1 < nb

    def hello(b, s):
        pl.semaphore_signal(bar, inc=1, device_id={"band": b, "sect": s}, device_id_type=MESH)

    for e in range(1, ns):
        hello(band, lax.rem(sect + e, ns))
    for e in range(1, nb):
        hello(lax.rem(band + e, nb), sect)

    def rcopy(src, dst, s, rs, **where):
        return pltpu.make_async_remote_copy(
            src_ref=src, dst_ref=dst, send_sem=s, recv_sem=rs, device_id=where, device_id_type=MESH
        )

    low_up = rcopy(
        r.low_h.at[mine, 0], r.low_halo.at[1], r.lo_s.at[0], r.lo_r.at[1], band=band - 1, sect=sect
    )
    low_dn = rcopy(
        r.low_h.at[mine, rows - 1], r.low_halo.at[0], r.lo_s.at[1], r.lo_r.at[0],
        band=band + 1, sect=sect,
    )

    def slots(m):
        on = [r.mask[m, y] for y in range(rows)]
        place_of = [0] + [None] * (rows - 2) + [1]
        row_of = [0, rows - 1] + [jnp.int32(0)] * (live - 2)
        count = jnp.int32(0)
        for y in range(1, rows - 1):
            place_of[y] = jnp.where(on[y] > 0, jnp.minimum(count + 2, live - 1), 0)
            for p in range(2, live):
                hit = jnp.logical_and(on[y] > 0, count == p - 2)
                row_of[p] = jnp.where(hit, y, row_of[p])
            count = count + on[y]
        return on, place_of, row_of

    for ref in (r.m_l, r.m_r):
        zero = jnp.zeros((ref.shape[0], pad, br_w), F32)
        ref[:, :pad] = zero
        ref[:, pad + cols :] = zero
    for at in (0, rows + 1):
        r.joined[at] = jnp.zeros((cols, br_w), BF16)

    def taps(lhs, n, wref, d):
        mid = jnp.dot(lhs, wref[1], preferred_element_type=F32).reshape(n, cols, br_w)
        r.m_l[:n, pl.ds(pad, cols)] = jnp.dot(
            lhs, wref[0], preferred_element_type=F32
        ).reshape(n, cols, br_w)
        r.m_r[:n, pl.ds(pad, cols)] = jnp.dot(
            lhs, wref[2], preferred_element_type=F32
        ).reshape(n, cols, br_w)
        return mid + r.m_l[:n, pl.ds(pad - d, cols)] + r.m_r[:n, pl.ds(pad + d, cols)]

    def core_copy(t):
        if t < 4:
            src, dst = r.part_own.at[t, 0], r.crecv_own.at[t]
        else:
            src, dst = r.part_off.at[t - 4, 0], r.crecv_off.at[t - 4]
        return rcopy(src, dst, r.c_s.at[max(t - 3, 0)], r.c_r.at[t], sect=peer)

    def run_of(t, g):
        return cuts[g] if t < 4 else off_cuts[g]

    def x_copy(t, g, e, incoming=False):
        lo, n = run_of(t, g)
        at = g * 2 + t // 3 if t < 4 else 2 * n_cut + (t - 4) * 2 + g
        send, recv, u = (
            (r.xsend_own, r.xrecv_own, t) if t < 4 else (r.xsend_off, r.xrecv_off, t - 4)
        )
        other = lax.rem(xi + e, nx)
        slot = other if incoming else xi
        return rcopy(
            send.at[u, other, pl.ds(lo, n)], recv.at[u, slot, pl.ds(lo, n)],
            r.x_s.at[max(t - 3, 0)], r.x_r.at[at, (e if incoming else nx - e) - 1],
            sect=other * 2 + core,
        )

    def x_arrived(g):
        for e in range(1, nx):
            whole = r.xrecv_own.at[pl.ds(0, 3), lax.rem(xi + e, nx), pl.ds(*cuts[g])]
            arrived(whole, r.x_r.at[g * 2, e - 1])

    def send_x(t, g):
        for e in range(1, nx):
            x_copy(t, g, e).start()

    def first(t, step):
        image = r.feat.at[0] if step == 0 else r.feat_own
        if t < 4:
            k = ORDER[t]
            row_of = facts[step][2]
            lhs = jnp.concatenate([image[row_of[p]] for p in range(live)], axis=0)
            if k:
                val = taps(lhs, live, r.wd.at[need.index((k, 1))], DILATIONS[k - 1])
            else:
                val = jnp.dot(lhs, r.wide[1], preferred_element_type=F32).reshape(live, cols, br_w)
            r.part_own[t, step] = val.astype(BF16)
        else:
            k, i, _ = off[t - 4]
            lhs = image[...].reshape(rows * cols, ch)
            val = taps(lhs, rows, r.wd.at[need.index((k, i))], DILATIONS[k - 1])
            r.part_off[t - 4, step] = val.astype(BF16)

    def second(t):
        core_copy(t).wait_recv()
        for c in range(nx):
            cell = pl.ds(c * cs, cs)
            if t < 4:
                total = r.part_own[t, 1, :, cell].astype(F32) + r.crecv_own[t, :, cell].astype(F32)
                r.xsend_own[t, c] = total.astype(BF16)

                @pl.when(xi == c)
                def _(total=total):
                    r.keep_own[t] = total
            else:
                u = t - 4
                total = r.part_off[u, 1, :, cell].astype(F32) + r.crecv_off[u, :, cell].astype(F32)
                total = jnp.concatenate([total[:1], total[rows - 1 :], total[1 : rows - 1]], axis=0)
                r.xsend_off[u, c] = total.astype(BF16)

                @pl.when(xi == c)
                def _(total=total, u=u):
                    r.keep_off[u] = total

    def sends_to(t):
        k, i, hop = off[t - 4]
        return band + hop < nb if i == 0 else band - hop >= 0

    def gets_from(t):
        k, i, hop = off[t - 4]
        return band - hop >= 0 if i == 0 else band + hop < nb

    def z_copy(t, h):
        k, i, hop = off[t - 4]
        run = pl.ds(*off_cuts[h])
        return rcopy(
            r.zsend.at[t - 4, run], r.zrecv.at[t - 4, run], r.z_s.at[t - 4], r.z_r.at[t - 4, h],
            band=band + hop if i == 0 else band - hop, sect=sect,
        )

    def forward_off(t, h):
        run = pl.ds(*off_cuts[h])
        total = r.keep_off[t - 4, run]
        for e in range(1, nx):
            x_copy(t, h, e, True).wait_recv()
            total = total + r.xrecv_off[t - 4, lax.rem(xi + e, nx), run].astype(F32)
        r.zsend[t - 4, run] = total.astype(BF16)
        z_copy(t, h).start()

    def for_off(fn, *rest):
        for t in range(4, 4 + n_off):
            @pl.when(sends_to(t))
            def _(t=t):
                fn(t, *rest)

    def pool_sect(e, incoming=False):
        other = lax.rem(sect + e, ns)
        slot = other if incoming else sect
        return rcopy(
            r.pool_s.at[sect], r.pool_s.at[slot], r.one_s.at[0], r.one_r.at[0], sect=other
        )

    def pool_band(e, incoming=False):
        other = lax.rem(band + e, nb)
        slot = other if incoming else band
        return rcopy(
            r.pool_b.at[band], r.pool_b.at[slot], r.one_s.at[1], r.one_r.at[1], band=other
        )

    def dot_f32(v, w):
        n = v.shape[0]
        high = v.astype(BF16).astype(F32)
        middle = (v - high).astype(BF16).astype(F32)
        terms = jnp.concatenate([high, middle, v - high - middle], axis=0).astype(BF16)
        p = jnp.dot(terms, w, preferred_element_type=F32)
        return p[:n] + p[n : 2 * n] + p[2 * n :]

    def all_of(ref, n):
        return ref.at[pl.ds(0, n)]

    def arrived(whole, sem):
        pltpu.make_async_copy(whole, whole, sem).wait()

    def pool():
        need_now("wide")
        ones = jnp.ones((8, rows * cols), BF16)
        at = lax.broadcasted_iota(jnp.int32, (8, ch), 0)
        sums = jnp.zeros((8, ch), F32)
        for m, image in ((mine, r.feat_own), (theirs, r.feat.at[0])):
            part = jnp.dot(
                ones, image[...].reshape(rows * cols, ch), preferred_element_type=F32
            )
            sums = jnp.where(at == m, part, sums)
        r.pool_s[sect] = dot_f32(sums, r.wide[0])
        for e in range(1, ns):
            pool_sect(e).start()

    need_now("mask")
    facts = [slots(theirs), slots(mine)]
    on, place_of, row_of = facts[1]

    with scope("w0"):
        need_now("theirs", "first")
    with scope("first0a"):
        first(0, 0)
    with scope("bar"):
        pl.semaphore_wait(bar, (ns - 1) + (nb - 1))
    core_copy(0).start()

    @pl.when(up_ok)
    def _():
        low_up.start()

    @pl.when(dn_ok)
    def _():
        low_dn.start()

    def off_theirs(t):
        first(t, 0)
        core_copy(t).start()

    if n_off:
        need_now("off")
    with scope("offa"):
        for_off(off_theirs)
    need_now("mine")
    with scope("first0b"):
        first(0, 1)
    with scope("pool"):
        pool()
    with scope("second0"):
        second(0)
    for g in range(n_cut):
        send_x(0, g)
    with scope("offb"):
        for_off(first, 1)

    def off_send(t):
        second(t)
        for h in range(2):
            send_x(t, h)

    with scope("offs"):
        for_off(off_send)

    def own_half(t, step):
        with scope(f"first{t}{'ab'[step]}"):
            first(t, step)
        if step == 0:
            core_copy(t).start()

    def own_sum(t):
        with scope(f"second{t}"):
            second(t)
        send_x(t, 0)

    need_now("rest")
    own_half(1, 0)
    own_half(1, 1)
    own_sum(1)
    own_half(2, 0)
    own_half(2, 1)
    own_half(3, 0)
    own_sum(2)
    own_half(3, 1)
    own_sum(3)
    for t in (1, 2):
        for g in range(1, n_cut):
            send_x(t, g)

    with scope("fwd0"):
        for_off(forward_off, 0)

    with scope("low"):
        need_now("low", "wr", "br", "wml", "vec")

        def reduced(v):
            return jax.nn.relu(
                lax.dot_general(
                    v, r.wr[...], (((1,), (1,)), ((), ())), preferred_element_type=F32
                )
                + r.br[...]
            ).astype(BF16)

        r.lowred[1 : rows + 1] = reduced(r.low[...].reshape(rows * cols, low_w)).reshape(
            rows, cols, lowp
        )
        for side, at, ok, copy in ((0, 0, up_ok, low_dn), (1, rows + 1, dn_ok, low_up)):
            @pl.when(ok)
            def _(side=side, at=at, copy=copy):
                copy.wait_recv()
                r.lowred[at] = reduced(r.low_halo[side])

            @pl.when(jnp.logical_not(ok))
            def _(at=at):
                r.lowred[at] = jnp.zeros((cols, lowp), BF16)

    with scope("fwd1"):
        for_off(forward_off, 1)

    with scope("poolb"):
        arrived(all_of(r.pool_s, ns - 1), r.one_r.at[0])
        total = r.pool_s[0]
        for s in range(1, ns):
            total = total + r.pool_s[s]
        r.pool_b[band] = total
    for e in range(1, nb):
        pool_band(e).start()

    def combine(mid, left, right, n):
        r.m_l[:n, pl.ds(pad, cols)] = left.reshape(n, cols, br_w)
        r.m_r[:n, pl.ds(pad, cols)] = right.reshape(n, cols, br_w)
        return (
            mid.reshape(n, cols, br_w)
            + r.m_l[:n, pl.ds(pad - 1, cols)]
            + r.m_r[:n, pl.ds(pad + 1, cols)]
        )

    with scope("lowconv"):
        terms = [None] * 3
        for i in range(3):
            lhs = jnp.concatenate([r.lowred[row_of[p] + i] for p in range(live)], axis=0)
            for j in range(3):
                term = jnp.dot(lhs, r.wml[i, j], preferred_element_type=F32)
                terms[j] = term if i == 0 else terms[j] + term
        r.lowacc[...] = combine(terms[1], terms[0], terms[2], live) + r.vec[0].reshape(1, 1, br_w)

    need_now("wproj", "bbr")
    with scope("ctx"):
        if nb > 1:
            arrived(all_of(r.pool_b, nb - 1), r.one_r.at[1])
        total = r.pool_b[0]
        for b in range(1, nb):
            total = total + r.pool_b[b]
        pooled = jax.nn.relu(total / (nb * rows * cols) + r.vec[1])
        context = dot_f32(pooled, r.wproj[4 * br_w :])
        own = context[0:1]
        for m in range(1, mb):
            own = jnp.where(mine == m, context[m : m + 1], own)
        base = own + r.vec[2]

    def branch(t, g):
        lo, n = cuts[g]
        k = ORDER[t]
        with scope(f"x{t}{g}"):
            if t == 0:
                x_arrived(g)
            if t == 3:
                for e in range(1, nx):
                    x_copy(t, g, e, True).wait_recv()
        for u in range(4, 4 + n_off):
            if off[u - 4][0] == k:
                @pl.when(gets_from(u))
                def _(u=u):
                    with scope(f"z{g}"):
                        if g < 2:
                            z_copy(u, g).wait_recv()
                    for p in range(lo, lo + n):
                        at = p if p < 2 else row_of[p] + 1
                        r.keep_own[t, p] = r.keep_own[t, p] + r.zrecv[u - 4, at].astype(F32)
        total = r.keep_own[t, lo : lo + n]
        for e in range(1, nx):
            total = total + r.xrecv_own[t, lax.rem(xi + e, nx), lo : lo + n].astype(F32)
        total = jax.nn.relu(total + r.bbr[k : k + 1].reshape(1, 1, br_w)).astype(BF16)
        return jnp.dot(
            total.reshape(n * cs, br_w), r.wproj[k * br_w : (k + 1) * br_w],
            preferred_element_type=F32,
        )

    def gather_x(g, e, incoming=False):
        run = pl.ds(*cuts[g])
        other = lax.rem(xi + e, nx)
        slot = other if incoming else xi
        return rcopy(
            r.gath.at[xi, run], r.gath.at[slot, run],
            r.one_s.at[2], r.gx_r.at[g, (e if incoming else nx - e) - 1], sect=other * 2 + core,
        )

    def early(g):
        lo, n = cuts[g]
        acc = branch(0, g)
        for t in (1, 2):
            acc = acc + branch(t, g)
        r.acc[lo : lo + n] = (acc + base).reshape(n, cs, br_w)

    def project(g):
        lo, n = cuts[g]
        last = branch(3, g).reshape(n, cs, br_w)
        done = jax.nn.relu(r.acc[lo : lo + n] + last)
        for p in range(n):
            v = done[p]
            if lo + p < 2:
                v = v * on[(0, rows - 1)[lo + p]].astype(F32)
            r.gath[xi, lo + p] = v.astype(BF16)
        for e in range(1, nx):
            gather_x(g, e).start()

    def halo_copy(side, c):
        return rcopy(
            r.gath.at[c, 1 - side], r.halo.at[side, c], r.h_s.at[side], r.h_r.at[side],
            band=band + 1 if side == 0 else band - 1, sect=sect,
        )

    early(0)
    project(0)
    for g in range(1, n_cut):
        send_x(3, g)
    for g in range(1, n_cut):
        early(g)
    with scope("ga"):
        for e in range(1, nx):
            gather_x(0, e, True).wait_recv()
    for side, ok in ((0, dn_ok), (1, up_ok)):
        @pl.when(ok)
        def _(side=side):
            for c in range(nx):
                halo_copy(side, c).start()
    for p, y in ((0, 0), (1, rows - 1)):
        for c in range(nx):
            r.joined[y + 1, pl.ds(c * cs, cs)] = r.gath[c, p]
    for g in range(1, n_cut):
        project(g)
    need_now("wmp")
    for side, at, ok in ((0, 0, up_ok), (1, rows + 1, dn_ok)):
        @pl.when(ok)
        def _(side=side, at=at):
            with scope("hw"):
                arrived(r.halo.at[side], r.h_r.at[side])
            for c in range(nx):
                r.joined[at, pl.ds(c * cs, cs)] = r.halo[side, c]
    with scope("gb"):
        for g in range(1, n_cut):
            for e in range(1, nx):
                gather_x(g, e, True).wait_recv()
    with scope("join"):
        for y in range(1, rows - 1):
            for c in range(nx):
                r.joined[y + 1, pl.ds(c * cs, cs)] = (
                    r.gath[c, place_of[y]].astype(F32) * on[y].astype(F32)
                ).astype(BF16)

    def merged_copy(h):
        run = pl.ds(*halves[h])
        return rcopy(
            r.merged.at[run], r.merged_in.at[run], r.one_s.at[3], r.one_r.at[2], sect=peer
        )

    halves = [(0, 2), (2, live - 2)]
    for h, (lo, n) in enumerate(halves):
        with scope(f"merge{h}"):
            lhs = jnp.concatenate(
                [
                    jnp.concatenate([r.joined[row_of[p] + i] for p in range(lo, lo + n)], axis=0)
                    for i in range(3)
                ],
                axis=1,
            )
            left, mid, right = [
                jnp.dot(lhs, r.wmp[j], preferred_element_type=F32) for j in range(3)
            ]
            total = combine(mid, left, right, n) + r.lowacc[lo : lo + n]
            r.merged[lo : lo + n] = jax.nn.relu(total).astype(BF16)
        merged_copy(h).start()

    def spread(image, src, flags, places):
        for y in range(rows):
            r.out[image, y] = (src[places[y]].astype(F32) * flags[y].astype(F32)).astype(BF16)

    with scope("spread"):
        spread(mine, r.merged, on, place_of)
    with scope("ow"):
        arrived(r.merged, r.one_r.at[2])
    with scope("spread2"):
        spread(theirs, r.merged_in, facts[0][0], facts[0][1])

    @pl.when(up_ok)
    def _():
        low_up.wait_send()

    @pl.when(dn_ok)
    def _():
        low_dn.wait_send()

    def off_sent(t):
        u = t - 4
        core_copy(t).wait_send()
        if nx > 1:
            arrived(all_of(r.xsend_off.at[u], nx - 1), r.x_s.at[1 + u])
        arrived(r.zsend.at[u], r.z_s.at[u])

    for_off(off_sent)
    arrived(r.part_own.at[:, 0], r.c_s.at[0])
    if nx > 1:
        arrived(r.xsend_own.at[:, pl.ds(0, nx - 1)], r.x_s.at[0])
        arrived(all_of(r.gath, nx - 1), r.one_s.at[2])
    arrived(all_of(r.pool_s, ns - 1), r.one_s.at[0])
    if nb > 1:
        arrived(all_of(r.pool_b, nb - 1), r.one_s.at[1])
    for side, ok in ((0, dn_ok), (1, up_ok)):
        @pl.when(ok)
        def _(side=side):
            arrived(r.halo.at[side], r.h_s.at[side])
    arrived(r.merged, r.one_s.at[3])


def shards(
    features, low_level, land_mask, weight_one, weight_dilated, bias_branch, weight_pool,
    bias_pool, weight_project, bias_project, weight_reduce, bias_reduce, weight_merging,
    bias_merging,
):
    mb, rows, cols, ch = features.shape
    br_w = weight_project.shape[1]
    dec = weight_merging.shape[3]
    low_w, lowp = weight_reduce.shape
    nb, ns = lax.axis_size("band"), lax.axis_size("sect")
    nx = ns // 2
    cs = cols // nx
    assert mb == 2 and ns % 2 == 0 and rows > 2
    live = rows // LAND_BLOCK * LAND_MOST if rows % LAND_BLOCK == 0 else rows
    off = offsets(rows, nb)
    n_off = max(len(off), 1)
    assert dec == br_w
    n_cut = len(pieces(live))
    pad = -(-max(DILATIONS) // 8) * 8
    vm, dma = pltpu.VMEM, pltpu.SemaphoreType.DMA
    dims = (mb, rows, cols, ch, br_w, live, nb, ns, low_w, lowp)
    args = dict(
        mask_h=land_mask, feat_h=features, low_h=low_level, w1_h=weight_one, wd_h=weight_dilated,
        bbr_h=bias_branch, wpool_h=weight_pool, bpool_h=bias_pool.reshape(1, -1),
        wproj_h=weight_project, bproj_h=bias_project.reshape(1, -1), wr_h=weight_reduce.T,
        br_h=bias_reduce.reshape(1, -1), wm_h=weight_merging, bm_h=bias_merging.reshape(1, -1),
    )
    scratch = dict(
        mask=pltpu.SMEM(land_mask.shape, jnp.int32),
        feat=vm((1, rows, cols, ch), BF16),
        feat_own=vm((rows, cols, ch), BF16),
        low=vm((rows, cols, low_w), BF16),
        low_halo=vm((2, cols, low_w), BF16),
        wide=vm((2, ch, br_w), BF16),
        wd=vm((3 + len(off), 3, ch, br_w), BF16),
        wproj=vm(weight_project.shape, BF16),
        wmp=vm((3, 3 * br_w, dec), BF16),
        wml=vm((3, 3, lowp, dec), BF16),
        wr=vm((lowp, low_w), BF16),
        br=vm((1, lowp), F32),
        vec=vm((3, 1, br_w), F32),
        bbr=vm(bias_branch.shape, F32),
        m_l=vm((rows, cols + 2 * pad, br_w), F32),
        m_r=vm((rows, cols + 2 * pad, br_w), F32),
        part_off=vm((n_off, 2, rows, cols, br_w), BF16),
        crecv_off=vm((n_off, rows, cols, br_w), BF16),
        xsend_off=vm((n_off, nx, rows, cs, br_w), BF16),
        xrecv_off=vm((n_off, nx, rows, cs, br_w), BF16),
        zsend=vm((n_off, rows, cs, br_w), BF16),
        zrecv=vm((n_off, rows, cs, br_w), BF16),
        keep_off=vm((n_off, rows, cs, br_w), F32),
        part_own=vm((4, 2, live, cols, br_w), BF16),
        crecv_own=vm((4, live, cols, br_w), BF16),
        xsend_own=vm((4, nx, live, cs, br_w), BF16),
        xrecv_own=vm((4, nx, live, cs, br_w), BF16),
        keep_own=vm((4, live, cs, br_w), F32),
        acc=vm((live, cs, br_w), F32),
        pool_s=vm((ns, 8, br_w), F32),
        pool_b=vm((nb, 8, br_w), F32),
        gath=vm((nx, live, cs, br_w), BF16),
        halo=vm((2, nx, cs, br_w), BF16),
        joined=vm((rows + 2, cols, br_w), BF16),
        lowred=vm((rows + 2, cols, lowp), BF16),
        lowacc=vm((live, cols, dec), F32),
        merged=vm((live, cols, dec), BF16),
        merged_in=vm((live, cols, dec), BF16),
        loc_sem=dma((15,)),
        one_s=dma((4,)),
        one_r=dma((3,)),
        lo_s=dma((2,)),
        lo_r=dma((2,)),
        c_s=dma((1 + n_off,)),
        c_r=dma((4 + n_off,)),
        x_s=dma((1 + n_off,)),
        x_r=dma((2 * n_cut + 2 * n_off, max(nx - 1, 1))),
        z_s=dma((n_off,)),
        z_r=dma((n_off, 2)),
        gx_r=dma((n_cut, max(nx - 1, 1))),
        h_s=dma((2,)),
        h_r=dma((2,)),
    )
    names = (*args, "out", *scratch)
    merged_map = pl.pallas_call(
        functools.partial(kernel, dims, names),
        out_shape=jax.ShapeDtypeStruct((mb, rows, cols, dec), BF16),
        in_specs=[pl.BlockSpec(memory_space=pltpu.HBM)] * len(args),
        out_specs=pl.BlockSpec(memory_space=pltpu.VMEM),
        scratch_shapes=list(scratch.values()),
        compiler_params=pltpu.CompilerParams(
            collective_id=0, has_side_effects=True, vmem_limit_bytes=48 * 1024 * 1024
        ),
    )(*[pltpu.with_memory_space_constraint(a, pltpu.HBM) for a in args.values()])
    return jnp.maximum(merged_map, jnp.zeros_like(merged_map))


def solution(mesh):
    in_specs = (
        P("grp", "band", None, "sect"),
        P("grp", "band", None, None),
        P("grp", "band"),
        P("sect", None),
        P(None, None, None, "sect", None),
        P(),
        P("sect", None),
        P(),
        P(),
        P(),
        P(),
        P(),
        P(),
        P(),
    )
    out_specs = P("grp", "band", None, None)
    return jax.shard_map(shards, mesh=mesh, in_specs=in_specs, out_specs=out_specs, check_vma=False)
```

```python
import functools
import types

import jax
import jax.numpy as jnp
from jax import lax
from jax.experimental import pallas as pl
from jax.experimental.pallas import tpu as pltpu
from jax.sharding import PartitionSpec as P

DILATIONS = (12, 24, 36)
LAND_BLOCK = 6
LAND_MOST = 4
MESH = pl.DeviceIdType.MESH
F32 = jnp.float32
BF16 = jnp.bfloat16
ORDER = (0, 3, 2, 1)


def offsets(rows, bands):
    off = []
    for k in (1, 2, 3):
        d = DILATIONS[k - 1]
        assert d % rows == 0
        hop = d // rows
        if hop < bands:
            off.append((k, 0, hop))
            off.append((k, 2, hop))
    return off


def pieces(live):
    inner = live - 2
    cuts = [(0, 2)]
    if inner > 1:
        cuts += [(2, inner - inner // 2), (live - inner // 2, inner // 2)]
    elif inner:
        cuts.append((2, inner))
    return cuts


def kernel(dims, names, *refs):
    r = types.SimpleNamespace(**dict(zip(names, refs, strict=True)))
    mb, rows, cols, ch, br_w, live, nb, ns, low_w, lowp = dims
    nx = ns // 2
    cs = cols // nx
    off = offsets(rows, nb)
    n_off = len(off)
    cuts = pieces(live)
    n_cut = len(cuts)
    off_cuts = [(0, 2), (2, live - 2)]
    need = [(k, 1) for k in ORDER if k] + [(k, i) for k, i, _ in off]
    pad = (r.m_l.shape[1] - cols) // 2
    scope = jax.named_scope

    band = lax.axis_index("band")
    sect = lax.axis_index("sect")
    core = lax.rem(sect, 2)
    xi = lax.div(sect, 2)
    mine, theirs = core, 1 - core
    peer = xi * 2 + 1 - core

    waits = {}

    def fetch(name, *copies, whole):
        sem = r.loc_sem.at[len(waits)]
        for src, dst in copies:
            pltpu.make_async_copy(src, dst, sem).start()
        waits[name] = pltpu.make_async_copy(whole, whole, sem)

    def need_now(*which):
        for name in which:
            waits[name].wait()

    def taps_of(k, i):
        return r.wd_h.at[k - 1, i], r.wd.at[need.index((k, i))]

    fetch("mask", (r.mask_h, r.mask), whole=r.mask)
    fetch("theirs", (r.feat_h.at[theirs], r.feat.at[0]), whole=r.feat.at[0])
    fetch("w1", (r.w1_h, r.w1), whole=r.w1)
    fetch("mine", (r.feat_h.at[mine], r.feat_own), whole=r.feat_own)
    fetch("wpool", (r.wpool_h, r.wpool), whole=r.wpool)
    if n_off:
        fetch("off", *[taps_of(*n) for n in need[3:]], whole=r.wd.at[pl.ds(3, n_off)])
    fetch("taps0", taps_of(*need[0]), whole=r.wd.at[0])
    fetch("taps1", *[taps_of(*n) for n in need[1:3]], whole=r.wd.at[pl.ds(1, 2)])
    fetch("low", (r.low_h.at[mine], r.low), whole=r.low)
    fetch("wr", (r.wr_h, r.wr), whole=r.wr)
    fetch("br", (r.br_h, r.br), whole=r.br)
    fetch("wml", (r.wm_h.at[:, :, pl.ds(br_w, lowp)], r.wml), whole=r.wml)
    fetch(
        "vec", (r.bm_h, r.vec.at[0]), (r.bpool_h, r.vec.at[1]), (r.bproj_h, r.vec.at[2]),
        whole=r.vec,
    )
    fetch("wproj", (r.wproj_h, r.wproj), whole=r.wproj)
    fetch("bbr", (r.bbr_h, r.bbr), whole=r.bbr)
    fetch(
        "wmp",
        *[
            (r.wm_h.at[i, j, pl.ds(0, br_w)], r.wmp.at[j, pl.ds(i * br_w, br_w)])
            for i in range(3) for j in range(3)
        ],
        whole=r.wmp,
    )

    bar = pltpu.get_barrier_semaphore()
    up_ok = band >= 1
    dn_ok = band + 1 < nb

    def hello(b, s):
        pl.semaphore_signal(bar, inc=1, device_id={"band": b, "sect": s}, device_id_type=MESH)

    for e in range(1, ns):
        hello(band, lax.rem(sect + e, ns))
    for e in range(1, nb):
        hello(lax.rem(band + e, nb), sect)

    def rcopy(src, dst, s, rs, **where):
        return pltpu.make_async_remote_copy(
            src_ref=src, dst_ref=dst, send_sem=s, recv_sem=rs, device_id=where, device_id_type=MESH
        )

    low_up = rcopy(
        r.low_h.at[mine, 0], r.low_halo.at[1], r.lo_s.at[0], r.lo_r.at[1], band=band - 1, sect=sect
    )
    low_dn = rcopy(
        r.low_h.at[mine, rows - 1], r.low_halo.at[0], r.lo_s.at[1], r.lo_r.at[0],
        band=band + 1, sect=sect,
    )

    def slots(m):
        on = [r.mask[m, y] for y in range(rows)]
        place_of = [0] + [None] * (rows - 2) + [1]
        row_of = [0, rows - 1] + [jnp.int32(0)] * (live - 2)
        hits = {}
        count = jnp.int32(0)
        for y in range(1, rows - 1):
            place_of[y] = jnp.where(on[y] > 0, jnp.minimum(count + 2, live - 1), 0)
            for p in range(2, live):
                hit = jnp.logical_and(on[y] > 0, count == p - 2)
                row_of[p] = jnp.where(hit, y, row_of[p])
                hits[p, y] = jnp.where(hit, 1, 0)
            count = count + on[y]
        return on, place_of, row_of, hits

    for ref in (r.m_l, r.m_r):
        zero = jnp.zeros((ref.shape[0], pad, br_w), F32)
        ref[:, :pad] = zero
        ref[:, pad + cols :] = zero
    for at in (0, rows + 1):
        r.joined[at] = jnp.zeros((cols, br_w), BF16)

    def taps(lhs, n, wref, d):
        mid = jnp.dot(lhs, wref[1], preferred_element_type=F32).reshape(n, cols, br_w)
        r.m_l[:n, pl.ds(pad, cols)] = jnp.dot(
            lhs, wref[0], preferred_element_type=F32
        ).reshape(n, cols, br_w)
        r.m_r[:n, pl.ds(pad, cols)] = jnp.dot(
            lhs, wref[2], preferred_element_type=F32
        ).reshape(n, cols, br_w)
        return mid + r.m_l[:n, pl.ds(pad - d, cols)] + r.m_r[:n, pl.ds(pad + d, cols)]

    def core_copy(t):
        if t < 4:
            src, dst = r.part_own.at[t, 0], r.crecv_own.at[t]
        else:
            src, dst = r.part_off.at[t - 4, 0], r.crecv_off.at[t - 4]
        return rcopy(src, dst, r.c_s.at[max(t - 3, 0)], r.c_r.at[t], sect=peer)

    def run_of(t, g):
        return cuts[g] if t < 4 else off_cuts[g]

    def x_copy(t, g, e, incoming=False):
        lo, n = run_of(t, g)
        at = g * 2 + t // 3 if t < 4 else 2 * n_cut + (t - 4) * 2 + g
        send, recv, u = (
            (r.xsend_own, r.xrecv_own, t) if t < 4 else (r.xsend_off, r.xrecv_off, t - 4)
        )
        other = lax.rem(xi + e, nx)
        slot = other if incoming else xi
        return rcopy(
            send.at[u, other, pl.ds(lo, n)], recv.at[u, slot, pl.ds(lo, n)],
            r.x_s.at[max(t - 3, 0)], r.x_r.at[at, (e if incoming else nx - e) - 1],
            sect=other * 2 + core,
        )

    def x_arrived(g):
        for e in range(1, nx):
            whole = r.xrecv_own.at[pl.ds(0, 3), lax.rem(xi + e, nx), pl.ds(*cuts[g])]
            arrived(whole, r.x_r.at[g * 2, e - 1])

    def send_x(t, g):
        for e in range(1, nx):
            x_copy(t, g, e).start()

    def first(t, step):
        image = r.feat.at[0] if step == 0 else r.feat_own
        if t < 4:
            k = ORDER[t]
            row_of = facts[step][2]
            lhs = jnp.concatenate([image[row_of[p]] for p in range(live)], axis=0)
            if k:
                val = taps(lhs, live, r.wd.at[need.index((k, 1))], DILATIONS[k - 1])
            else:
                val = jnp.dot(lhs, r.w1[...], preferred_element_type=F32).reshape(live, cols, br_w)
            r.part_own[t, step] = val.astype(BF16)
        else:
            k, i, _ = off[t - 4]
            lhs = image[...].reshape(rows * cols, ch)
            val = taps(lhs, rows, r.wd.at[need.index((k, i))], DILATIONS[k - 1])
            r.part_off[t - 4, step] = val.astype(BF16)

    def second(t):
        core_copy(t).wait_recv()
        for c in range(nx):
            cell = pl.ds(c * cs, cs)
            total = r.part_own[t, 1, :, cell].astype(F32) + r.crecv_own[t, :, cell].astype(F32)
            r.xsend_own[t, c] = total.astype(BF16)

            @pl.when(xi == c)
            def _(total=total):
                r.keep_own[t] = total

    def second_off(t, h):
        u = t - 4
        if h == 0:
            core_copy(t).wait_recv()
        else:
            sel_copy(t).wait_recv()
        lo, n = off_cuts[h]
        for c in range(nx):
            cell = pl.ds(c * cs, cs)

            def row(y, cell=cell):
                return r.part_off[u, 1, y, cell].astype(F32) + r.crecv_off[u, y, cell].astype(F32)

            if h == 0:
                picked = [row(0), row(rows - 1)]
            else:
                inner = [row(y) for y in range(1, rows - 1)]
                picked = []
                for p in range(2, live):
                    total = jnp.zeros((cs, br_w), F32)
                    for y in range(1, rows - 1):
                        at = (p - 2) * (rows - 2) + y - 1
                        total = total + inner[y - 1] * r.sel_in[u, at : at + 1]
                    picked.append(total)
            for p, total in enumerate(picked):
                r.xsend_off[u, c, lo + p] = total.astype(BF16)

            @pl.when(xi == c)
            def _(picked=picked):
                for p, total in enumerate(picked):
                    r.keep_off[u, lo + p] = total

    def sends_to(t):
        k, i, hop = off[t - 4]
        return band + hop < nb if i == 0 else band - hop >= 0

    def gets_from(t):
        k, i, hop = off[t - 4]
        return band - hop >= 0 if i == 0 else band + hop < nb

    def sel_copy(t):
        k, i, hop = off[t - 4]
        return rcopy(
            r.sel_out, r.sel_in.at[t - 4], r.s_s.at[t - 4], r.s_r.at[t - 4],
            band=band - hop if i == 0 else band + hop, sect=sect,
        )

    def z_copy(t, h):
        k, i, hop = off[t - 4]
        run = pl.ds(*off_cuts[h])
        return rcopy(
            r.zsend.at[t - 4, run], r.zrecv.at[t - 4, run], r.z_s.at[t - 4], r.z_r.at[t - 4, h],
            band=band + hop if i == 0 else band - hop, sect=sect,
        )

    def forward_off(t, h):
        run = pl.ds(*off_cuts[h])
        total = r.keep_off[t - 4, run]
        for e in range(1, nx):
            x_copy(t, h, e, True).wait_recv()
            total = total + r.xrecv_off[t - 4, lax.rem(xi + e, nx), run].astype(F32)
        r.zsend[t - 4, run] = total.astype(BF16)
        z_copy(t, h).start()

    def for_off(fn, *rest):
        for t in range(4, 4 + n_off):
            @pl.when(sends_to(t))
            def _(t=t):
                fn(t, *rest)

    def pool_sect(e, incoming=False):
        other = lax.rem(sect + e, ns)
        slot = other if incoming else sect
        return rcopy(
            r.pool_s.at[sect], r.pool_s.at[slot], r.one_s.at[0], r.one_r.at[0], sect=other
        )

    def pool_band(e, incoming=False):
        other = lax.rem(band + e, nb)
        slot = other if incoming else band
        return rcopy(
            r.pool_b.at[band], r.pool_b.at[slot], r.one_s.at[1], r.one_r.at[1], band=other
        )

    def dot_f32(v, w):
        n = v.shape[0]
        high = v.astype(BF16).astype(F32)
        middle = (v - high).astype(BF16).astype(F32)
        terms = jnp.concatenate([high, middle, v - high - middle], axis=0).astype(BF16)
        p = jnp.dot(terms, w, preferred_element_type=F32)
        return p[:n] + p[n : 2 * n] + p[2 * n :]

    def all_of(ref, n):
        return ref.at[pl.ds(0, n)]

    def arrived(whole, sem):
        pltpu.make_async_copy(whole, whole, sem).wait()

    def pool():
        need_now("wpool")
        ones = jnp.ones((8, rows * cols), BF16)
        at = lax.broadcasted_iota(jnp.int32, (8, ch), 0)
        sums = jnp.zeros((8, ch), F32)
        for m, image in ((mine, r.feat_own), (theirs, r.feat.at[0])):
            part = jnp.dot(
                ones, image[...].reshape(rows * cols, ch), preferred_element_type=F32
            )
            sums = jnp.where(at == m, part, sums)
        r.pool_s[sect] = dot_f32(sums, r.wpool[...])[:mb]
        for e in range(1, ns):
            pool_sect(e).start()

    need_now("mask")
    facts = [slots(theirs), slots(mine)]
    on, place_of, row_of, hits = facts[1]

    for p in range(2, live):
        for y in range(1, rows - 1):
            at = (p - 2) * (rows - 2) + y - 1
            r.sel_out[at : at + 1] = jnp.full((1, br_w), hits[p, y].astype(F32))

    def own_half(t, step):
        with scope(f"first{t}{'ab'[step]}"):
            first(t, step)
        if step == 0:
            core_copy(t).start()

    def off_theirs(t):
        first(t, 0)
        core_copy(t).start()

    def off_send(t, h):
        second_off(t, h)
        send_x(t, h)

    with scope("w0"):
        need_now("theirs", "w1")
    with scope("first0a"):
        first(0, 0)
    with scope("bar"):
        pl.semaphore_wait(bar, (ns - 1) + (nb - 1))
    core_copy(0).start()
    for t in range(4, 4 + n_off):
        @pl.when(gets_from(t))
        def _(t=t):
            sel_copy(t).start()

    @pl.when(up_ok)
    def _():
        low_up.start()

    @pl.when(dn_ok)
    def _():
        low_dn.start()

    need_now("mine")
    own_half(0, 1)
    with scope("pool"):
        pool()
    if n_off:
        need_now("off")
    with scope("offa"):
        for_off(off_theirs)
    with scope("second0"):
        second(0)
    for g in range(n_cut):
        send_x(0, g)
    with scope("offb"):
        for_off(first, 1)
    with scope("offs0"):
        for_off(off_send, 0)
    need_now("taps0")
    own_half(1, 0)
    own_half(1, 1)
    with scope("second1"):
        second(1)
    send_x(1, 0)
    with scope("offs1"):
        for_off(off_send, 1)
    need_now("taps1")
    own_half(2, 0)
    own_half(2, 1)
    own_half(3, 0)
    with scope("second2"):
        second(2)
    send_x(2, 0)
    with scope("poolb"):
        arrived(all_of(r.pool_s, ns - 1), r.one_r.at[0])
        total = r.pool_s[0]
        for s in range(1, ns):
            total = total + r.pool_s[s]
        r.pool_b[band] = total
    for e in range(1, nb):
        pool_band(e).start()
    own_half(3, 1)
    with scope("second3"):
        second(3)
    send_x(3, 0)
    for t in (1, 2):
        for g in range(1, n_cut):
            send_x(t, g)

    with scope("fwd0"):
        for_off(forward_off, 0)

    with scope("low"):
        need_now("low", "wr", "br", "wml", "vec")

        def reduced(v):
            return jax.nn.relu(
                lax.dot_general(
                    v, r.wr[...], (((1,), (1,)), ((), ())), preferred_element_type=F32
                )
                + r.br[...]
            ).astype(BF16)

        r.lowred[1 : rows + 1] = reduced(r.low[...].reshape(rows * cols, low_w)).reshape(
            rows, cols, lowp
        )
        for side, at, ok, copy in ((0, 0, up_ok, low_dn), (1, rows + 1, dn_ok, low_up)):
            @pl.when(ok)
            def _(side=side, at=at, copy=copy):
                copy.wait_recv()
                r.lowred[at] = reduced(r.low_halo[side])

            @pl.when(jnp.logical_not(ok))
            def _(at=at):
                r.lowred[at] = jnp.zeros((cols, lowp), BF16)

    with scope("fwd1"):
        for_off(forward_off, 1)

    def combine(mid, left, right, n):
        r.m_l[:n, pl.ds(pad, cols)] = left.reshape(n, cols, br_w)
        r.m_r[:n, pl.ds(pad, cols)] = right.reshape(n, cols, br_w)
        return (
            mid.reshape(n, cols, br_w)
            + r.m_l[:n, pl.ds(pad - 1, cols)]
            + r.m_r[:n, pl.ds(pad + 1, cols)]
        )

    with scope("lowconv"):
        terms = [None] * 3
        for i in range(3):
            lhs = jnp.concatenate([r.lowred[row_of[p] + i] for p in range(live)], axis=0)
            for j in range(3):
                term = jnp.dot(lhs, r.wml[i, j], preferred_element_type=F32)
                terms[j] = term if i == 0 else terms[j] + term
        r.lowacc[...] = combine(terms[1], terms[0], terms[2], live) + r.vec[0].reshape(1, 1, br_w)

    need_now("wproj", "bbr")
    with scope("ctx"):
        if nb > 1:
            arrived(all_of(r.pool_b, nb - 1), r.one_r.at[1])
        total = r.pool_b[0]
        for b in range(1, nb):
            total = total + r.pool_b[b]
        pooled = jax.nn.relu(total / (nb * rows * cols) + r.vec[1])
        context = dot_f32(pooled, r.wproj[4 * br_w :])
        own = context[0:1]
        for m in range(1, mb):
            own = jnp.where(mine == m, context[m : m + 1], own)
        base = own + r.vec[2]

    def branch(t, g):
        lo, n = cuts[g]
        k = ORDER[t]
        with scope(f"x{t}{g}"):
            if t == 0:
                x_arrived(g)
            if t == 3:
                for e in range(1, nx):
                    x_copy(t, g, e, True).wait_recv()
        for u in range(4, 4 + n_off):
            if off[u - 4][0] == k:
                @pl.when(gets_from(u))
                def _(u=u):
                    with scope(f"z{g}"):
                        if g < 2:
                            z_copy(u, g).wait_recv()
                    run = pl.ds(lo, n)
                    r.keep_own[t, run] = r.keep_own[t, run] + r.zrecv[u - 4, run].astype(F32)
        total = r.keep_own[t, lo : lo + n]
        for e in range(1, nx):
            total = total + r.xrecv_own[t, lax.rem(xi + e, nx), lo : lo + n].astype(F32)
        total = jax.nn.relu(total + r.bbr[k : k + 1].reshape(1, 1, br_w)).astype(BF16)
        return jnp.dot(
            total.reshape(n * cs, br_w), r.wproj[k * br_w : (k + 1) * br_w],
            preferred_element_type=F32,
        )

    def gather_x(g, e, incoming=False):
        run = pl.ds(*cuts[g])
        other = lax.rem(xi + e, nx)
        slot = other if incoming else xi
        return rcopy(
            r.gath.at[xi, run], r.gath.at[slot, run],
            r.one_s.at[2], r.gx_r.at[g, (e if incoming else nx - e) - 1], sect=other * 2 + core,
        )

    def early(g):
        lo, n = cuts[g]
        acc = branch(0, g)
        for t in (1, 2):
            acc = acc + branch(t, g)
        r.acc[lo : lo + n] = (acc + base).reshape(n, cs, br_w)

    def project(g):
        lo, n = cuts[g]
        last = branch(3, g).reshape(n, cs, br_w)
        done = jax.nn.relu(r.acc[lo : lo + n] + last)
        for p in range(n):
            v = done[p]
            if lo + p < 2:
                v = v * on[(0, rows - 1)[lo + p]].astype(F32)
            r.gath[xi, lo + p] = v.astype(BF16)
        for e in range(1, nx):
            gather_x(g, e).start()

    def halo_copy(side, c):
        return rcopy(
            r.gath.at[c, 1 - side], r.halo.at[side, c], r.h_s.at[side], r.h_r.at[side],
            band=band + 1 if side == 0 else band - 1, sect=sect,
        )

    early(0)
    project(0)
    for g in range(1, n_cut):
        send_x(3, g)
    for g in range(1, n_cut):
        early(g)
    with scope("ga"):
        for e in range(1, nx):
            gather_x(0, e, True).wait_recv()
    for side, ok in ((0, dn_ok), (1, up_ok)):
        @pl.when(ok)
        def _(side=side):
            for c in range(nx):
                halo_copy(side, c).start()
    for p, y in ((0, 0), (1, rows - 1)):
        for c in range(nx):
            r.joined[y + 1, pl.ds(c * cs, cs)] = r.gath[c, p]
    for g in range(1, n_cut):
        project(g)
    need_now("wmp")
    for side, at, ok in ((0, 0, up_ok), (1, rows + 1, dn_ok)):
        @pl.when(ok)
        def _(side=side, at=at):
            with scope("hw"):
                arrived(r.halo.at[side], r.h_r.at[side])
            for c in range(nx):
                r.joined[at, pl.ds(c * cs, cs)] = r.halo[side, c]
    with scope("gb"):
        for g in range(1, n_cut):
            for e in range(1, nx):
                gather_x(g, e, True).wait_recv()
    with scope("join"):
        for y in range(1, rows - 1):
            for c in range(nx):
                r.joined[y + 1, pl.ds(c * cs, cs)] = (
                    r.gath[c, place_of[y]].astype(F32) * on[y].astype(F32)
                ).astype(BF16)

    def merged_copy(h):
        run = pl.ds(*halves[h])
        return rcopy(
            r.merged.at[run], r.merged_in.at[run], r.one_s.at[3], r.one_r.at[2], sect=peer
        )

    halves = [(0, 2), (2, live - 2)]
    for h, (lo, n) in enumerate(halves):
        with scope(f"merge{h}"):
            lhs = jnp.concatenate(
                [
                    jnp.concatenate([r.joined[row_of[p] + i] for p in range(lo, lo + n)], axis=0)
                    for i in range(3)
                ],
                axis=1,
            )
            left, mid, right = [
                jnp.dot(lhs, r.wmp[j], preferred_element_type=F32) for j in range(3)
            ]
            total = combine(mid, left, right, n) + r.lowacc[lo : lo + n]
            r.merged[lo : lo + n] = jax.nn.relu(total).astype(BF16)
        merged_copy(h).start()

    def spread(image, src, flags, places):
        for y in range(rows):
            r.out[image, y] = (src[places[y]].astype(F32) * flags[y].astype(F32)).astype(BF16)

    with scope("spread"):
        spread(mine, r.merged, on, place_of)
    with scope("ow"):
        arrived(r.merged, r.one_r.at[2])
    with scope("spread2"):
        spread(theirs, r.merged_in, facts[0][0], facts[0][1])

    @pl.when(up_ok)
    def _():
        low_up.wait_send()

    @pl.when(dn_ok)
    def _():
        low_dn.wait_send()

    def off_sent(t):
        u = t - 4
        core_copy(t).wait_send()
        if nx > 1:
            arrived(all_of(r.xsend_off.at[u], nx - 1), r.x_s.at[1 + u])
        arrived(r.zsend.at[u], r.z_s.at[u])

    for t in range(4, 4 + n_off):
        @pl.when(gets_from(t))
        def _(t=t):
            sel_copy(t).wait_send()
    for_off(off_sent)
    arrived(r.part_own.at[:, 0], r.c_s.at[0])
    if nx > 1:
        arrived(r.xsend_own.at[:, pl.ds(0, nx - 1)], r.x_s.at[0])
        arrived(all_of(r.gath, nx - 1), r.one_s.at[2])
    arrived(all_of(r.pool_s, ns - 1), r.one_s.at[0])
    if nb > 1:
        arrived(all_of(r.pool_b, nb - 1), r.one_s.at[1])
    for side, ok in ((0, dn_ok), (1, up_ok)):
        @pl.when(ok)
        def _(side=side):
            arrived(r.halo.at[side], r.h_s.at[side])
    arrived(r.merged, r.one_s.at[3])


def shards(
    features, low_level, land_mask, weight_one, weight_dilated, bias_branch, weight_pool,
    bias_pool, weight_project, bias_project, weight_reduce, bias_reduce, weight_merging,
    bias_merging,
):
    mb, rows, cols, ch = features.shape
    br_w = weight_project.shape[1]
    dec = weight_merging.shape[3]
    low_w, lowp = weight_reduce.shape
    nb, ns = lax.axis_size("band"), lax.axis_size("sect")
    nx = ns // 2
    cs = cols // nx
    assert mb == 2 and ns % 2 == 0 and rows > 2
    live = rows // LAND_BLOCK * LAND_MOST if rows % LAND_BLOCK == 0 else rows
    off = offsets(rows, nb)
    n_off = max(len(off), 1)
    assert dec == br_w
    n_cut = len(pieces(live))
    n_sel = -(-(live - 2) * (rows - 2) // 8) * 8
    pad = -(-max(DILATIONS) // 8) * 8
    vm, dma = pltpu.VMEM, pltpu.SemaphoreType.DMA
    dims = (mb, rows, cols, ch, br_w, live, nb, ns, low_w, lowp)
    args = dict(
        mask_h=land_mask, feat_h=features, low_h=low_level, w1_h=weight_one, wd_h=weight_dilated,
        bbr_h=bias_branch, wpool_h=weight_pool, bpool_h=bias_pool.reshape(1, -1),
        wproj_h=weight_project, bproj_h=bias_project.reshape(1, -1), wr_h=weight_reduce.T,
        br_h=bias_reduce.reshape(1, -1), wm_h=weight_merging, bm_h=bias_merging.reshape(1, -1),
    )
    scratch = dict(
        mask=pltpu.SMEM(land_mask.shape, jnp.int32),
        feat=vm((1, rows, cols, ch), BF16),
        feat_own=vm((rows, cols, ch), BF16),
        low=vm((rows, cols, low_w), BF16),
        low_halo=vm((2, cols, low_w), BF16),
        w1=vm(weight_one.shape, BF16),
        wpool=vm(weight_pool.shape, BF16),
        sel_out=vm((n_sel, br_w), F32),
        sel_in=vm((n_off, n_sel, br_w), F32),
        wd=vm((3 + len(off), 3, ch, br_w), BF16),
        wproj=vm(weight_project.shape, BF16),
        wmp=vm((3, 3 * br_w, dec), BF16),
        wml=vm((3, 3, lowp, dec), BF16),
        wr=vm((lowp, low_w), BF16),
        br=vm((1, lowp), F32),
        vec=vm((3, 1, br_w), F32),
        bbr=vm(bias_branch.shape, F32),
        m_l=vm((rows, cols + 2 * pad, br_w), F32),
        m_r=vm((rows, cols + 2 * pad, br_w), F32),
        part_off=vm((n_off, 2, rows, cols, br_w), BF16),
        crecv_off=vm((n_off, rows, cols, br_w), BF16),
        xsend_off=vm((n_off, nx, live, cs, br_w), BF16),
        xrecv_off=vm((n_off, nx, live, cs, br_w), BF16),
        zsend=vm((n_off, live, cs, br_w), BF16),
        zrecv=vm((n_off, live, cs, br_w), BF16),
        keep_off=vm((n_off, live, cs, br_w), F32),
        part_own=vm((4, 2, live, cols, br_w), BF16),
        crecv_own=vm((4, live, cols, br_w), BF16),
        xsend_own=vm((4, nx, live, cs, br_w), BF16),
        xrecv_own=vm((4, nx, live, cs, br_w), BF16),
        keep_own=vm((4, live, cs, br_w), F32),
        acc=vm((live, cs, br_w), F32),
        pool_s=vm((ns, mb, br_w), F32),
        pool_b=vm((nb, mb, br_w), F32),
        gath=vm((nx, live, cs, br_w), BF16),
        halo=vm((2, nx, cs, br_w), BF16),
        joined=vm((rows + 2, cols, br_w), BF16),
        lowred=vm((rows + 2, cols, lowp), BF16),
        lowacc=vm((live, cols, dec), F32),
        merged=vm((live, cols, dec), BF16),
        merged_in=vm((live, cols, dec), BF16),
        loc_sem=dma((16,)),
        one_s=dma((4,)),
        one_r=dma((3,)),
        lo_s=dma((2,)),
        lo_r=dma((2,)),
        c_s=dma((1 + n_off,)),
        c_r=dma((4 + n_off,)),
        x_s=dma((1 + n_off,)),
        x_r=dma((2 * n_cut + 2 * n_off, max(nx - 1, 1))),
        s_s=dma((n_off,)),
        s_r=dma((n_off,)),
        z_s=dma((n_off,)),
        z_r=dma((n_off, 2)),
        gx_r=dma((n_cut, max(nx - 1, 1))),
        h_s=dma((2,)),
        h_r=dma((2,)),
    )
    names = (*args, "out", *scratch)
    merged_map = pl.pallas_call(
        functools.partial(kernel, dims, names),
        out_shape=jax.ShapeDtypeStruct((mb, rows, cols, dec), BF16),
        in_specs=[pl.BlockSpec(memory_space=pltpu.HBM)] * len(args),
        out_specs=pl.BlockSpec(memory_space=pltpu.VMEM),
        scratch_shapes=list(scratch.values()),
        compiler_params=pltpu.CompilerParams(
            collective_id=0, has_side_effects=True, vmem_limit_bytes=48 * 1024 * 1024
        ),
    )(*[pltpu.with_memory_space_constraint(a, pltpu.HBM) for a in args.values()])
    return jnp.maximum(merged_map, jnp.zeros_like(merged_map))


def solution(mesh):
    in_specs = (
        P("grp", "band", None, "sect"),
        P("grp", "band", None, None),
        P("grp", "band"),
        P("sect", None),
        P(None, None, None, "sect", None),
        P(),
        P("sect", None),
        P(),
        P(),
        P(),
        P(),
        P(),
        P(),
        P(),
    )
    out_specs = P("grp", "band", None, None)
    return jax.shard_map(shards, mesh=mesh, in_specs=in_specs, out_specs=out_specs, check_vma=False)
```

```python
import functools
import types

import jax
import jax.numpy as jnp
from jax import lax
from jax.experimental import pallas as pl
from jax.experimental.pallas import tpu as pltpu
from jax.sharding import PartitionSpec as P

DILATIONS = (12, 24, 36)
LAND_BLOCK = 6
LAND_MOST = 4
MESH = pl.DeviceIdType.MESH
F32 = jnp.float32
BF16 = jnp.bfloat16
ORDER = (0, 3, 2, 1)


def offsets(rows, bands):
    off = []
    for k in (1, 2, 3):
        d = DILATIONS[k - 1]
        assert d % rows == 0
        hop = d // rows
        if hop < bands:
            off.append((k, 0, hop))
            off.append((k, 2, hop))
    return off


def pieces(live):
    inner = live - 2
    cuts = [(0, 2)]
    if inner > 1:
        cuts += [(2, inner - inner // 2), (live - inner // 2, inner // 2)]
    elif inner:
        cuts.append((2, inner))
    return cuts


def kernel(dims, names, *refs):
    r = types.SimpleNamespace(**dict(zip(names, refs, strict=True)))
    mb, rows, cols, ch, br_w, live, nb, ns, low_w, lowp = dims
    nx = ns // 2
    cs = cols // nx
    off = offsets(rows, nb)
    n_off = len(off)
    cuts = pieces(live)
    n_cut = len(cuts)
    off_cuts = [(0, 2), (2, live - 2)]
    need = [(k, 1) for k in ORDER if k] + [(k, i) for k, i, _ in off]
    pad = (r.m_l.shape[1] - cols) // 2
    scope = jax.named_scope

    band = lax.axis_index("band")
    sect = lax.axis_index("sect")
    core = lax.rem(sect, 2)
    xi = lax.div(sect, 2)
    mine, theirs = core, 1 - core
    peer = xi * 2 + 1 - core

    waits = {}

    def fetch(name, *copies, whole):
        sem = r.loc_sem.at[len(waits)]
        for src, dst in copies:
            pltpu.make_async_copy(src, dst, sem).start()
        waits[name] = pltpu.make_async_copy(whole, whole, sem)

    def need_now(*which):
        for name in which:
            waits[name].wait()

    def taps_of(k, i):
        return r.wd_h.at[k - 1, i], r.wd.at[need.index((k, i))]

    fetch("mask", (r.mask_h, r.mask), whole=r.mask)
    fetch("theirs", (r.feat_h.at[theirs], r.feat.at[0]), whole=r.feat.at[0])
    fetch("w1", (r.w1_h, r.w1), whole=r.w1)
    fetch("mine", (r.feat_h.at[mine], r.feat_own), whole=r.feat_own)
    fetch("wpool", (r.wpool_h, r.wpool), whole=r.wpool)
    if n_off:
        fetch("off", *[taps_of(*n) for n in need[3:]], whole=r.wd.at[pl.ds(3, n_off)])
    fetch("taps0", taps_of(*need[0]), whole=r.wd.at[0])
    fetch("taps1", *[taps_of(*n) for n in need[1:3]], whole=r.wd.at[pl.ds(1, 2)])
    fetch("low", (r.low_h.at[mine], r.low), whole=r.low)
    fetch("wr", (r.wr_h, r.wr), whole=r.wr)
    fetch("br", (r.br_h, r.br), whole=r.br)
    fetch("wml", (r.wm_h.at[:, :, pl.ds(br_w, lowp)], r.wml), whole=r.wml)
    fetch(
        "vec", (r.bm_h, r.vec.at[0]), (r.bpool_h, r.vec.at[1]), (r.bproj_h, r.vec.at[2]),
        whole=r.vec,
    )
    fetch("wproj", (r.wproj_h, r.wproj), whole=r.wproj)
    fetch("bbr", (r.bbr_h, r.bbr), whole=r.bbr)
    fetch(
        "wmp",
        *[
            (r.wm_h.at[i, j, pl.ds(0, br_w)], r.wmp.at[j, pl.ds(i * br_w, br_w)])
            for i in range(3) for j in range(3)
        ],
        whole=r.wmp,
    )

    bar = pltpu.get_barrier_semaphore()
    up_ok = band >= 1
    dn_ok = band + 1 < nb

    def hello(b, s):
        pl.semaphore_signal(bar, inc=1, device_id={"band": b, "sect": s}, device_id_type=MESH)

    for e in range(1, ns):
        hello(band, lax.rem(sect + e, ns))
    for e in range(1, nb):
        hello(lax.rem(band + e, nb), sect)

    def rcopy(src, dst, s, rs, **where):
        return pltpu.make_async_remote_copy(
            src_ref=src, dst_ref=dst, send_sem=s, recv_sem=rs, device_id=where, device_id_type=MESH
        )

    low_up = rcopy(
        r.low_h.at[mine, 0], r.low_halo.at[1], r.lo_s.at[0], r.lo_r.at[1], band=band - 1, sect=sect
    )
    low_dn = rcopy(
        r.low_h.at[mine, rows - 1], r.low_halo.at[0], r.lo_s.at[1], r.lo_r.at[0],
        band=band + 1, sect=sect,
    )

    def slots(m):
        on = [r.mask[m, y] for y in range(rows)]
        place_of = [0] + [None] * (rows - 2) + [1]
        row_of = [0, rows - 1] + [jnp.int32(0)] * (live - 2)
        hits = {}
        count = jnp.int32(0)
        for y in range(1, rows - 1):
            place_of[y] = jnp.where(on[y] > 0, jnp.minimum(count + 2, live - 1), 0)
            for p in range(2, live):
                hit = jnp.logical_and(on[y] > 0, count == p - 2)
                row_of[p] = jnp.where(hit, y, row_of[p])
                hits[p, y] = jnp.where(hit, 1, 0)
            count = count + on[y]
        return on, place_of, row_of, hits

    for ref in (r.m_l, r.m_r):
        zero = jnp.zeros((ref.shape[0], pad, br_w), F32)
        ref[:, :pad] = zero
        ref[:, pad + cols :] = zero
    for at in (0, rows + 1):
        r.joined[at] = jnp.zeros((cols, br_w), BF16)

    def taps(lhs, n, wref, d):
        mid = jnp.dot(lhs, wref[1], preferred_element_type=F32).reshape(n, cols, br_w)
        r.m_l[:n, pl.ds(pad, cols)] = jnp.dot(
            lhs, wref[0], preferred_element_type=F32
        ).reshape(n, cols, br_w)
        r.m_r[:n, pl.ds(pad, cols)] = jnp.dot(
            lhs, wref[2], preferred_element_type=F32
        ).reshape(n, cols, br_w)
        return mid + r.m_l[:n, pl.ds(pad - d, cols)] + r.m_r[:n, pl.ds(pad + d, cols)]

    def core_copy(t):
        if t < 4:
            src, dst = r.part_own.at[t, 0], r.crecv_own.at[t]
        else:
            src, dst = r.part_off.at[t - 4, 0], r.crecv_off.at[t - 4]
        return rcopy(src, dst, r.c_s.at[max(t - 3, 0)], r.c_r.at[t], sect=peer)

    def run_of(t, g):
        return cuts[g] if t < 4 else off_cuts[g]

    def x_copy(t, g, e, incoming=False):
        lo, n = run_of(t, g)
        at = g * 2 + t // 3 if t < 4 else 2 * n_cut + (t - 4) * 2 + g
        send, recv, u = (
            (r.xsend_own, r.xrecv_own, t) if t < 4 else (r.xsend_off, r.xrecv_off, t - 4)
        )
        other = lax.rem(xi + e, nx)
        slot = other if incoming else xi
        return rcopy(
            send.at[u, other, pl.ds(lo, n)], recv.at[u, slot, pl.ds(lo, n)],
            r.x_s.at[max(t - 3, 0)], r.x_r.at[at, (e if incoming else nx - e) - 1],
            sect=other * 2 + core,
        )

    def x_arrived(g):
        for e in range(1, nx):
            whole = r.xrecv_own.at[pl.ds(0, 3), lax.rem(xi + e, nx), pl.ds(*cuts[g])]
            arrived(whole, r.x_r.at[g * 2, e - 1])

    def send_x(t, g):
        for e in range(1, nx):
            x_copy(t, g, e).start()

    def first(t, step):
        image = r.feat.at[0] if step == 0 else r.feat_own
        if t < 4:
            k = ORDER[t]
            row_of = facts[step][2]
            lhs = jnp.concatenate([image[row_of[p]] for p in range(live)], axis=0)
            if k:
                val = taps(lhs, live, r.wd.at[need.index((k, 1))], DILATIONS[k - 1])
            else:
                val = jnp.dot(lhs, r.w1[...], preferred_element_type=F32).reshape(live, cols, br_w)
            r.part_own[t, step] = val.astype(BF16)
        else:
            k, i, _ = off[t - 4]
            lhs = image[...].reshape(rows * cols, ch)
            val = taps(lhs, rows, r.wd.at[need.index((k, i))], DILATIONS[k - 1])
            r.part_off[t - 4, step] = val.astype(BF16)

    def second(t):
        core_copy(t).wait_recv()
        for c in range(nx):
            cell = pl.ds(c * cs, cs)
            total = r.part_own[t, 1, :, cell].astype(F32) + r.crecv_own[t, :, cell].astype(F32)
            r.xsend_own[t, c] = total.astype(BF16)

            @pl.when(xi == c)
            def _(total=total):
                r.keep_own[t] = total

    def second_off(t, h):
        u = t - 4
        if h == 0:
            core_copy(t).wait_recv()
        else:
            sel_copy(t).wait_recv()
        lo, n = off_cuts[h]
        for c in range(nx):
            cell = pl.ds(c * cs, cs)

            def row(y, cell=cell):
                return r.part_off[u, 1, y, cell].astype(F32) + r.crecv_off[u, y, cell].astype(F32)

            if h == 0:
                picked = [row(0), row(rows - 1)]
            else:
                inner = [row(y) for y in range(1, rows - 1)]
                picked = []
                for p in range(2, live):
                    total = jnp.zeros((cs, br_w), F32)
                    for y in range(1, rows - 1):
                        at = (p - 2) * (rows - 2) + y - 1
                        total = total + inner[y - 1] * r.sel_in[u, at : at + 1]
                    picked.append(total)
            for p, total in enumerate(picked):
                r.xsend_off[u, c, lo + p] = total.astype(BF16)

            @pl.when(xi == c)
            def _(picked=picked):
                for p, total in enumerate(picked):
                    r.keep_off[u, lo + p] = total

    def sends_to(t):
        k, i, hop = off[t - 4]
        return band + hop < nb if i == 0 else band - hop >= 0

    def gets_from(t):
        k, i, hop = off[t - 4]
        return band - hop >= 0 if i == 0 else band + hop < nb

    def sel_copy(t):
        k, i, hop = off[t - 4]
        return rcopy(
            r.sel_out, r.sel_in.at[t - 4], r.s_s.at[t - 4], r.s_r.at[t - 4],
            band=band - hop if i == 0 else band + hop, sect=sect,
        )

    def z_copy(t, h):
        k, i, hop = off[t - 4]
        run = pl.ds(*off_cuts[h])
        return rcopy(
            r.zsend.at[t - 4, run], r.zrecv.at[t - 4, run], r.z_s.at[t - 4], r.z_r.at[t - 4, h],
            band=band + hop if i == 0 else band - hop, sect=sect,
        )

    def forward_off(t, h):
        run = pl.ds(*off_cuts[h])
        total = r.keep_off[t - 4, run]
        for e in range(1, nx):
            x_copy(t, h, e, True).wait_recv()
            total = total + r.xrecv_off[t - 4, lax.rem(xi + e, nx), run].astype(F32)
        r.zsend[t - 4, run] = total.astype(BF16)
        z_copy(t, h).start()

    def for_off(fn, *rest):
        for t in range(4, 4 + n_off):
            @pl.when(sends_to(t))
            def _(t=t):
                fn(t, *rest)

    def pool_sect(e, incoming=False):
        other = lax.rem(sect + e, ns)
        slot = other if incoming else sect
        return rcopy(
            r.pool_s.at[sect], r.pool_s.at[slot], r.one_s.at[0], r.one_r.at[0], sect=other
        )

    def pool_band(e, incoming=False):
        other = lax.rem(band + e, nb)
        slot = other if incoming else band
        return rcopy(
            r.pool_b.at[band], r.pool_b.at[slot], r.one_s.at[1], r.one_r.at[1], band=other
        )

    def dot_f32(v, w):
        n = v.shape[0]
        high = v.astype(BF16).astype(F32)
        middle = (v - high).astype(BF16).astype(F32)
        terms = jnp.concatenate([high, middle, v - high - middle], axis=0).astype(BF16)
        p = jnp.dot(terms, w, preferred_element_type=F32)
        return p[:n] + p[n : 2 * n] + p[2 * n :]

    def all_of(ref, n):
        return ref.at[pl.ds(0, n)]

    def arrived(whole, sem):
        pltpu.make_async_copy(whole, whole, sem).wait()

    def pool():
        need_now("wpool")
        ones = jnp.ones((8, rows * cols), BF16)
        at = lax.broadcasted_iota(jnp.int32, (8, ch), 0)
        sums = jnp.zeros((8, ch), F32)
        for m, image in ((mine, r.feat_own), (theirs, r.feat.at[0])):
            part = jnp.dot(
                ones, image[...].reshape(rows * cols, ch), preferred_element_type=F32
            )
            sums = jnp.where(at == m, part, sums)
        r.pool_s[sect] = dot_f32(sums, r.wpool[...])[:mb]
        for e in range(1, ns):
            pool_sect(e).start()

    need_now("mask")
    facts = [slots(theirs), slots(mine)]
    on, place_of, row_of, hits = facts[1]

    for p in range(2, live):
        for y in range(1, rows - 1):
            at = (p - 2) * (rows - 2) + y - 1
            r.sel_out[at : at + 1] = jnp.full((1, br_w), hits[p, y].astype(F32))

    def own_half(t, step):
        with scope(f"first{t}{'ab'[step]}"):
            first(t, step)
        if step == 0:
            core_copy(t).start()

    def off_theirs(t):
        first(t, 0)
        core_copy(t).start()

    def off_send(t, h):
        second_off(t, h)
        send_x(t, h)

    with scope("w0"):
        need_now("theirs", "w1")
    with scope("first0a"):
        first(0, 0)
    with scope("bar"):
        pl.semaphore_wait(bar, (ns - 1) + (nb - 1))
    core_copy(0).start()
    for t in range(4, 4 + n_off):
        @pl.when(gets_from(t))
        def _(t=t):
            sel_copy(t).start()

    @pl.when(up_ok)
    def _():
        low_up.start()

    @pl.when(dn_ok)
    def _():
        low_dn.start()

    need_now("mine")
    own_half(0, 1)
    with scope("pool"):
        pool()
    with scope("second0"):
        second(0)
    for g in range(n_cut):
        send_x(0, g)
    if n_off:
        need_now("off")
    with scope("offa"):
        for_off(off_theirs)
    with scope("offb"):
        for_off(first, 1)
    with scope("offs0"):
        for_off(off_send, 0)
    need_now("taps0")
    own_half(1, 0)
    own_half(1, 1)
    with scope("poolb"):
        arrived(all_of(r.pool_s, ns - 1), r.one_r.at[0])
        total = r.pool_s[0]
        for s in range(1, ns):
            total = total + r.pool_s[s]
        r.pool_b[band] = total
    for e in range(1, nb):
        pool_band(e).start()
    with scope("second1"):
        second(1)
    send_x(1, 0)
    with scope("offs1"):
        for_off(off_send, 1)
    for g in range(1, n_cut):
        send_x(1, g)
    need_now("taps1")
    own_half(2, 0)
    own_half(2, 1)
    own_half(3, 0)
    with scope("second2"):
        second(2)
    send_x(2, 0)
    with scope("fwd0"):
        for_off(forward_off, 0)
    own_half(3, 1)
    with scope("second3"):
        second(3)
    send_x(3, 0)
    for t in (2, 3):
        for g in range(1, n_cut):
            send_x(t, g)

    with scope("low"):
        need_now("low", "wr", "br", "wml", "vec")

        def reduced(v):
            return jax.nn.relu(
                lax.dot_general(
                    v, r.wr[...], (((1,), (1,)), ((), ())), preferred_element_type=F32
                )
                + r.br[...]
            ).astype(BF16)

        r.lowred[1 : rows + 1] = reduced(r.low[...].reshape(rows * cols, low_w)).reshape(
            rows, cols, lowp
        )
        for side, at, ok, copy in ((0, 0, up_ok, low_dn), (1, rows + 1, dn_ok, low_up)):
            @pl.when(ok)
            def _(side=side, at=at, copy=copy):
                copy.wait_recv()
                r.lowred[at] = reduced(r.low_halo[side])

            @pl.when(jnp.logical_not(ok))
            def _(at=at):
                r.lowred[at] = jnp.zeros((cols, lowp), BF16)

    def combine(mid, left, right, n):
        r.m_l[:n, pl.ds(pad, cols)] = left.reshape(n, cols, br_w)
        r.m_r[:n, pl.ds(pad, cols)] = right.reshape(n, cols, br_w)
        return (
            mid.reshape(n, cols, br_w)
            + r.m_l[:n, pl.ds(pad - 1, cols)]
            + r.m_r[:n, pl.ds(pad + 1, cols)]
        )

    with scope("lowconv"):
        terms = [None] * 3
        for i in range(3):
            lhs = jnp.concatenate([r.lowred[row_of[p] + i] for p in range(live)], axis=0)
            for j in range(3):
                term = jnp.dot(lhs, r.wml[i, j], preferred_element_type=F32)
                terms[j] = term if i == 0 else terms[j] + term
        r.lowacc[...] = combine(terms[1], terms[0], terms[2], live) + r.vec[0].reshape(1, 1, br_w)

    with scope("fwd1"):
        for_off(forward_off, 1)

    need_now("wproj", "bbr")
    with scope("ctx"):
        if nb > 1:
            arrived(all_of(r.pool_b, nb - 1), r.one_r.at[1])
        total = r.pool_b[0]
        for b in range(1, nb):
            total = total + r.pool_b[b]
        pooled = jax.nn.relu(total / (nb * rows * cols) + r.vec[1])
        context = dot_f32(pooled, r.wproj[4 * br_w :])
        own = context[0:1]
        for m in range(1, mb):
            own = jnp.where(mine == m, context[m : m + 1], own)
        base = own + r.vec[2]

    def branch(t, g):
        lo, n = cuts[g]
        k = ORDER[t]
        with scope(f"x{t}{g}"):
            if t == 0:
                x_arrived(g)
            if t == 3:
                for e in range(1, nx):
                    x_copy(t, g, e, True).wait_recv()
        for u in range(4, 4 + n_off):
            if off[u - 4][0] == k:
                @pl.when(gets_from(u))
                def _(u=u):
                    with scope(f"z{g}"):
                        if g < 2:
                            z_copy(u, g).wait_recv()
                    run = pl.ds(lo, n)
                    r.keep_own[t, run] = r.keep_own[t, run] + r.zrecv[u - 4, run].astype(F32)
        total = r.keep_own[t, lo : lo + n]
        for e in range(1, nx):
            total = total + r.xrecv_own[t, lax.rem(xi + e, nx), lo : lo + n].astype(F32)
        total = jax.nn.relu(total + r.bbr[k : k + 1].reshape(1, 1, br_w)).astype(BF16)
        return jnp.dot(
            total.reshape(n * cs, br_w), r.wproj[k * br_w : (k + 1) * br_w],
            preferred_element_type=F32,
        )

    def gather_x(g, e, incoming=False):
        run = pl.ds(*cuts[g])
        other = lax.rem(xi + e, nx)
        slot = other if incoming else xi
        return rcopy(
            r.gath.at[xi, run], r.gath.at[slot, run],
            r.one_s.at[2], r.gx_r.at[g, (e if incoming else nx - e) - 1], sect=other * 2 + core,
        )

    def early(g):
        lo, n = cuts[g]
        acc = branch(0, g)
        for t in (1, 2):
            acc = acc + branch(t, g)
        r.acc[lo : lo + n] = (acc + base).reshape(n, cs, br_w)

    def project(g):
        lo, n = cuts[g]
        last = branch(3, g).reshape(n, cs, br_w)
        done = jax.nn.relu(r.acc[lo : lo + n] + last)
        for p in range(n):
            v = done[p]
            if lo + p < 2:
                v = v * on[(0, rows - 1)[lo + p]].astype(F32)
            r.gath[xi, lo + p] = v.astype(BF16)
        for e in range(1, nx):
            gather_x(g, e).start()

    def halo_copy(side, c):
        return rcopy(
            r.gath.at[c, 1 - side], r.halo.at[side, c], r.h_s.at[side], r.h_r.at[side],
            band=band + 1 if side == 0 else band - 1, sect=sect,
        )

    def send_halo(c):
        for side, ok in ((0, dn_ok), (1, up_ok)):
            @pl.when(ok)
            def _(side=side):
                halo_copy(side, c).start()

    early(0)
    project(0)
    send_halo(xi)
    for g in range(1, n_cut):
        early(g)
    for g in range(1, n_cut):
        project(g)
    for e in range(1, nx):
        with scope("ga"):
            gather_x(0, e, True).wait_recv()
        send_halo(lax.rem(xi + e, nx))
    for c in range(nx):
        for p, y in ((0, 0), (1, rows - 1)):
            r.joined[y + 1, pl.ds(c * cs, cs)] = r.gath[c, p]
    need_now("wmp")
    with scope("gb"):
        for g in range(1, n_cut):
            for e in range(1, nx):
                gather_x(g, e, True).wait_recv()
    with scope("join"):
        for y in range(1, rows - 1):
            for c in range(nx):
                r.joined[y + 1, pl.ds(c * cs, cs)] = (
                    r.gath[c, place_of[y]].astype(F32) * on[y].astype(F32)
                ).astype(BF16)

    def take_halo():
        for side, at, ok in ((0, 0, up_ok), (1, rows + 1, dn_ok)):
            @pl.when(ok)
            def _(side=side, at=at):
                with scope("hw"):
                    arrived(r.halo.at[side], r.h_r.at[side])
                for c in range(nx):
                    r.joined[at, pl.ds(c * cs, cs)] = r.halo[side, c]

    def merged_copy(h):
        run = pl.ds(*halves[h])
        return rcopy(
            r.merged.at[run], r.merged_in.at[run], r.one_s.at[3], r.one_r.at[2], sect=peer
        )

    halves = [(2, live - 2), (0, 2)]
    for h, (lo, n) in enumerate(halves):
        if h == 1:
            take_halo()
        with scope(f"merge{h}"):
            lhs = jnp.concatenate(
                [
                    jnp.concatenate([r.joined[row_of[p] + i] for p in range(lo, lo + n)], axis=0)
                    for i in range(3)
                ],
                axis=1,
            )
            left, mid, right = [
                jnp.dot(lhs, r.wmp[j], preferred_element_type=F32) for j in range(3)
            ]
            total = combine(mid, left, right, n) + r.lowacc[lo : lo + n]
            r.merged[lo : lo + n] = jax.nn.relu(total).astype(BF16)
        merged_copy(h).start()

    def spread(image, src, flags, places):
        for y in range(rows):
            r.out[image, y] = (src[places[y]].astype(F32) * flags[y].astype(F32)).astype(BF16)

    with scope("spread"):
        spread(mine, r.merged, on, place_of)
    with scope("ow"):
        arrived(r.merged, r.one_r.at[2])
    with scope("spread2"):
        spread(theirs, r.merged_in, facts[0][0], facts[0][1])

    @pl.when(up_ok)
    def _():
        low_up.wait_send()

    @pl.when(dn_ok)
    def _():
        low_dn.wait_send()

    def off_sent(t):
        u = t - 4
        core_copy(t).wait_send()
        if nx > 1:
            arrived(all_of(r.xsend_off.at[u], nx - 1), r.x_s.at[1 + u])
        arrived(r.zsend.at[u], r.z_s.at[u])

    for t in range(4, 4 + n_off):
        @pl.when(gets_from(t))
        def _(t=t):
            sel_copy(t).wait_send()
    for_off(off_sent)
    arrived(r.part_own.at[:, 0], r.c_s.at[0])
    if nx > 1:
        arrived(r.xsend_own.at[:, pl.ds(0, nx - 1)], r.x_s.at[0])
        arrived(all_of(r.gath, nx - 1), r.one_s.at[2])
    arrived(all_of(r.pool_s, ns - 1), r.one_s.at[0])
    if nb > 1:
        arrived(all_of(r.pool_b, nb - 1), r.one_s.at[1])
    for side, ok in ((0, dn_ok), (1, up_ok)):
        @pl.when(ok)
        def _(side=side):
            arrived(r.halo.at[side], r.h_s.at[side])
    arrived(r.merged, r.one_s.at[3])


def shards(
    features, low_level, land_mask, weight_one, weight_dilated, bias_branch, weight_pool,
    bias_pool, weight_project, bias_project, weight_reduce, bias_reduce, weight_merging,
    bias_merging,
):
    mb, rows, cols, ch = features.shape
    br_w = weight_project.shape[1]
    dec = weight_merging.shape[3]
    low_w, lowp = weight_reduce.shape
    nb, ns = lax.axis_size("band"), lax.axis_size("sect")
    nx = ns // 2
    cs = cols // nx
    assert mb == 2 and ns % 2 == 0 and rows > 2
    live = rows // LAND_BLOCK * LAND_MOST if rows % LAND_BLOCK == 0 else rows
    off = offsets(rows, nb)
    n_off = max(len(off), 1)
    assert dec == br_w
    n_cut = len(pieces(live))
    n_sel = -(-(live - 2) * (rows - 2) // 8) * 8
    pad = -(-max(DILATIONS) // 8) * 8
    vm, dma = pltpu.VMEM, pltpu.SemaphoreType.DMA
    dims = (mb, rows, cols, ch, br_w, live, nb, ns, low_w, lowp)
    args = dict(
        mask_h=land_mask, feat_h=features, low_h=low_level, w1_h=weight_one, wd_h=weight_dilated,
        bbr_h=bias_branch, wpool_h=weight_pool, bpool_h=bias_pool.reshape(1, -1),
        wproj_h=weight_project, bproj_h=bias_project.reshape(1, -1), wr_h=weight_reduce.T,
        br_h=bias_reduce.reshape(1, -1), wm_h=weight_merging, bm_h=bias_merging.reshape(1, -1),
    )
    scratch = dict(
        mask=pltpu.SMEM(land_mask.shape, jnp.int32),
        feat=vm((1, rows, cols, ch), BF16),
        feat_own=vm((rows, cols, ch), BF16),
        low=vm((rows, cols, low_w), BF16),
        low_halo=vm((2, cols, low_w), BF16),
        w1=vm(weight_one.shape, BF16),
        wpool=vm(weight_pool.shape, BF16),
        sel_out=vm((n_sel, br_w), F32),
        sel_in=vm((n_off, n_sel, br_w), F32),
        wd=vm((3 + len(off), 3, ch, br_w), BF16),
        wproj=vm(weight_project.shape, BF16),
        wmp=vm((3, 3 * br_w, dec), BF16),
        wml=vm((3, 3, lowp, dec), BF16),
        wr=vm((lowp, low_w), BF16),
        br=vm((1, lowp), F32),
        vec=vm((3, 1, br_w), F32),
        bbr=vm(bias_branch.shape, F32),
        m_l=vm((rows, cols + 2 * pad, br_w), F32),
        m_r=vm((rows, cols + 2 * pad, br_w), F32),
        part_off=vm((n_off, 2, rows, cols, br_w), BF16),
        crecv_off=vm((n_off, rows, cols, br_w), BF16),
        xsend_off=vm((n_off, nx, live, cs, br_w), BF16),
        xrecv_off=vm((n_off, nx, live, cs, br_w), BF16),
        zsend=vm((n_off, live, cs, br_w), BF16),
        zrecv=vm((n_off, live, cs, br_w), BF16),
        keep_off=vm((n_off, live, cs, br_w), F32),
        part_own=vm((4, 2, live, cols, br_w), BF16),
        crecv_own=vm((4, live, cols, br_w), BF16),
        xsend_own=vm((4, nx, live, cs, br_w), BF16),
        xrecv_own=vm((4, nx, live, cs, br_w), BF16),
        keep_own=vm((4, live, cs, br_w), F32),
        acc=vm((live, cs, br_w), F32),
        pool_s=vm((ns, mb, br_w), F32),
        pool_b=vm((nb, mb, br_w), F32),
        gath=vm((nx, live, cs, br_w), BF16),
        halo=vm((2, nx, cs, br_w), BF16),
        joined=vm((rows + 2, cols, br_w), BF16),
        lowred=vm((rows + 2, cols, lowp), BF16),
        lowacc=vm((live, cols, dec), F32),
        merged=vm((live, cols, dec), BF16),
        merged_in=vm((live, cols, dec), BF16),
        loc_sem=dma((16,)),
        one_s=dma((4,)),
        one_r=dma((3,)),
        lo_s=dma((2,)),
        lo_r=dma((2,)),
        c_s=dma((1 + n_off,)),
        c_r=dma((4 + n_off,)),
        x_s=dma((1 + n_off,)),
        x_r=dma((2 * n_cut + 2 * n_off, max(nx - 1, 1))),
        s_s=dma((n_off,)),
        s_r=dma((n_off,)),
        z_s=dma((n_off,)),
        z_r=dma((n_off, 2)),
        gx_r=dma((n_cut, max(nx - 1, 1))),
        h_s=dma((2,)),
        h_r=dma((2,)),
    )
    names = (*args, "out", *scratch)
    merged_map = pl.pallas_call(
        functools.partial(kernel, dims, names),
        out_shape=jax.ShapeDtypeStruct((mb, rows, cols, dec), BF16),
        in_specs=[pl.BlockSpec(memory_space=pltpu.HBM)] * len(args),
        out_specs=pl.BlockSpec(memory_space=pltpu.VMEM),
        scratch_shapes=list(scratch.values()),
        compiler_params=pltpu.CompilerParams(
            collective_id=0, has_side_effects=True, vmem_limit_bytes=48 * 1024 * 1024
        ),
    )(*[pltpu.with_memory_space_constraint(a, pltpu.HBM) for a in args.values()])
    return jnp.maximum(merged_map, jnp.zeros_like(merged_map))


def solution(mesh):
    in_specs = (
        P("grp", "band", None, "sect"),
        P("grp", "band", None, None),
        P("grp", "band"),
        P("sect", None),
        P(None, None, None, "sect", None),
        P(),
        P("sect", None),
        P(),
        P(),
        P(),
        P(),
        P(),
        P(),
        P(),
    )
    out_specs = P("grp", "band", None, None)
    return jax.shard_map(shards, mesh=mesh, in_specs=in_specs, out_specs=out_specs, check_vma=False)
```

```python
import functools
import types

import jax
import jax.numpy as jnp
from jax import lax
from jax.experimental import pallas as pl
from jax.experimental.pallas import tpu as pltpu
from jax.sharding import PartitionSpec as P

DILATIONS = (12, 24, 36)
LAND_BLOCK = 6
LAND_MOST = 4
MESH = pl.DeviceIdType.MESH
F32 = jnp.float32
BF16 = jnp.bfloat16
ORDER = (0, 3, 2, 1)


def offsets(rows, bands):
    off = []
    for k in (1, 2, 3):
        d = DILATIONS[k - 1]
        assert d % rows == 0
        hop = d // rows
        if hop < bands:
            off.append((k, 0, hop))
            off.append((k, 2, hop))
    return off


def pieces(live):
    inner = live - 2
    cuts = [(0, 2)]
    if inner > 1:
        cuts += [(2, inner - inner // 2), (live - inner // 2, inner // 2)]
    elif inner:
        cuts.append((2, inner))
    return cuts


def kernel(dims, names, *refs):
    r = types.SimpleNamespace(**dict(zip(names, refs, strict=True)))
    mb, rows, cols, ch, br_w, live, nb, ns, low_w, lowp = dims
    nx = ns // 2
    cs = cols // nx
    off = offsets(rows, nb)
    n_off = len(off)
    cuts = pieces(live)
    n_cut = len(cuts)
    off_cuts = [(0, 2), (2, live - 2)]
    need = [(k, 1) for k in ORDER if k] + [(k, i) for k, i, _ in off]
    pad = (r.m_l.shape[1] - cols) // 2
    scope = jax.named_scope

    band = lax.axis_index("band")
    sect = lax.axis_index("sect")
    core = lax.rem(sect, 2)
    xi = lax.div(sect, 2)
    mine, theirs = core, 1 - core
    peer = xi * 2 + 1 - core

    waits = {}

    def fetch(name, *copies, whole):
        sem = r.loc_sem.at[len(waits)]
        for src, dst in copies:
            pltpu.make_async_copy(src, dst, sem).start()
        waits[name] = pltpu.make_async_copy(whole, whole, sem)

    def need_now(*which):
        for name in which:
            waits[name].wait()

    def taps_of(k, i):
        return r.wd_h.at[k - 1, i], r.wd.at[need.index((k, i))]

    fetch("mask", (r.mask_h, r.mask), whole=r.mask)
    fetch("theirs", (r.feat_h.at[theirs], r.feat.at[0]), whole=r.feat.at[0])
    fetch("w1", (r.w1_h, r.w1), whole=r.w1)
    fetch("mine", (r.feat_h.at[mine], r.feat_own), whole=r.feat_own)
    fetch("wpool", (r.wpool_h, r.wpool), whole=r.wpool)
    if n_off:
        fetch("off", *[taps_of(*n) for n in need[3:]], whole=r.wd.at[pl.ds(3, n_off)])
    fetch("taps0", taps_of(*need[0]), whole=r.wd.at[0])
    fetch("taps1", *[taps_of(*n) for n in need[1:3]], whole=r.wd.at[pl.ds(1, 2)])
    fetch("low", (r.low_h.at[mine], r.low), whole=r.low)
    fetch("wr", (r.wr_h, r.wr), whole=r.wr)
    fetch("br", (r.br_h, r.br), whole=r.br)
    fetch("wml", (r.wm_h.at[:, :, pl.ds(br_w, lowp)], r.wml), whole=r.wml)
    fetch(
        "vec", (r.bm_h, r.vec.at[0]), (r.bpool_h, r.vec.at[1]), (r.bproj_h, r.vec.at[2]),
        whole=r.vec,
    )
    fetch("wproj", (r.wproj_h, r.wproj), whole=r.wproj)
    fetch("bbr", (r.bbr_h, r.bbr), whole=r.bbr)
    fetch(
        "wmp",
        *[
            (r.wm_h.at[i, j, pl.ds(0, br_w)], r.wmp.at[j, pl.ds(i * br_w, br_w)])
            for i in range(3) for j in range(3)
        ],
        whole=r.wmp,
    )

    bar = pltpu.get_barrier_semaphore()
    up_ok = band >= 1
    dn_ok = band + 1 < nb

    def hello(b, s):
        pl.semaphore_signal(bar, inc=1, device_id={"band": b, "sect": s}, device_id_type=MESH)

    for e in range(1, ns):
        hello(band, lax.rem(sect + e, ns))
    for e in range(1, nb):
        hello(lax.rem(band + e, nb), sect)

    def rcopy(src, dst, s, rs, **where):
        return pltpu.make_async_remote_copy(
            src_ref=src, dst_ref=dst, send_sem=s, recv_sem=rs, device_id=where, device_id_type=MESH
        )

    low_up = rcopy(
        r.low_h.at[mine, 0], r.low_halo.at[1], r.lo_s.at[0], r.lo_r.at[1], band=band - 1, sect=sect
    )
    low_dn = rcopy(
        r.low_h.at[mine, rows - 1], r.low_halo.at[0], r.lo_s.at[1], r.lo_r.at[0],
        band=band + 1, sect=sect,
    )

    def slots(m):
        on = [r.mask[m, y] for y in range(rows)]
        place_of = [0] + [None] * (rows - 2) + [1]
        row_of = [0, rows - 1] + [jnp.int32(0)] * (live - 2)
        hits = {}
        count = jnp.int32(0)
        for y in range(1, rows - 1):
            place_of[y] = jnp.where(on[y] > 0, jnp.minimum(count + 2, live - 1), 0)
            for p in range(2, live):
                hit = jnp.logical_and(on[y] > 0, count == p - 2)
                row_of[p] = jnp.where(hit, y, row_of[p])
                hits[p, y] = jnp.where(hit, 1, 0)
            count = count + on[y]
        return on, place_of, row_of, hits

    for ref in (r.m_l, r.m_r):
        zero = jnp.zeros((ref.shape[0], pad, br_w), F32)
        ref[:, :pad] = zero
        ref[:, pad + cols :] = zero
    for at in (0, rows + 1):
        r.joined[at] = jnp.zeros((cols, br_w), BF16)

    def taps(lhs, n, wref, d):
        mid = jnp.dot(lhs, wref[1], preferred_element_type=F32).reshape(n, cols, br_w)
        r.m_l[:n, pl.ds(pad, cols)] = jnp.dot(
            lhs, wref[0], preferred_element_type=F32
        ).reshape(n, cols, br_w)
        r.m_r[:n, pl.ds(pad, cols)] = jnp.dot(
            lhs, wref[2], preferred_element_type=F32
        ).reshape(n, cols, br_w)
        return mid + r.m_l[:n, pl.ds(pad - d, cols)] + r.m_r[:n, pl.ds(pad + d, cols)]

    def core_copy(t):
        if t < 4:
            src, dst = r.part_own.at[t, 0], r.crecv_own.at[t]
        else:
            src, dst = r.part_off.at[t - 4, 0], r.crecv_off.at[t - 4]
        return rcopy(src, dst, r.c_s.at[max(t - 3, 0)], r.c_r.at[t], sect=peer)

    def run_of(t, g):
        return cuts[g] if t < 4 else off_cuts[g]

    def x_copy(t, g, e, incoming=False):
        lo, n = run_of(t, g)
        at = g * 2 + t // 3 if t < 4 else 2 * n_cut + (t - 4) * 2 + g
        send, recv, u = (
            (r.xsend_own, r.xrecv_own, t) if t < 4 else (r.xsend_off, r.xrecv_off, t - 4)
        )
        other = lax.rem(xi + e, nx)
        slot = other if incoming else xi
        return rcopy(
            send.at[u, other, pl.ds(lo, n)], recv.at[u, slot, pl.ds(lo, n)],
            r.x_s.at[max(t - 3, 0)], r.x_r.at[at, (e if incoming else nx - e) - 1],
            sect=other * 2 + core,
        )

    def x_arrived(g):
        for e in range(1, nx):
            whole = r.xrecv_own.at[pl.ds(0, 3), lax.rem(xi + e, nx), pl.ds(*cuts[g])]
            arrived(whole, r.x_r.at[g * 2, e - 1])

    def send_x(t, g):
        for e in range(1, nx):
            x_copy(t, g, e).start()

    def first(t, step):
        image = r.feat.at[0] if step == 0 else r.feat_own
        if t < 4:
            k = ORDER[t]
            row_of = facts[step][2]
            lhs = jnp.concatenate([image[row_of[p]] for p in range(live)], axis=0)
            if k:
                val = taps(lhs, live, r.wd.at[need.index((k, 1))], DILATIONS[k - 1])
            else:
                val = jnp.dot(lhs, r.w1[...], preferred_element_type=F32).reshape(live, cols, br_w)
            r.part_own[t, step] = val.astype(BF16)
        else:
            k, i, _ = off[t - 4]
            lhs = image[...].reshape(rows * cols, ch)
            val = taps(lhs, rows, r.wd.at[need.index((k, i))], DILATIONS[k - 1])
            r.part_off[t - 4, step] = val.astype(BF16)

    def second(t):
        core_copy(t).wait_recv()
        for c in range(nx):
            cell = pl.ds(c * cs, cs)
            total = r.part_own[t, 1, :, cell].astype(F32) + r.crecv_own[t, :, cell].astype(F32)
            r.xsend_own[t, c] = total.astype(BF16)

            @pl.when(xi == c)
            def _(total=total):
                r.keep_own[t] = total

    def second_off(t, h):
        u = t - 4
        if h == 0:
            core_copy(t).wait_recv()
        else:
            sel_copy(t).wait_recv()
        lo, n = off_cuts[h]
        for c in range(nx):
            cell = pl.ds(c * cs, cs)

            def row(y, cell=cell):
                return r.part_off[u, 1, y, cell].astype(F32) + r.crecv_off[u, y, cell].astype(F32)

            if h == 0:
                picked = [row(0), row(rows - 1)]
            else:
                inner = [row(y) for y in range(1, rows - 1)]
                picked = []
                for p in range(2, live):
                    total = jnp.zeros((cs, br_w), F32)
                    for y in range(1, rows - 1):
                        at = (p - 2) * (rows - 2) + y - 1
                        total = total + inner[y - 1] * r.sel_in[u, at : at + 1]
                    picked.append(total)
            for p, total in enumerate(picked):
                r.xsend_off[u, c, lo + p] = total.astype(BF16)

            @pl.when(xi == c)
            def _(picked=picked):
                for p, total in enumerate(picked):
                    r.keep_off[u, lo + p] = total

    def sends_to(t):
        k, i, hop = off[t - 4]
        return band + hop < nb if i == 0 else band - hop >= 0

    def gets_from(t):
        k, i, hop = off[t - 4]
        return band - hop >= 0 if i == 0 else band + hop < nb

    def sel_copy(t):
        k, i, hop = off[t - 4]
        return rcopy(
            r.sel_out, r.sel_in.at[t - 4], r.s_s.at[t - 4], r.s_r.at[t - 4],
            band=band - hop if i == 0 else band + hop, sect=sect,
        )

    def z_copy(t, h):
        k, i, hop = off[t - 4]
        run = pl.ds(*off_cuts[h])
        return rcopy(
            r.zsend.at[t - 4, run], r.zrecv.at[t - 4, run], r.z_s.at[t - 4], r.z_r.at[t - 4, h],
            band=band + hop if i == 0 else band - hop, sect=sect,
        )

    def forward_off(t, h):
        run = pl.ds(*off_cuts[h])
        total = r.keep_off[t - 4, run]
        for e in range(1, nx):
            x_copy(t, h, e, True).wait_recv()
            total = total + r.xrecv_off[t - 4, lax.rem(xi + e, nx), run].astype(F32)
        r.zsend[t - 4, run] = total.astype(BF16)
        z_copy(t, h).start()

    def for_off(fn, *rest):
        for t in range(4, 4 + n_off):
            @pl.when(sends_to(t))
            def _(t=t):
                fn(t, *rest)

    def pool_sect(e, incoming=False):
        other = lax.rem(sect + e, ns)
        slot = other if incoming else sect
        return rcopy(
            r.pool_s.at[sect], r.pool_s.at[slot], r.one_s.at[0], r.one_r.at[0], sect=other
        )

    def pool_band(e, incoming=False):
        other = lax.rem(band + e, nb)
        slot = other if incoming else band
        return rcopy(
            r.pool_b.at[band], r.pool_b.at[slot], r.one_s.at[1], r.one_r.at[1], band=other
        )

    def dot_f32(v, w):
        n = v.shape[0]
        high = v.astype(BF16).astype(F32)
        middle = (v - high).astype(BF16).astype(F32)
        terms = jnp.concatenate([high, middle, v - high - middle], axis=0).astype(BF16)
        p = jnp.dot(terms, w, preferred_element_type=F32)
        return p[:n] + p[n : 2 * n] + p[2 * n :]

    def all_of(ref, n):
        return ref.at[pl.ds(0, n)]

    def arrived(whole, sem):
        pltpu.make_async_copy(whole, whole, sem).wait()

    def pool():
        need_now("wpool")
        ones = jnp.ones((8, rows * cols), BF16)
        at = lax.broadcasted_iota(jnp.int32, (8, ch), 0)
        sums = jnp.zeros((8, ch), F32)
        for m, image in ((mine, r.feat_own), (theirs, r.feat.at[0])):
            part = jnp.dot(
                ones, image[...].reshape(rows * cols, ch), preferred_element_type=F32
            )
            sums = jnp.where(at == m, part, sums)
        r.pool_s[sect] = dot_f32(sums, r.wpool[...])[:mb]
        for e in range(1, ns):
            pool_sect(e).start()

    need_now("mask")
    facts = [slots(theirs), slots(mine)]
    on, place_of, row_of, hits = facts[1]

    for p in range(2, live):
        for y in range(1, rows - 1):
            at = (p - 2) * (rows - 2) + y - 1
            r.sel_out[at : at + 1] = jnp.full((1, br_w), hits[p, y].astype(F32))

    def own_half(t, step):
        with scope(f"first{t}{'ab'[step]}"):
            first(t, step)
        if step == 0:
            core_copy(t).start()

    def off_theirs(t):
        first(t, 0)
        core_copy(t).start()

    def off_send(t, h):
        second_off(t, h)
        send_x(t, h)

    with scope("w0"):
        need_now("theirs", "w1")
    with scope("first0a"):
        first(0, 0)
    with scope("bar"):
        pl.semaphore_wait(bar, (ns - 1) + (nb - 1))
    core_copy(0).start()
    for t in range(4, 4 + n_off):
        @pl.when(gets_from(t))
        def _(t=t):
            sel_copy(t).start()

    @pl.when(up_ok)
    def _():
        low_up.start()

    @pl.when(dn_ok)
    def _():
        low_dn.start()

    need_now("mine")
    own_half(0, 1)
    with scope("pool"):
        pool()
    with scope("second0"):
        second(0)
    for g in range(n_cut):
        send_x(0, g)
    if n_off:
        need_now("off")
    with scope("offa"):
        for_off(off_theirs)
    need_now("taps0")
    own_half(1, 0)
    with scope("offb"):
        for_off(first, 1)
    with scope("offs0"):
        for_off(off_send, 0)
    own_half(1, 1)
    with scope("second1"):
        second(1)
    send_x(1, 0)
    with scope("offs1"):
        for_off(off_send, 1)
    for g in range(1, n_cut):
        send_x(1, g)
    with scope("poolb"):
        arrived(all_of(r.pool_s, ns - 1), r.one_r.at[0])
        total = r.pool_s[0]
        for s in range(1, ns):
            total = total + r.pool_s[s]
        r.pool_b[band] = total
    for e in range(1, nb):
        pool_band(e).start()
    need_now("taps1")
    own_half(2, 0)
    own_half(3, 0)
    own_half(2, 1)
    with scope("second2"):
        second(2)
    send_x(2, 0)
    own_half(3, 1)
    with scope("second3"):
        second(3)
    send_x(3, 0)
    for t in (2, 3):
        for g in range(1, n_cut):
            send_x(t, g)
    with scope("fwd0"):
        for_off(forward_off, 0)

    with scope("low"):
        need_now("low", "wr", "br", "wml", "vec")

        def reduced(v):
            return jax.nn.relu(
                lax.dot_general(
                    v, r.wr[...], (((1,), (1,)), ((), ())), preferred_element_type=F32
                )
                + r.br[...]
            ).astype(BF16)

        r.lowred[1 : rows + 1] = reduced(r.low[...].reshape(rows * cols, low_w)).reshape(
            rows, cols, lowp
        )
        for side, at, ok, copy in ((0, 0, up_ok, low_dn), (1, rows + 1, dn_ok, low_up)):
            @pl.when(ok)
            def _(side=side, at=at, copy=copy):
                copy.wait_recv()
                r.lowred[at] = reduced(r.low_halo[side])

            @pl.when(jnp.logical_not(ok))
            def _(at=at):
                r.lowred[at] = jnp.zeros((cols, lowp), BF16)

    def combine(mid, left, right, n):
        r.m_l[:n, pl.ds(pad, cols)] = left.reshape(n, cols, br_w)
        r.m_r[:n, pl.ds(pad, cols)] = right.reshape(n, cols, br_w)
        return (
            mid.reshape(n, cols, br_w)
            + r.m_l[:n, pl.ds(pad - 1, cols)]
            + r.m_r[:n, pl.ds(pad + 1, cols)]
        )

    with scope("lowconv"):
        terms = [None] * 3
        for i in range(3):
            lhs = jnp.concatenate([r.lowred[row_of[p] + i] for p in range(live)], axis=0)
            for j in range(3):
                term = jnp.dot(lhs, r.wml[i, j], preferred_element_type=F32)
                terms[j] = term if i == 0 else terms[j] + term
        r.lowacc[...] = combine(terms[1], terms[0], terms[2], live) + r.vec[0].reshape(1, 1, br_w)

    with scope("fwd1"):
        for_off(forward_off, 1)

    need_now("wproj", "bbr")
    with scope("ctx"):
        if nb > 1:
            arrived(all_of(r.pool_b, nb - 1), r.one_r.at[1])
        total = r.pool_b[0]
        for b in range(1, nb):
            total = total + r.pool_b[b]
        pooled = jax.nn.relu(total / (nb * rows * cols) + r.vec[1])
        context = dot_f32(pooled, r.wproj[4 * br_w :])
        own = context[0:1]
        for m in range(1, mb):
            own = jnp.where(mine == m, context[m : m + 1], own)
        base = own + r.vec[2]

    def branch(t, g):
        lo, n = cuts[g]
        k = ORDER[t]
        with scope(f"x{t}{g}"):
            if t == 0:
                x_arrived(g)
            if t == 3:
                for e in range(1, nx):
                    x_copy(t, g, e, True).wait_recv()
        for u in range(4, 4 + n_off):
            if off[u - 4][0] == k:
                @pl.when(gets_from(u))
                def _(u=u):
                    with scope(f"z{g}"):
                        if g < 2:
                            z_copy(u, g).wait_recv()
                    run = pl.ds(lo, n)
                    r.keep_own[t, run] = r.keep_own[t, run] + r.zrecv[u - 4, run].astype(F32)
        total = r.keep_own[t, lo : lo + n]
        for e in range(1, nx):
            total = total + r.xrecv_own[t, lax.rem(xi + e, nx), lo : lo + n].astype(F32)
        total = jax.nn.relu(total + r.bbr[k : k + 1].reshape(1, 1, br_w)).astype(BF16)
        return jnp.dot(
            total.reshape(n * cs, br_w), r.wproj[k * br_w : (k + 1) * br_w],
            preferred_element_type=F32,
        )

    def gather_x(g, e, incoming=False):
        run = pl.ds(*cuts[g])
        other = lax.rem(xi + e, nx)
        slot = other if incoming else xi
        return rcopy(
            r.gath.at[xi, run], r.gath.at[slot, run],
            r.one_s.at[2], r.gx_r.at[g, (e if incoming else nx - e) - 1], sect=other * 2 + core,
        )

    def early(g):
        lo, n = cuts[g]
        acc = branch(0, g)
        for t in (1, 2):
            acc = acc + branch(t, g)
        r.acc[lo : lo + n] = (acc + base).reshape(n, cs, br_w)

    def project(g):
        lo, n = cuts[g]
        last = branch(3, g).reshape(n, cs, br_w)
        done = jax.nn.relu(r.acc[lo : lo + n] + last)
        for p in range(n):
            v = done[p]
            if lo + p < 2:
                v = v * on[(0, rows - 1)[lo + p]].astype(F32)
            r.gath[xi, lo + p] = v.astype(BF16)
        for e in range(1, nx):
            gather_x(g, e).start()

    def halo_copy(side, c):
        return rcopy(
            r.gath.at[c, 1 - side], r.halo.at[side, c], r.h_s.at[side], r.h_r.at[side],
            band=band + 1 if side == 0 else band - 1, sect=sect,
        )

    def send_halo(c):
        for side, ok in ((0, dn_ok), (1, up_ok)):
            @pl.when(ok)
            def _(side=side):
                halo_copy(side, c).start()

    early(0)
    project(0)
    send_halo(xi)
    for g in range(1, n_cut):
        early(g)
    for g in range(1, n_cut):
        project(g)
    for e in range(1, nx):
        with scope("ga"):
            gather_x(0, e, True).wait_recv()
        send_halo(lax.rem(xi + e, nx))
    for c in range(nx):
        for p, y in ((0, 0), (1, rows - 1)):
            r.joined[y + 1, pl.ds(c * cs, cs)] = r.gath[c, p]
    need_now("wmp")
    with scope("gb"):
        for g in range(1, n_cut):
            for e in range(1, nx):
                gather_x(g, e, True).wait_recv()
    with scope("join"):
        for y in range(1, rows - 1):
            for c in range(nx):
                r.joined[y + 1, pl.ds(c * cs, cs)] = (
                    r.gath[c, place_of[y]].astype(F32) * on[y].astype(F32)
                ).astype(BF16)

    def take_halo():
        for side, at, ok in ((0, 0, up_ok), (1, rows + 1, dn_ok)):
            @pl.when(ok)
            def _(side=side, at=at):
                with scope("hw"):
                    arrived(r.halo.at[side], r.h_r.at[side])
                for c in range(nx):
                    r.joined[at, pl.ds(c * cs, cs)] = r.halo[side, c]

    def merged_copy(h):
        run = pl.ds(*halves[h])
        return rcopy(
            r.merged.at[run], r.merged_in.at[run], r.one_s.at[3], r.one_r.at[2], sect=peer
        )

    halves = [(2, live - 2), (0, 2)]
    for h, (lo, n) in enumerate(halves):
        if h == 1:
            take_halo()
        with scope(f"merge{h}"):
            lhs = jnp.concatenate(
                [
                    jnp.concatenate([r.joined[row_of[p] + i] for p in range(lo, lo + n)], axis=0)
                    for i in range(3)
                ],
                axis=1,
            )
            left, mid, right = [
                jnp.dot(lhs, r.wmp[j], preferred_element_type=F32) for j in range(3)
            ]
            total = combine(mid, left, right, n) + r.lowacc[lo : lo + n]
            r.merged[lo : lo + n] = jax.nn.relu(total).astype(BF16)
        merged_copy(h).start()

    def spread(image, src, flags, places):
        for y in range(rows):
            r.out[image, y] = (src[places[y]].astype(F32) * flags[y].astype(F32)).astype(BF16)

    with scope("spread"):
        spread(mine, r.merged, on, place_of)
    with scope("ow"):
        arrived(r.merged, r.one_r.at[2])
    with scope("spread2"):
        spread(theirs, r.merged_in, facts[0][0], facts[0][1])

    @pl.when(up_ok)
    def _():
        low_up.wait_send()

    @pl.when(dn_ok)
    def _():
        low_dn.wait_send()

    def off_sent(t):
        u = t - 4
        core_copy(t).wait_send()
        if nx > 1:
            arrived(all_of(r.xsend_off.at[u], nx - 1), r.x_s.at[1 + u])
        arrived(r.zsend.at[u], r.z_s.at[u])

    for t in range(4, 4 + n_off):
        @pl.when(gets_from(t))
        def _(t=t):
            sel_copy(t).wait_send()
    for_off(off_sent)
    arrived(r.part_own.at[:, 0], r.c_s.at[0])
    if nx > 1:
        arrived(r.xsend_own.at[:, pl.ds(0, nx - 1)], r.x_s.at[0])
        arrived(all_of(r.gath, nx - 1), r.one_s.at[2])
    arrived(all_of(r.pool_s, ns - 1), r.one_s.at[0])
    if nb > 1:
        arrived(all_of(r.pool_b, nb - 1), r.one_s.at[1])
    for side, ok in ((0, dn_ok), (1, up_ok)):
        @pl.when(ok)
        def _(side=side):
            arrived(r.halo.at[side], r.h_s.at[side])
    arrived(r.merged, r.one_s.at[3])


def shards(
    features, low_level, land_mask, weight_one, weight_dilated, bias_branch, weight_pool,
    bias_pool, weight_project, bias_project, weight_reduce, bias_reduce, weight_merging,
    bias_merging,
):
    mb, rows, cols, ch = features.shape
    br_w = weight_project.shape[1]
    dec = weight_merging.shape[3]
    low_w, lowp = weight_reduce.shape
    nb, ns = lax.axis_size("band"), lax.axis_size("sect")
    nx = ns // 2
    cs = cols // nx
    assert mb == 2 and ns % 2 == 0 and rows > 2
    live = rows // LAND_BLOCK * LAND_MOST if rows % LAND_BLOCK == 0 else rows
    off = offsets(rows, nb)
    n_off = max(len(off), 1)
    assert dec == br_w
    n_cut = len(pieces(live))
    n_sel = -(-(live - 2) * (rows - 2) // 8) * 8
    pad = -(-max(DILATIONS) // 8) * 8
    vm, dma = pltpu.VMEM, pltpu.SemaphoreType.DMA
    dims = (mb, rows, cols, ch, br_w, live, nb, ns, low_w, lowp)
    args = dict(
        mask_h=land_mask, feat_h=features, low_h=low_level, w1_h=weight_one, wd_h=weight_dilated,
        bbr_h=bias_branch, wpool_h=weight_pool, bpool_h=bias_pool.reshape(1, -1),
        wproj_h=weight_project, bproj_h=bias_project.reshape(1, -1), wr_h=weight_reduce.T,
        br_h=bias_reduce.reshape(1, -1), wm_h=weight_merging, bm_h=bias_merging.reshape(1, -1),
    )
    scratch = dict(
        mask=pltpu.SMEM(land_mask.shape, jnp.int32),
        feat=vm((1, rows, cols, ch), BF16),
        feat_own=vm((rows, cols, ch), BF16),
        low=vm((rows, cols, low_w), BF16),
        low_halo=vm((2, cols, low_w), BF16),
        w1=vm(weight_one.shape, BF16),
        wpool=vm(weight_pool.shape, BF16),
        sel_out=vm((n_sel, br_w), F32),
        sel_in=vm((n_off, n_sel, br_w), F32),
        wd=vm((3 + len(off), 3, ch, br_w), BF16),
        wproj=vm(weight_project.shape, BF16),
        wmp=vm((3, 3 * br_w, dec), BF16),
        wml=vm((3, 3, lowp, dec), BF16),
        wr=vm((lowp, low_w), BF16),
        br=vm((1, lowp), F32),
        vec=vm((3, 1, br_w), F32),
        bbr=vm(bias_branch.shape, F32),
        m_l=vm((rows, cols + 2 * pad, br_w), F32),
        m_r=vm((rows, cols + 2 * pad, br_w), F32),
        part_off=vm((n_off, 2, rows, cols, br_w), BF16),
        crecv_off=vm((n_off, rows, cols, br_w), BF16),
        xsend_off=vm((n_off, nx, live, cs, br_w), BF16),
        xrecv_off=vm((n_off, nx, live, cs, br_w), BF16),
        zsend=vm((n_off, live, cs, br_w), BF16),
        zrecv=vm((n_off, live, cs, br_w), BF16),
        keep_off=vm((n_off, live, cs, br_w), F32),
        part_own=vm((4, 2, live, cols, br_w), BF16),
        crecv_own=vm((4, live, cols, br_w), BF16),
        xsend_own=vm((4, nx, live, cs, br_w), BF16),
        xrecv_own=vm((4, nx, live, cs, br_w), BF16),
        keep_own=vm((4, live, cs, br_w), F32),
        acc=vm((live, cs, br_w), F32),
        pool_s=vm((ns, mb, br_w), F32),
        pool_b=vm((nb, mb, br_w), F32),
        gath=vm((nx, live, cs, br_w), BF16),
        halo=vm((2, nx, cs, br_w), BF16),
        joined=vm((rows + 2, cols, br_w), BF16),
        lowred=vm((rows + 2, cols, lowp), BF16),
        lowacc=vm((live, cols, dec), F32),
        merged=vm((live, cols, dec), BF16),
        merged_in=vm((live, cols, dec), BF16),
        loc_sem=dma((16,)),
        one_s=dma((4,)),
        one_r=dma((3,)),
        lo_s=dma((2,)),
        lo_r=dma((2,)),
        c_s=dma((1 + n_off,)),
        c_r=dma((4 + n_off,)),
        x_s=dma((1 + n_off,)),
        x_r=dma((2 * n_cut + 2 * n_off, max(nx - 1, 1))),
        s_s=dma((n_off,)),
        s_r=dma((n_off,)),
        z_s=dma((n_off,)),
        z_r=dma((n_off, 2)),
        gx_r=dma((n_cut, max(nx - 1, 1))),
        h_s=dma((2,)),
        h_r=dma((2,)),
    )
    names = (*args, "out", *scratch)
    merged_map = pl.pallas_call(
        functools.partial(kernel, dims, names),
        out_shape=jax.ShapeDtypeStruct((mb, rows, cols, dec), BF16),
        in_specs=[pl.BlockSpec(memory_space=pltpu.HBM)] * len(args),
        out_specs=pl.BlockSpec(memory_space=pltpu.VMEM),
        scratch_shapes=list(scratch.values()),
        compiler_params=pltpu.CompilerParams(
            collective_id=0, has_side_effects=True, vmem_limit_bytes=48 * 1024 * 1024
        ),
    )(*[pltpu.with_memory_space_constraint(a, pltpu.HBM) for a in args.values()])
    return jnp.maximum(merged_map, jnp.zeros_like(merged_map))


def solution(mesh):
    in_specs = (
        P("grp", "band", None, "sect"),
        P("grp", "band", None, None),
        P("grp", "band"),
        P("sect", None),
        P(None, None, None, "sect", None),
        P(),
        P("sect", None),
        P(),
        P(),
        P(),
        P(),
        P(),
        P(),
        P(),
    )
    out_specs = P("grp", "band", None, None)
    return jax.shard_map(shards, mesh=mesh, in_specs=in_specs, out_specs=out_specs, check_vma=False)
```

```python
import functools
import types

import jax
import jax.numpy as jnp
from jax import lax
from jax.experimental import pallas as pl
from jax.experimental.pallas import tpu as pltpu
from jax.sharding import PartitionSpec as P

DILATIONS = (12, 24, 36)
LAND_BLOCK = 6
LAND_MOST = 4
MESH = pl.DeviceIdType.MESH
F32 = jnp.float32
BF16 = jnp.bfloat16
ORDER = (0, 3, 2, 1)


def offsets(rows, bands):
    off = []
    for k in (1, 2, 3):
        d = DILATIONS[k - 1]
        assert d % rows == 0
        hop = d // rows
        if hop < bands:
            off.append((k, 0, hop))
            off.append((k, 2, hop))
    return off


def pieces(live):
    inner = live - 2
    cuts = [(0, 2)]
    if inner > 1:
        cuts += [(2, inner - inner // 2), (live - inner // 2, inner // 2)]
    elif inner:
        cuts.append((2, inner))
    return cuts


def kernel(dims, names, *refs):
    r = types.SimpleNamespace(**dict(zip(names, refs, strict=True)))
    mb, rows, cols, ch, br_w, live, nb, ns, low_w, lowp = dims
    nx = ns // 2
    cs = cols // nx
    off = offsets(rows, nb)
    n_off = len(off)
    cuts = pieces(live)
    n_cut = len(cuts)
    off_cuts = [(0, 2), (2, live - 2)]
    need = [(k, 1) for k in ORDER if k] + [(k, i) for k, i, _ in off]
    pad = (r.m_l.shape[1] - cols) // 2
    scope = jax.named_scope

    band = lax.axis_index("band")
    sect = lax.axis_index("sect")
    core = lax.rem(sect, 2)
    xi = lax.div(sect, 2)
    mine, theirs = core, 1 - core
    peer = xi * 2 + 1 - core

    waits = {}

    def fetch(name, *copies, whole):
        sem = r.loc_sem.at[len(waits)]
        for src, dst in copies:
            pltpu.make_async_copy(src, dst, sem).start()
        waits[name] = pltpu.make_async_copy(whole, whole, sem)

    def need_now(*which):
        for name in which:
            waits[name].wait()

    def taps_of(k, i):
        return r.wd_h.at[k - 1, i], r.wd.at[need.index((k, i))]

    fetch("mask", (r.mask_h, r.mask), whole=r.mask)
    fetch("theirs", (r.feat_h.at[theirs], r.feat.at[0]), whole=r.feat.at[0])
    fetch("w1", (r.w1_h, r.w1), whole=r.w1)
    fetch("mine", (r.feat_h.at[mine], r.feat_own), whole=r.feat_own)
    fetch("wpool", (r.wpool_h, r.wpool), whole=r.wpool)
    if n_off:
        fetch("off", *[taps_of(*n) for n in need[3:]], whole=r.wd.at[pl.ds(3, n_off)])
    fetch("taps0", taps_of(*need[0]), whole=r.wd.at[0])
    fetch("taps1", *[taps_of(*n) for n in need[1:3]], whole=r.wd.at[pl.ds(1, 2)])
    fetch("low", (r.low_h.at[mine], r.low), whole=r.low)
    fetch("wr", (r.wr_h, r.wr), whole=r.wr)
    fetch("br", (r.br_h, r.br), whole=r.br)
    fetch("wml", (r.wm_h.at[:, :, pl.ds(br_w, lowp)], r.wml), whole=r.wml)
    fetch(
        "vec", (r.bm_h, r.vec.at[0]), (r.bpool_h, r.vec.at[1]), (r.bproj_h, r.vec.at[2]),
        whole=r.vec,
    )
    fetch("wproj", (r.wproj_h, r.wproj), whole=r.wproj)
    fetch("bbr", (r.bbr_h, r.bbr), whole=r.bbr)
    fetch(
        "wmp",
        *[
            (r.wm_h.at[i, j, pl.ds(0, br_w)], r.wmp.at[j, pl.ds(i * br_w, br_w)])
            for i in range(3) for j in range(3)
        ],
        whole=r.wmp,
    )

    bar = pltpu.get_barrier_semaphore()
    up_ok = band >= 1
    dn_ok = band + 1 < nb

    def hello(b, s):
        pl.semaphore_signal(bar, inc=1, device_id={"band": b, "sect": s}, device_id_type=MESH)

    for e in range(1, ns):
        hello(band, lax.rem(sect + e, ns))
    for ok, step in ((up_ok, -1), (dn_ok, 1)):
        @pl.when(ok)
        def _(step=step):
            hello(band + step, sect)

    def pass_on(sem, step, ok):
        @pl.when(jnp.logical_and(jnp.logical_and(up_ok, dn_ok), ok))
        def _():
            pl.semaphore_signal(
                sem, inc=1, device_id={"band": band + step, "sect": sect}, device_id_type=MESH
            )

    def word_from(sem, ok):
        @pl.when(ok)
        def _():
            pl.semaphore_wait(sem, 1)

    def rcopy(src, dst, s, rs, **where):
        return pltpu.make_async_remote_copy(
            src_ref=src, dst_ref=dst, send_sem=s, recv_sem=rs, device_id=where, device_id_type=MESH
        )

    low_up = rcopy(
        r.low_h.at[mine, 0], r.low_halo.at[1], r.lo_s.at[0], r.lo_r.at[1], band=band - 1, sect=sect
    )
    low_dn = rcopy(
        r.low_h.at[mine, rows - 1], r.low_halo.at[0], r.lo_s.at[1], r.lo_r.at[0],
        band=band + 1, sect=sect,
    )

    def slots(m):
        on = [r.mask[m, y] for y in range(rows)]
        place_of = [0] + [None] * (rows - 2) + [1]
        row_of = [0, rows - 1] + [jnp.int32(0)] * (live - 2)
        hits = {}
        count = jnp.int32(0)
        for y in range(1, rows - 1):
            place_of[y] = jnp.where(on[y] > 0, jnp.minimum(count + 2, live - 1), 0)
            for p in range(2, live):
                hit = jnp.logical_and(on[y] > 0, count == p - 2)
                row_of[p] = jnp.where(hit, y, row_of[p])
                hits[p, y] = jnp.where(hit, 1, 0)
            count = count + on[y]
        return on, place_of, row_of, hits

    for ref in (r.m_l, r.m_r):
        zero = jnp.zeros((ref.shape[0], pad, br_w), F32)
        ref[:, :pad] = zero
        ref[:, pad + cols :] = zero
    for at in (0, rows + 1):
        r.joined[at] = jnp.zeros((cols, br_w), BF16)

    def taps(lhs, n, wref, d):
        mid = jnp.dot(lhs, wref[1], preferred_element_type=F32).reshape(n, cols, br_w)
        r.m_l[:n, pl.ds(pad, cols)] = jnp.dot(
            lhs, wref[0], preferred_element_type=F32
        ).reshape(n, cols, br_w)
        r.m_r[:n, pl.ds(pad, cols)] = jnp.dot(
            lhs, wref[2], preferred_element_type=F32
        ).reshape(n, cols, br_w)
        return mid + r.m_l[:n, pl.ds(pad - d, cols)] + r.m_r[:n, pl.ds(pad + d, cols)]

    def core_copy(t):
        if t < 4:
            src, dst = r.part_own.at[t, 0], r.crecv_own.at[t]
        else:
            src, dst = r.part_off.at[t - 4, 0], r.crecv_off.at[t - 4]
        return rcopy(src, dst, r.c_s.at[max(t - 3, 0)], r.c_r.at[t], sect=peer)

    def run_of(t, g):
        return cuts[g] if t < 4 else off_cuts[g]

    def x_copy(t, g, e, incoming=False):
        lo, n = run_of(t, g)
        at = g * 2 + t // 3 if t < 4 else 2 * n_cut + (t - 4) * 2 + g
        send, recv, u = (
            (r.xsend_own, r.xrecv_own, t) if t < 4 else (r.xsend_off, r.xrecv_off, t - 4)
        )
        other = lax.rem(xi + e, nx)
        slot = other if incoming else xi
        return rcopy(
            send.at[u, other, pl.ds(lo, n)], recv.at[u, slot, pl.ds(lo, n)],
            r.x_s.at[max(t - 3, 0)], r.x_r.at[at, (e if incoming else nx - e) - 1],
            sect=other * 2 + core,
        )

    def x_arrived(g):
        for e in range(1, nx):
            whole = r.xrecv_own.at[pl.ds(0, 3), lax.rem(xi + e, nx), pl.ds(*cuts[g])]
            arrived(whole, r.x_r.at[g * 2, e - 1])

    def send_x(t, g):
        for e in range(1, nx):
            x_copy(t, g, e).start()

    def first(t, step):
        image = r.feat.at[0] if step == 0 else r.feat_own
        if t < 4:
            k = ORDER[t]
            row_of = facts[step][2]
            lhs = jnp.concatenate([image[row_of[p]] for p in range(live)], axis=0)
            if k:
                val = taps(lhs, live, r.wd.at[need.index((k, 1))], DILATIONS[k - 1])
            else:
                val = jnp.dot(lhs, r.w1[...], preferred_element_type=F32).reshape(live, cols, br_w)
            r.part_own[t, step] = val.astype(BF16)
        else:
            k, i, _ = off[t - 4]
            lhs = image[...].reshape(rows * cols, ch)
            val = taps(lhs, rows, r.wd.at[need.index((k, i))], DILATIONS[k - 1])
            r.part_off[t - 4, step] = val.astype(BF16)

    def second(t):
        core_copy(t).wait_recv()
        for c in range(nx):
            cell = pl.ds(c * cs, cs)
            total = r.part_own[t, 1, :, cell].astype(F32) + r.crecv_own[t, :, cell].astype(F32)
            r.xsend_own[t, c] = total.astype(BF16)

            @pl.when(xi == c)
            def _(total=total):
                r.keep_own[t] = total

    def second_off(t, h):
        u = t - 4
        if h == 0:
            core_copy(t).wait_recv()
        else:
            sel_copy(t).wait_recv()
        lo, n = off_cuts[h]
        for c in range(nx):
            cell = pl.ds(c * cs, cs)

            def row(y, cell=cell):
                return r.part_off[u, 1, y, cell].astype(F32) + r.crecv_off[u, y, cell].astype(F32)

            if h == 0:
                picked = [row(0), row(rows - 1)]
            else:
                inner = [row(y) for y in range(1, rows - 1)]
                picked = []
                for p in range(2, live):
                    total = jnp.zeros((cs, br_w), F32)
                    for y in range(1, rows - 1):
                        at = (p - 2) * (rows - 2) + y - 1
                        total = total + inner[y - 1] * r.sel_in[u, at : at + 1]
                    picked.append(total)
            for p, total in enumerate(picked):
                r.xsend_off[u, c, lo + p] = total.astype(BF16)

            @pl.when(xi == c)
            def _(picked=picked):
                for p, total in enumerate(picked):
                    r.keep_off[u, lo + p] = total

    def sends_to(t):
        k, i, hop = off[t - 4]
        return band + hop < nb if i == 0 else band - hop >= 0

    def gets_from(t):
        k, i, hop = off[t - 4]
        return band - hop >= 0 if i == 0 else band + hop < nb

    def sel_copy(t):
        k, i, hop = off[t - 4]
        return rcopy(
            r.sel_out, r.sel_in.at[t - 4], r.s_s.at[t - 4], r.s_r.at[t - 4],
            band=band - hop if i == 0 else band + hop, sect=sect,
        )

    def z_copy(t, h):
        k, i, hop = off[t - 4]
        run = pl.ds(*off_cuts[h])
        return rcopy(
            r.zsend.at[t - 4, run], r.zrecv.at[t - 4, run], r.z_s.at[t - 4], r.z_r.at[t - 4, h],
            band=band + hop if i == 0 else band - hop, sect=sect,
        )

    def forward_off(t, h):
        run = pl.ds(*off_cuts[h])
        total = r.keep_off[t - 4, run]
        for e in range(1, nx):
            x_copy(t, h, e, True).wait_recv()
            total = total + r.xrecv_off[t - 4, lax.rem(xi + e, nx), run].astype(F32)
        r.zsend[t - 4, run] = total.astype(BF16)
        z_copy(t, h).start()

    def for_off(fn, *rest):
        for t in range(4, 4 + n_off):
            @pl.when(sends_to(t))
            def _(t=t):
                fn(t, *rest)

    def pool_sect(e, incoming=False):
        other = lax.rem(sect + e, ns)
        slot = other if incoming else sect
        return rcopy(
            r.pool_s.at[sect], r.pool_s.at[slot], r.one_s.at[0], r.one_r.at[0], sect=other
        )

    def pool_band(e, incoming=False):
        other = lax.rem(band + e, nb)
        slot = other if incoming else band
        return rcopy(
            r.pool_b.at[band], r.pool_b.at[slot], r.one_s.at[1], r.one_r.at[1], band=other
        )

    def dot_f32(v, w):
        n = v.shape[0]
        high = v.astype(BF16).astype(F32)
        middle = (v - high).astype(BF16).astype(F32)
        terms = jnp.concatenate([high, middle, v - high - middle], axis=0).astype(BF16)
        p = jnp.dot(terms, w, preferred_element_type=F32)
        return p[:n] + p[n : 2 * n] + p[2 * n :]

    def all_of(ref, n):
        return ref.at[pl.ds(0, n)]

    def arrived(whole, sem):
        pltpu.make_async_copy(whole, whole, sem).wait()

    def pool():
        need_now("wpool")
        ones = jnp.ones((8, rows * cols), BF16)
        at = lax.broadcasted_iota(jnp.int32, (8, ch), 0)
        sums = jnp.zeros((8, ch), F32)
        for m, image in ((mine, r.feat_own), (theirs, r.feat.at[0])):
            part = jnp.dot(
                ones, image[...].reshape(rows * cols, ch), preferred_element_type=F32
            )
            sums = jnp.where(at == m, part, sums)
        r.pool_s[sect] = dot_f32(sums, r.wpool[...])[:mb]
        for e in range(1, ns):
            pool_sect(e).start()

    need_now("mask")
    facts = [slots(theirs), slots(mine)]
    on, place_of, row_of, hits = facts[1]

    for p in range(2, live):
        for y in range(1, rows - 1):
            at = (p - 2) * (rows - 2) + y - 1
            r.sel_out[at : at + 1] = jnp.full((1, br_w), hits[p, y].astype(F32))

    def own_half(t, step):
        with scope(f"first{t}{'ab'[step]}"):
            first(t, step)
        if step == 0:
            core_copy(t).start()

    def off_theirs(t):
        first(t, 0)
        core_copy(t).start()

    def off_send(t, h):
        second_off(t, h)
        send_x(t, h)

    with scope("w0"):
        need_now("theirs", "w1")
    with scope("first0a"):
        first(0, 0)
    with scope("bar"):
        sides = jnp.minimum(band, 1) + jnp.minimum(nb - 1 - band, 1)
        pl.semaphore_wait(bar, (ns - 1) + sides)
    core_copy(0).start()
    pass_on(r.above, 1, band < 2)
    pass_on(r.below, -1, band + 2 >= nb)

    def tell(i, ok):
        for t in range(4, 4 + n_off):
            if off[t - 4][1] == i:
                @pl.when(jnp.logical_and(gets_from(t), ok))
                def _(t=t):
                    sel_copy(t).start()

    @pl.when(up_ok)
    def _():
        low_up.start()

    @pl.when(dn_ok)
    def _():
        low_dn.start()

    need_now("mine")
    own_half(0, 1)
    with scope("pool"):
        pool()
    with scope("second0"):
        second(0)
    for g in range(n_cut):
        send_x(0, g)
    with scope("p1"):
        word_from(r.above, band >= 2)
    pass_on(r.above, 1, band >= 2)
    tell(0, band >= 0)
    if n_off:
        need_now("off")
    with scope("offa"):
        for_off(off_theirs)
    need_now("taps0")
    own_half(1, 0)
    with scope("p2"):
        word_from(r.below, jnp.logical_and(up_ok, band + 2 < nb))
    pass_on(r.below, -1, band + 2 < nb)
    tell(2, up_ok)
    with scope("offb"):
        for_off(first, 1)
    with scope("offs0"):
        for_off(off_send, 0)
    own_half(1, 1)
    with scope("second1"):
        second(1)
    for g in range(n_cut):
        send_x(1, g)
    with scope("p3"):
        word_from(r.below, jnp.logical_and(jnp.logical_not(up_ok), band + 2 < nb))
    tell(2, jnp.logical_not(up_ok))
    with scope("poolb"):
        arrived(all_of(r.pool_s, ns - 1), r.one_r.at[0])
        total = r.pool_s[0]
        for s in range(1, ns):
            total = total + r.pool_s[s]
        r.pool_b[band] = total
    for e in range(1, nb):
        pool_band(e).start()
    need_now("taps1")
    own_half(2, 0)
    own_half(3, 0)
    own_half(2, 1)
    with scope("offs1"):
        for_off(off_send, 1)
    with scope("second2"):
        second(2)
    send_x(2, 0)
    own_half(3, 1)
    with scope("second3"):
        second(3)
    send_x(3, 0)
    for t in (2, 3):
        for g in range(1, n_cut):
            send_x(t, g)
    with scope("fwd0"):
        for_off(forward_off, 0)

    with scope("low"):
        need_now("low", "wr", "br", "wml", "vec")

        def reduced(v):
            return jax.nn.relu(
                lax.dot_general(
                    v, r.wr[...], (((1,), (1,)), ((), ())), preferred_element_type=F32
                )
                + r.br[...]
            ).astype(BF16)

        r.lowred[1 : rows + 1] = reduced(r.low[...].reshape(rows * cols, low_w)).reshape(
            rows, cols, lowp
        )
        for side, at, ok, copy in ((0, 0, up_ok, low_dn), (1, rows + 1, dn_ok, low_up)):
            @pl.when(ok)
            def _(side=side, at=at, copy=copy):
                copy.wait_recv()
                r.lowred[at] = reduced(r.low_halo[side])

            @pl.when(jnp.logical_not(ok))
            def _(at=at):
                r.lowred[at] = jnp.zeros((cols, lowp), BF16)

    def combine(mid, left, right, n):
        r.m_l[:n, pl.ds(pad, cols)] = left.reshape(n, cols, br_w)
        r.m_r[:n, pl.ds(pad, cols)] = right.reshape(n, cols, br_w)
        return (
            mid.reshape(n, cols, br_w)
            + r.m_l[:n, pl.ds(pad - 1, cols)]
            + r.m_r[:n, pl.ds(pad + 1, cols)]
        )

    with scope("lowconv"):
        terms = [None] * 3
        for i in range(3):
            lhs = jnp.concatenate([r.lowred[row_of[p] + i] for p in range(live)], axis=0)
            for j in range(3):
                term = jnp.dot(lhs, r.wml[i, j], preferred_element_type=F32)
                terms[j] = term if i == 0 else terms[j] + term
        r.lowacc[...] = combine(terms[1], terms[0], terms[2], live) + r.vec[0].reshape(1, 1, br_w)

    with scope("fwd1"):
        for_off(forward_off, 1)

    need_now("wproj", "bbr")
    with scope("ctx"):
        if nb > 1:
            arrived(all_of(r.pool_b, nb - 1), r.one_r.at[1])
        total = r.pool_b[0]
        for b in range(1, nb):
            total = total + r.pool_b[b]
        pooled = jax.nn.relu(total / (nb * rows * cols) + r.vec[1])
        context = dot_f32(pooled, r.wproj[4 * br_w :])
        own = context[0:1]
        for m in range(1, mb):
            own = jnp.where(mine == m, context[m : m + 1], own)
        base = own + r.vec[2]

    def branch(t, g):
        lo, n = cuts[g]
        k = ORDER[t]
        with scope(f"x{t}{g}"):
            if t == 0:
                x_arrived(g)
            if t == 3:
                for e in range(1, nx):
                    x_copy(t, g, e, True).wait_recv()
        for u in range(4, 4 + n_off):
            if off[u - 4][0] == k:
                @pl.when(gets_from(u))
                def _(u=u):
                    with scope(f"z{g}"):
                        if g < 2:
                            z_copy(u, g).wait_recv()
                    run = pl.ds(lo, n)
                    r.keep_own[t, run] = r.keep_own[t, run] + r.zrecv[u - 4, run].astype(F32)
        total = r.keep_own[t, lo : lo + n]
        for e in range(1, nx):
            total = total + r.xrecv_own[t, lax.rem(xi + e, nx), lo : lo + n].astype(F32)
        total = jax.nn.relu(total + r.bbr[k : k + 1].reshape(1, 1, br_w)).astype(BF16)
        return jnp.dot(
            total.reshape(n * cs, br_w), r.wproj[k * br_w : (k + 1) * br_w],
            preferred_element_type=F32,
        )

    def gather_x(g, e, incoming=False):
        run = pl.ds(*cuts[g])
        other = lax.rem(xi + e, nx)
        slot = other if incoming else xi
        return rcopy(
            r.gath.at[xi, run], r.gath.at[slot, run],
            r.one_s.at[2], r.gx_r.at[g, (e if incoming else nx - e) - 1], sect=other * 2 + core,
        )

    def early(g):
        lo, n = cuts[g]
        acc = branch(0, g)
        for t in (1, 2):
            acc = acc + branch(t, g)
        r.acc[lo : lo + n] = (acc + base).reshape(n, cs, br_w)

    def project(g):
        lo, n = cuts[g]
        last = branch(3, g).reshape(n, cs, br_w)
        done = jax.nn.relu(r.acc[lo : lo + n] + last)
        for p in range(n):
            v = done[p]
            if lo + p < 2:
                v = v * on[(0, rows - 1)[lo + p]].astype(F32)
            r.gath[xi, lo + p] = v.astype(BF16)
        for e in range(1, nx):
            gather_x(g, e).start()

    def halo_copy(side, c):
        return rcopy(
            r.gath.at[c, 1 - side], r.halo.at[side, c], r.h_s.at[side], r.h_r.at[side],
            band=band + 1 if side == 0 else band - 1, sect=sect,
        )

    def send_halo(c):
        for side, ok in ((0, dn_ok), (1, up_ok)):
            @pl.when(ok)
            def _(side=side):
                halo_copy(side, c).start()

    early(0)
    project(0)
    send_halo(xi)
    for g in range(1, n_cut):
        early(g)
    for g in range(1, n_cut):
        project(g)
    for e in range(1, nx):
        with scope("ga"):
            gather_x(0, e, True).wait_recv()
        send_halo(lax.rem(xi + e, nx))
    for c in range(nx):
        for p, y in ((0, 0), (1, rows - 1)):
            r.joined[y + 1, pl.ds(c * cs, cs)] = r.gath[c, p]
    need_now("wmp")
    with scope("gb"):
        for g in range(1, n_cut):
            for e in range(1, nx):
                gather_x(g, e, True).wait_recv()
    with scope("join"):
        for y in range(1, rows - 1):
            for c in range(nx):
                r.joined[y + 1, pl.ds(c * cs, cs)] = (
                    r.gath[c, place_of[y]].astype(F32) * on[y].astype(F32)
                ).astype(BF16)

    def take_halo():
        for side, at, ok in ((0, 0, up_ok), (1, rows + 1, dn_ok)):
            @pl.when(ok)
            def _(side=side, at=at):
                with scope("hw"):
                    arrived(r.halo.at[side], r.h_r.at[side])
                for c in range(nx):
                    r.joined[at, pl.ds(c * cs, cs)] = r.halo[side, c]

    def merged_copy(h):
        run = pl.ds(*halves[h])
        return rcopy(
            r.merged.at[run], r.merged_in.at[run], r.one_s.at[3], r.one_r.at[2], sect=peer
        )

    halves = [(2, live - 2), (0, 2)]
    for h, (lo, n) in enumerate(halves):
        if h == 1:
            take_halo()
        with scope(f"merge{h}"):
            lhs = jnp.concatenate(
                [
                    jnp.concatenate([r.joined[row_of[p] + i] for p in range(lo, lo + n)], axis=0)
                    for i in range(3)
                ],
                axis=1,
            )
            left, mid, right = [
                jnp.dot(lhs, r.wmp[j], preferred_element_type=F32) for j in range(3)
            ]
            total = combine(mid, left, right, n) + r.lowacc[lo : lo + n]
            r.merged[lo : lo + n] = jax.nn.relu(total).astype(BF16)
        merged_copy(h).start()

    def spread(image, src, flags, places):
        for y in range(rows):
            r.out[image, y] = (src[places[y]].astype(F32) * flags[y].astype(F32)).astype(BF16)

    with scope("spread"):
        spread(mine, r.merged, on, place_of)
    with scope("ow"):
        arrived(r.merged, r.one_r.at[2])
    with scope("spread2"):
        spread(theirs, r.merged_in, facts[0][0], facts[0][1])

    @pl.when(up_ok)
    def _():
        low_up.wait_send()

    @pl.when(dn_ok)
    def _():
        low_dn.wait_send()

    def off_sent(t):
        u = t - 4
        core_copy(t).wait_send()
        if nx > 1:
            arrived(all_of(r.xsend_off.at[u], nx - 1), r.x_s.at[1 + u])
        arrived(r.zsend.at[u], r.z_s.at[u])

    for t in range(4, 4 + n_off):
        @pl.when(gets_from(t))
        def _(t=t):
            sel_copy(t).wait_send()
    for_off(off_sent)
    arrived(r.part_own.at[:, 0], r.c_s.at[0])
    if nx > 1:
        arrived(r.xsend_own.at[:, pl.ds(0, nx - 1)], r.x_s.at[0])
        arrived(all_of(r.gath, nx - 1), r.one_s.at[2])
    arrived(all_of(r.pool_s, ns - 1), r.one_s.at[0])
    if nb > 1:
        arrived(all_of(r.pool_b, nb - 1), r.one_s.at[1])
    for side, ok in ((0, dn_ok), (1, up_ok)):
        @pl.when(ok)
        def _(side=side):
            arrived(r.halo.at[side], r.h_s.at[side])
    arrived(r.merged, r.one_s.at[3])


def shards(
    features, low_level, land_mask, weight_one, weight_dilated, bias_branch, weight_pool,
    bias_pool, weight_project, bias_project, weight_reduce, bias_reduce, weight_merging,
    bias_merging,
):
    mb, rows, cols, ch = features.shape
    br_w = weight_project.shape[1]
    dec = weight_merging.shape[3]
    low_w, lowp = weight_reduce.shape
    nb, ns = lax.axis_size("band"), lax.axis_size("sect")
    nx = ns // 2
    cs = cols // nx
    assert mb == 2 and ns % 2 == 0 and rows > 2
    live = rows // LAND_BLOCK * LAND_MOST if rows % LAND_BLOCK == 0 else rows
    off = offsets(rows, nb)
    n_off = max(len(off), 1)
    assert dec == br_w
    n_cut = len(pieces(live))
    n_sel = -(-(live - 2) * (rows - 2) // 8) * 8
    pad = -(-max(DILATIONS) // 8) * 8
    vm, dma = pltpu.VMEM, pltpu.SemaphoreType.DMA
    dims = (mb, rows, cols, ch, br_w, live, nb, ns, low_w, lowp)
    args = dict(
        mask_h=land_mask, feat_h=features, low_h=low_level, w1_h=weight_one, wd_h=weight_dilated,
        bbr_h=bias_branch, wpool_h=weight_pool, bpool_h=bias_pool.reshape(1, -1),
        wproj_h=weight_project, bproj_h=bias_project.reshape(1, -1), wr_h=weight_reduce.T,
        br_h=bias_reduce.reshape(1, -1), wm_h=weight_merging, bm_h=bias_merging.reshape(1, -1),
    )
    scratch = dict(
        mask=pltpu.SMEM(land_mask.shape, jnp.int32),
        feat=vm((1, rows, cols, ch), BF16),
        feat_own=vm((rows, cols, ch), BF16),
        low=vm((rows, cols, low_w), BF16),
        low_halo=vm((2, cols, low_w), BF16),
        w1=vm(weight_one.shape, BF16),
        wpool=vm(weight_pool.shape, BF16),
        sel_out=vm((n_sel, br_w), F32),
        sel_in=vm((n_off, n_sel, br_w), F32),
        wd=vm((3 + len(off), 3, ch, br_w), BF16),
        wproj=vm(weight_project.shape, BF16),
        wmp=vm((3, 3 * br_w, dec), BF16),
        wml=vm((3, 3, lowp, dec), BF16),
        wr=vm((lowp, low_w), BF16),
        br=vm((1, lowp), F32),
        vec=vm((3, 1, br_w), F32),
        bbr=vm(bias_branch.shape, F32),
        m_l=vm((rows, cols + 2 * pad, br_w), F32),
        m_r=vm((rows, cols + 2 * pad, br_w), F32),
        part_off=vm((n_off, 2, rows, cols, br_w), BF16),
        crecv_off=vm((n_off, rows, cols, br_w), BF16),
        xsend_off=vm((n_off, nx, live, cs, br_w), BF16),
        xrecv_off=vm((n_off, nx, live, cs, br_w), BF16),
        zsend=vm((n_off, live, cs, br_w), BF16),
        zrecv=vm((n_off, live, cs, br_w), BF16),
        keep_off=vm((n_off, live, cs, br_w), F32),
        part_own=vm((4, 2, live, cols, br_w), BF16),
        crecv_own=vm((4, live, cols, br_w), BF16),
        xsend_own=vm((4, nx, live, cs, br_w), BF16),
        xrecv_own=vm((4, nx, live, cs, br_w), BF16),
        keep_own=vm((4, live, cs, br_w), F32),
        acc=vm((live, cs, br_w), F32),
        pool_s=vm((ns, mb, br_w), F32),
        pool_b=vm((nb, mb, br_w), F32),
        gath=vm((nx, live, cs, br_w), BF16),
        halo=vm((2, nx, cs, br_w), BF16),
        joined=vm((rows + 2, cols, br_w), BF16),
        lowred=vm((rows + 2, cols, lowp), BF16),
        lowacc=vm((live, cols, dec), F32),
        merged=vm((live, cols, dec), BF16),
        merged_in=vm((live, cols, dec), BF16),
        above=pltpu.SemaphoreType.REGULAR,
        below=pltpu.SemaphoreType.REGULAR,
        loc_sem=dma((16,)),
        one_s=dma((4,)),
        one_r=dma((3,)),
        lo_s=dma((2,)),
        lo_r=dma((2,)),
        c_s=dma((1 + n_off,)),
        c_r=dma((4 + n_off,)),
        x_s=dma((1 + n_off,)),
        x_r=dma((2 * n_cut + 2 * n_off, max(nx - 1, 1))),
        s_s=dma((n_off,)),
        s_r=dma((n_off,)),
        z_s=dma((n_off,)),
        z_r=dma((n_off, 2)),
        gx_r=dma((n_cut, max(nx - 1, 1))),
        h_s=dma((2,)),
        h_r=dma((2,)),
    )
    names = (*args, "out", *scratch)
    merged_map = pl.pallas_call(
        functools.partial(kernel, dims, names),
        out_shape=jax.ShapeDtypeStruct((mb, rows, cols, dec), BF16),
        in_specs=[pl.BlockSpec(memory_space=pltpu.HBM)] * len(args),
        out_specs=pl.BlockSpec(memory_space=pltpu.VMEM),
        scratch_shapes=list(scratch.values()),
        compiler_params=pltpu.CompilerParams(
            collective_id=0, has_side_effects=True, vmem_limit_bytes=48 * 1024 * 1024
        ),
    )(*[pltpu.with_memory_space_constraint(a, pltpu.HBM) for a in args.values()])
    return jnp.maximum(merged_map, jnp.zeros_like(merged_map))


def solution(mesh):
    in_specs = (
        P("grp", "band", None, "sect"),
        P("grp", "band", None, None),
        P("grp", "band"),
        P("sect", None),
        P(None, None, None, "sect", None),
        P(),
        P("sect", None),
        P(),
        P(),
        P(),
        P(),
        P(),
        P(),
        P(),
    )
    out_specs = P("grp", "band", None, None)
    return jax.shard_map(shards, mesh=mesh, in_specs=in_specs, out_specs=out_specs, check_vma=False)
```

```python
import functools
import types

import jax
import jax.numpy as jnp
from jax import lax
from jax.experimental import pallas as pl
from jax.experimental.pallas import tpu as pltpu
from jax.sharding import PartitionSpec as P

DILATIONS = (12, 24, 36)
LAND_BLOCK = 6
LAND_MOST = 4
MESH = pl.DeviceIdType.MESH
F32 = jnp.float32
BF16 = jnp.bfloat16
ORDER = (0, 3, 2, 1)


def offsets(rows, bands):
    off = []
    for k in (1, 2, 3):
        d = DILATIONS[k - 1]
        assert d % rows == 0
        hop = d // rows
        if hop < bands:
            off.append((k, 0, hop))
            off.append((k, 2, hop))
    return off


def pieces(live):
    inner = live - 2
    cuts = [(0, 2)]
    if inner > 1:
        cuts += [(2, inner - inner // 2), (live - inner // 2, inner // 2)]
    elif inner:
        cuts.append((2, inner))
    return cuts


def kernel(dims, names, *refs):
    r = types.SimpleNamespace(**dict(zip(names, refs, strict=True)))
    mb, rows, cols, ch, br_w, live, nb, ns, low_w, lowp = dims
    nx = ns // 2
    cs = cols // nx
    off = offsets(rows, nb)
    n_off = len(off)
    cuts = pieces(live)
    n_cut = len(cuts)
    off_cuts = [(0, 2), (2, live - 2)]
    need = [(k, 1) for k in ORDER if k] + [(k, i) for k, i, _ in off]
    pad = (r.m_l.shape[1] - cols) // 2
    scope = jax.named_scope

    band = lax.axis_index("band")
    sect = lax.axis_index("sect")
    core = lax.rem(sect, 2)
    xi = lax.div(sect, 2)
    mine, theirs = core, 1 - core
    peer = xi * 2 + 1 - core

    bar = pltpu.get_barrier_semaphore()
    up_ok = band >= 1
    dn_ok = band + 1 < nb

    def hello(b, s):
        pl.semaphore_signal(bar, inc=1, device_id={"band": b, "sect": s}, device_id_type=MESH)

    for e in range(1, ns):
        hello(band, lax.rem(sect + e, ns))
    for ok, step in ((up_ok, -1), (dn_ok, 1)):
        @pl.when(ok)
        def _(step=step):
            hello(band + step, sect)

    waits = {}

    def fetch(name, *copies, whole):
        sem = r.loc_sem.at[len(waits)]
        for src, dst in copies:
            pltpu.make_async_copy(src, dst, sem).start()
        waits[name] = pltpu.make_async_copy(whole, whole, sem)

    def need_now(*which):
        for name in which:
            waits[name].wait()

    def taps_of(k, i):
        return r.wd_h.at[k - 1, i], r.wd.at[need.index((k, i))]

    fetch("mask", (r.mask_h, r.mask), whole=r.mask)
    fetch("theirs", (r.feat_h.at[theirs], r.feat.at[0]), whole=r.feat.at[0])
    fetch("w1", (r.w1_h, r.w1), whole=r.w1)
    fetch("mine", (r.feat_h.at[mine], r.feat_own), whole=r.feat_own)
    fetch("wpool", (r.wpool_h, r.wpool), whole=r.wpool)
    def pass_on(sem, step, ok):
        @pl.when(jnp.logical_and(jnp.logical_and(up_ok, dn_ok), ok))
        def _():
            pl.semaphore_signal(
                sem, inc=1, device_id={"band": band + step, "sect": sect}, device_id_type=MESH
            )

    def word_from(sem, ok):
        @pl.when(ok)
        def _():
            pl.semaphore_wait(sem, 1)

    def rcopy(src, dst, s, rs, **where):
        return pltpu.make_async_remote_copy(
            src_ref=src, dst_ref=dst, send_sem=s, recv_sem=rs, device_id=where, device_id_type=MESH
        )

    low_up = rcopy(
        r.low_h.at[mine, 0], r.low_halo.at[1], r.lo_s.at[0], r.lo_r.at[1], band=band - 1, sect=sect
    )
    low_dn = rcopy(
        r.low_h.at[mine, rows - 1], r.low_halo.at[0], r.lo_s.at[1], r.lo_r.at[0],
        band=band + 1, sect=sect,
    )

    def slots(m):
        on = [r.mask[m, y] for y in range(rows)]
        place_of = [0] + [None] * (rows - 2) + [1]
        row_of = [0, rows - 1] + [jnp.int32(0)] * (live - 2)
        hits = {}
        count = jnp.int32(0)
        for y in range(1, rows - 1):
            place_of[y] = jnp.where(on[y] > 0, jnp.minimum(count + 2, live - 1), 0)
            for p in range(2, live):
                hit = jnp.logical_and(on[y] > 0, count == p - 2)
                row_of[p] = jnp.where(hit, y, row_of[p])
                hits[p, y] = jnp.where(hit, 1, 0)
            count = count + on[y]
        return on, place_of, row_of, hits

    for ref in (r.m_l, r.m_r):
        zero = jnp.zeros((ref.shape[0], pad, br_w), F32)
        ref[:, :pad] = zero
        ref[:, pad + cols :] = zero
    for at in (0, rows + 1):
        r.joined[at] = jnp.zeros((cols, br_w), BF16)

    def taps(lhs, n, wref, d):
        mid = jnp.dot(lhs, wref[1], preferred_element_type=F32).reshape(n, cols, br_w)
        r.m_l[:n, pl.ds(pad, cols)] = jnp.dot(
            lhs, wref[0], preferred_element_type=F32
        ).reshape(n, cols, br_w)
        r.m_r[:n, pl.ds(pad, cols)] = jnp.dot(
            lhs, wref[2], preferred_element_type=F32
        ).reshape(n, cols, br_w)
        return mid + r.m_l[:n, pl.ds(pad - d, cols)] + r.m_r[:n, pl.ds(pad + d, cols)]

    def core_copy(t):
        if t < 4:
            src, dst = r.part_own.at[t, 0], r.crecv_own.at[t]
        else:
            src, dst = r.part_off.at[t - 4, 0], r.crecv_off.at[t - 4]
        return rcopy(src, dst, r.c_s.at[max(t - 3, 0)], r.c_r.at[t], sect=peer)

    def run_of(t, g):
        return cuts[g] if t < 4 else off_cuts[g]

    def x_copy(t, g, e, incoming=False):
        lo, n = run_of(t, g)
        at = g * 2 + t // 3 if t < 4 else 2 * n_cut + (t - 4) * 2 + g
        send, recv, u = (
            (r.xsend_own, r.xrecv_own, t) if t < 4 else (r.xsend_off, r.xrecv_off, t - 4)
        )
        other = lax.rem(xi + e, nx)
        slot = other if incoming else xi
        return rcopy(
            send.at[u, other, pl.ds(lo, n)], recv.at[u, slot, pl.ds(lo, n)],
            r.x_s.at[max(t - 3, 0)], r.x_r.at[at, (e if incoming else nx - e) - 1],
            sect=other * 2 + core,
        )

    def x_arrived(g):
        for e in range(1, nx):
            whole = r.xrecv_own.at[pl.ds(0, 3), lax.rem(xi + e, nx), pl.ds(*cuts[g])]
            arrived(whole, r.x_r.at[g * 2, e - 1])

    def send_x(t, g):
        for e in range(1, nx):
            x_copy(t, g, e).start()

    def first(t, step):
        image = r.feat.at[0] if step == 0 else r.feat_own
        if t < 4:
            k = ORDER[t]
            row_of = facts[step][2]
            lhs = jnp.concatenate([image[row_of[p]] for p in range(live)], axis=0)
            if k:
                val = taps(lhs, live, r.wd.at[need.index((k, 1))], DILATIONS[k - 1])
            else:
                val = jnp.dot(lhs, r.w1[...], preferred_element_type=F32).reshape(live, cols, br_w)
            r.part_own[t, step] = val.astype(BF16)
        else:
            k, i, _ = off[t - 4]
            lhs = image[...].reshape(rows * cols, ch)
            val = taps(lhs, rows, r.wd.at[need.index((k, i))], DILATIONS[k - 1])
            r.part_off[t - 4, step] = val.astype(BF16)

    def second(t):
        core_copy(t).wait_recv()
        for c in range(nx):
            cell = pl.ds(c * cs, cs)
            total = r.part_own[t, 1, :, cell].astype(F32) + r.crecv_own[t, :, cell].astype(F32)
            r.xsend_own[t, c] = total.astype(BF16)

            @pl.when(xi == c)
            def _(total=total):
                r.keep_own[t] = total

    def second_off(t, h):
        u = t - 4
        if h == 0:
            core_copy(t).wait_recv()
        else:
            sel_copy(t).wait_recv()
        lo, n = off_cuts[h]
        for c in range(nx):
            cell = pl.ds(c * cs, cs)

            def row(y, cell=cell):
                return r.part_off[u, 1, y, cell].astype(F32) + r.crecv_off[u, y, cell].astype(F32)

            if h == 0:
                picked = [row(0), row(rows - 1)]
            else:
                inner = [row(y) for y in range(1, rows - 1)]
                picked = []
                for p in range(2, live):
                    total = jnp.zeros((cs, br_w), F32)
                    for y in range(1, rows - 1):
                        at = (p - 2) * (rows - 2) + y - 1
                        total = total + inner[y - 1] * r.sel_in[u, at : at + 1]
                    picked.append(total)
            for p, total in enumerate(picked):
                r.xsend_off[u, c, lo + p] = total.astype(BF16)

            @pl.when(xi == c)
            def _(picked=picked):
                for p, total in enumerate(picked):
                    r.keep_off[u, lo + p] = total

    def sends_to(t):
        k, i, hop = off[t - 4]
        return band + hop < nb if i == 0 else band - hop >= 0

    def gets_from(t):
        k, i, hop = off[t - 4]
        return band - hop >= 0 if i == 0 else band + hop < nb

    def sel_copy(t):
        k, i, hop = off[t - 4]
        return rcopy(
            r.sel_out, r.sel_in.at[t - 4], r.s_s.at[t - 4], r.s_r.at[t - 4],
            band=band - hop if i == 0 else band + hop, sect=sect,
        )

    def z_copy(t, h):
        k, i, hop = off[t - 4]
        run = pl.ds(*off_cuts[h])
        return rcopy(
            r.zsend.at[t - 4, run], r.zrecv.at[t - 4, run], r.z_s.at[t - 4], r.z_r.at[t - 4, h],
            band=band + hop if i == 0 else band - hop, sect=sect,
        )

    def forward_off(t, h):
        run = pl.ds(*off_cuts[h])
        total = r.keep_off[t - 4, run]
        for e in range(1, nx):
            x_copy(t, h, e, True).wait_recv()
            total = total + r.xrecv_off[t - 4, lax.rem(xi + e, nx), run].astype(F32)
        r.zsend[t - 4, run] = total.astype(BF16)
        z_copy(t, h).start()

    def for_off(fn, *rest):
        for t in range(4, 4 + n_off):
            @pl.when(sends_to(t))
            def _(t=t):
                fn(t, *rest)

    def pool_sect(e, incoming=False):
        other = lax.rem(sect + e, ns)
        slot = other if incoming else sect
        return rcopy(
            r.pool_s.at[sect], r.pool_s.at[slot], r.one_s.at[0], r.one_r.at[0], sect=other
        )

    def pool_band(e, incoming=False):
        other = lax.rem(band + e, nb)
        slot = other if incoming else band
        return rcopy(
            r.pool_b.at[band], r.pool_b.at[slot], r.one_s.at[1], r.one_r.at[1], band=other
        )

    def dot_f32(v, w):
        n = v.shape[0]
        high = v.astype(BF16).astype(F32)
        middle = (v - high).astype(BF16).astype(F32)
        terms = jnp.concatenate([high, middle, v - high - middle], axis=0).astype(BF16)
        p = jnp.dot(terms, w, preferred_element_type=F32)
        return p[:n] + p[n : 2 * n] + p[2 * n :]

    def all_of(ref, n):
        return ref.at[pl.ds(0, n)]

    def arrived(whole, sem):
        pltpu.make_async_copy(whole, whole, sem).wait()

    def pool():
        need_now("wpool")
        ones = jnp.ones((8, rows * cols), BF16)
        at = lax.broadcasted_iota(jnp.int32, (8, ch), 0)
        sums = jnp.zeros((8, ch), F32)
        for m, image in ((mine, r.feat_own), (theirs, r.feat.at[0])):
            part = jnp.dot(
                ones, image[...].reshape(rows * cols, ch), preferred_element_type=F32
            )
            sums = jnp.where(at == m, part, sums)
        r.pool_s[sect] = dot_f32(sums, r.wpool[...])[:mb]
        for e in range(1, ns):
            pool_sect(e).start()

    need_now("mask")
    facts = [slots(theirs), slots(mine)]
    on, place_of, row_of, hits = facts[1]

    for p in range(2, live):
        for y in range(1, rows - 1):
            at = (p - 2) * (rows - 2) + y - 1
            r.sel_out[at : at + 1] = jnp.full((1, br_w), hits[p, y].astype(F32))

    def own_half(t, step):
        with scope(f"first{t}{'ab'[step]}"):
            first(t, step)
        if step == 0:
            core_copy(t).start()

    def off_theirs(t):
        first(t, 0)
        core_copy(t).start()

    def off_send(t, h):
        second_off(t, h)
        send_x(t, h)

    with scope("w0"):
        need_now("theirs", "w1")
    if n_off:
        fetch("off", *[taps_of(*n) for n in need[3:]], whole=r.wd.at[pl.ds(3, n_off)])
    fetch("taps0", taps_of(*need[0]), whole=r.wd.at[0])
    fetch("taps1", *[taps_of(*n) for n in need[1:3]], whole=r.wd.at[pl.ds(1, 2)])
    fetch("low", (r.low_h.at[mine], r.low), whole=r.low)
    fetch("wr", (r.wr_h, r.wr), whole=r.wr)
    fetch("br", (r.br_h, r.br), whole=r.br)
    fetch("wml", (r.wm_h.at[:, :, pl.ds(br_w, lowp)], r.wml), whole=r.wml)
    fetch(
        "vec", (r.bm_h, r.vec.at[0]), (r.bpool_h, r.vec.at[1]), (r.bproj_h, r.vec.at[2]),
        whole=r.vec,
    )
    fetch("wproj", (r.wproj_h, r.wproj), whole=r.wproj)
    fetch("bbr", (r.bbr_h, r.bbr), whole=r.bbr)
    fetch(
        "wmp",
        *[
            (r.wm_h.at[i, j, pl.ds(0, br_w)], r.wmp.at[j, pl.ds(i * br_w, br_w)])
            for i in range(3) for j in range(3)
        ],
        whole=r.wmp,
    )
    with scope("first0a"):
        first(0, 0)
    with scope("bar"):
        sides = jnp.minimum(band, 1) + jnp.minimum(nb - 1 - band, 1)
        pl.semaphore_wait(bar, (ns - 1) + sides)
    core_copy(0).start()
    for e in range(1, nx):
        pl.semaphore_signal(
            r.across, inc=1, device_id={"sect": lax.rem(sect + 2 * e, ns)}, device_id_type=MESH
        )
    pass_on(r.above, 1, band < 2)
    pass_on(r.below, -1, band + 2 >= nb)

    def tell(i, ok):
        for t in range(4, 4 + n_off):
            if off[t - 4][1] == i:
                @pl.when(jnp.logical_and(gets_from(t), ok))
                def _(t=t):
                    sel_copy(t).start()

    @pl.when(up_ok)
    def _():
        low_up.start()

    @pl.when(dn_ok)
    def _():
        low_dn.start()

    need_now("mine")
    own_half(0, 1)
    with scope("pool"):
        pool()
    with scope("second0"):
        second(0)
    for g in range(n_cut):
        send_x(0, g)
    with scope("p1"):
        word_from(r.above, band >= 2)
    pass_on(r.above, 1, band >= 2)
    tell(0, band >= 0)
    if n_off:
        need_now("off")
    with scope("offa"):
        for_off(off_theirs)
    with scope("p2"):
        word_from(r.below, jnp.logical_and(up_ok, band + 2 < nb))
    pass_on(r.below, -1, band + 2 < nb)
    tell(2, up_ok)
    need_now("taps0")
    own_half(1, 0)
    with scope("offb"):
        for_off(first, 1)
    with scope("offs0"):
        for_off(off_send, 0)
    with scope("p3"):
        word_from(r.below, jnp.logical_and(jnp.logical_not(up_ok), band + 2 < nb))
    tell(2, jnp.logical_not(up_ok))
    own_half(1, 1)
    with scope("second1"):
        second(1)
    for g in range(n_cut - 1):
        send_x(1, g)
    with scope("poolb"):
        arrived(all_of(r.pool_s, ns - 1), r.one_r.at[0])
        total = r.pool_s[0]
        for s in range(1, ns):
            total = total + r.pool_s[s]
        r.pool_b[band] = total
    for e in range(1, nb):
        pool_band(e).start()
    need_now("taps1")
    own_half(2, 0)
    own_half(3, 0)
    own_half(2, 1)
    with scope("offs1"):
        for_off(off_send, 1)
    send_x(1, n_cut - 1)
    with scope("second2"):
        second(2)
    send_x(2, 0)
    own_half(3, 1)
    with scope("second3"):
        second(3)
    send_x(3, 0)
    for t in (2, 3):
        for g in range(1, n_cut):
            send_x(t, g)
    with scope("fwd0"):
        for_off(forward_off, 0)

    with scope("low"):
        need_now("low", "wr", "br", "wml", "vec")

        def reduced(v):
            return jax.nn.relu(
                lax.dot_general(
                    v, r.wr[...], (((1,), (1,)), ((), ())), preferred_element_type=F32
                )
                + r.br[...]
            ).astype(BF16)

        r.lowred[1 : rows + 1] = reduced(r.low[...].reshape(rows * cols, low_w)).reshape(
            rows, cols, lowp
        )
        for side, at, ok, copy in ((0, 0, up_ok, low_dn), (1, rows + 1, dn_ok, low_up)):
            @pl.when(ok)
            def _(side=side, at=at, copy=copy):
                copy.wait_recv()
                r.lowred[at] = reduced(r.low_halo[side])

            @pl.when(jnp.logical_not(ok))
            def _(at=at):
                r.lowred[at] = jnp.zeros((cols, lowp), BF16)

    def combine(mid, left, right, n):
        r.m_l[:n, pl.ds(pad, cols)] = left.reshape(n, cols, br_w)
        r.m_r[:n, pl.ds(pad, cols)] = right.reshape(n, cols, br_w)
        return (
            mid.reshape(n, cols, br_w)
            + r.m_l[:n, pl.ds(pad - 1, cols)]
            + r.m_r[:n, pl.ds(pad + 1, cols)]
        )

    with scope("lowconv"):
        terms = [None] * 3
        for i in range(3):
            lhs = jnp.concatenate([r.lowred[row_of[p] + i] for p in range(live)], axis=0)
            for j in range(3):
                term = jnp.dot(lhs, r.wml[i, j], preferred_element_type=F32)
                terms[j] = term if i == 0 else terms[j] + term
        r.lowacc[...] = combine(terms[1], terms[0], terms[2], live) + r.vec[0].reshape(1, 1, br_w)

    with scope("fwd1"):
        for_off(forward_off, 1)

    need_now("wproj", "bbr")
    with scope("ctx"):
        if nb > 1:
            arrived(all_of(r.pool_b, nb - 1), r.one_r.at[1])
        total = r.pool_b[0]
        for b in range(1, nb):
            total = total + r.pool_b[b]
        pooled = jax.nn.relu(total / (nb * rows * cols) + r.vec[1])
        context = dot_f32(pooled, r.wproj[4 * br_w :])
        own = context[0:1]
        for m in range(1, mb):
            own = jnp.where(mine == m, context[m : m + 1], own)
        base = own + r.vec[2]

    def branch(t, g):
        lo, n = cuts[g]
        k = ORDER[t]
        with scope(f"x{t}{g}"):
            if t == 0:
                x_arrived(g)
            if t == 3:
                for e in range(1, nx):
                    x_copy(t, g, e, True).wait_recv()
        for u in range(4, 4 + n_off):
            if off[u - 4][0] == k:
                @pl.when(gets_from(u))
                def _(u=u):
                    with scope(f"z{g}"):
                        if g < 2:
                            z_copy(u, g).wait_recv()
                    run = pl.ds(lo, n)
                    r.keep_own[t, run] = r.keep_own[t, run] + r.zrecv[u - 4, run].astype(F32)
        total = r.keep_own[t, lo : lo + n]
        for e in range(1, nx):
            total = total + r.xrecv_own[t, lax.rem(xi + e, nx), lo : lo + n].astype(F32)
        total = jax.nn.relu(total + r.bbr[k : k + 1].reshape(1, 1, br_w)).astype(BF16)
        return jnp.dot(
            total.reshape(n * cs, br_w), r.wproj[k * br_w : (k + 1) * br_w],
            preferred_element_type=F32,
        )

    def gather_x(g, e, incoming=False):
        run = pl.ds(*cuts[g])
        other = lax.rem(xi + e, nx)
        slot = other if incoming else xi
        return rcopy(
            r.gath.at[xi, run], r.gath.at[slot, run],
            r.one_s.at[2], r.gx_r.at[g, (e if incoming else nx - e) - 1], sect=other * 2 + core,
        )

    def early(g):
        lo, n = cuts[g]
        acc = branch(0, g)
        for t in (1, 2):
            acc = acc + branch(t, g)
        r.acc[lo : lo + n] = (acc + base).reshape(n, cs, br_w)

    def project(g):
        lo, n = cuts[g]
        last = branch(3, g).reshape(n, cs, br_w)
        done = jax.nn.relu(r.acc[lo : lo + n] + last)
        for p in range(n):
            v = done[p]
            if lo + p < 2:
                v = v * on[(0, rows - 1)[lo + p]].astype(F32)
            r.gath[xi, lo + p] = v.astype(BF16)
        if g == 0:
            if nx > 1:
                pl.semaphore_wait(r.across, nx - 1)
            for e in reversed(range(nx)):
                for side, ok in ((0, dn_ok), (1, up_ok)):
                    @pl.when(ok)
                    def _(side=side, e=e):
                        halo_copy(side, e).start()
        for e in range(1, nx):
            gather_x(g, e).start()

    def halo_copy(side, e):
        other = lax.rem(xi + e, nx)
        return rcopy(
            r.gath.at[xi, 1 - side], r.halo.at[side, xi], r.h_s.at[side], r.h_r.at[side],
            band=band + 1 if side == 0 else band - 1, sect=other * 2 + core,
        )

    early(0)
    project(0)
    for g in range(1, n_cut):
        early(g)
    for g in range(1, n_cut):
        project(g)
    with scope("ga"):
        for e in range(1, nx):
            gather_x(0, e, True).wait_recv()
    for c in range(nx):
        for p, y in ((0, 0), (1, rows - 1)):
            r.joined[y + 1, pl.ds(c * cs, cs)] = r.gath[c, p]
    need_now("wmp")
    with scope("gb"):
        for g in range(1, n_cut):
            for e in range(1, nx):
                gather_x(g, e, True).wait_recv()
    with scope("join"):
        for y in range(1, rows - 1):
            for c in range(nx):
                r.joined[y + 1, pl.ds(c * cs, cs)] = (
                    r.gath[c, place_of[y]].astype(F32) * on[y].astype(F32)
                ).astype(BF16)

    def take_halo():
        for side, at, ok in ((0, 0, up_ok), (1, rows + 1, dn_ok)):
            @pl.when(ok)
            def _(side=side, at=at):
                with scope("hw"):
                    arrived(r.halo.at[side], r.h_r.at[side])
                for c in range(nx):
                    r.joined[at, pl.ds(c * cs, cs)] = r.halo[side, c]

    def merged_copy(h):
        run = pl.ds(*halves[h])
        return rcopy(
            r.merged.at[run], r.merged_in.at[run], r.one_s.at[3], r.one_r.at[2], sect=peer
        )

    halves = [(2, live - 2), (0, 2)]
    for h, (lo, n) in enumerate(halves):
        if h == 1:
            take_halo()
        with scope(f"merge{h}"):
            lhs = jnp.concatenate(
                [
                    jnp.concatenate([r.joined[row_of[p] + i] for p in range(lo, lo + n)], axis=0)
                    for i in range(3)
                ],
                axis=1,
            )
            left, mid, right = [
                jnp.dot(lhs, r.wmp[j], preferred_element_type=F32) for j in range(3)
            ]
            total = combine(mid, left, right, n) + r.lowacc[lo : lo + n]
            r.merged[lo : lo + n] = jax.nn.relu(total).astype(BF16)
        merged_copy(h).start()

    def spread(image, src, flags, places):
        for y in range(rows):
            r.out[image, y] = (src[places[y]].astype(F32) * flags[y].astype(F32)).astype(BF16)

    with scope("spread"):
        spread(mine, r.merged, on, place_of)
    with scope("ow"):
        arrived(r.merged, r.one_r.at[2])
    with scope("spread2"):
        spread(theirs, r.merged_in, facts[0][0], facts[0][1])

    @pl.when(up_ok)
    def _():
        low_up.wait_send()

    @pl.when(dn_ok)
    def _():
        low_dn.wait_send()

    def off_sent(t):
        u = t - 4
        core_copy(t).wait_send()
        if nx > 1:
            arrived(all_of(r.xsend_off.at[u], nx - 1), r.x_s.at[1 + u])
        arrived(r.zsend.at[u], r.z_s.at[u])

    for t in range(4, 4 + n_off):
        @pl.when(gets_from(t))
        def _(t=t):
            sel_copy(t).wait_send()
    for_off(off_sent)
    arrived(r.part_own.at[:, 0], r.c_s.at[0])
    if nx > 1:
        arrived(r.xsend_own.at[:, pl.ds(0, nx - 1)], r.x_s.at[0])
        arrived(all_of(r.gath, nx - 1), r.one_s.at[2])
    arrived(all_of(r.pool_s, ns - 1), r.one_s.at[0])
    if nb > 1:
        arrived(all_of(r.pool_b, nb - 1), r.one_s.at[1])
    for side, ok in ((0, dn_ok), (1, up_ok)):
        @pl.when(ok)
        def _(side=side):
            arrived(r.halo.at[side], r.h_s.at[side])
    arrived(r.merged, r.one_s.at[3])


def shards(
    features, low_level, land_mask, weight_one, weight_dilated, bias_branch, weight_pool,
    bias_pool, weight_project, bias_project, weight_reduce, bias_reduce, weight_merging,
    bias_merging,
):
    mb, rows, cols, ch = features.shape
    br_w = weight_project.shape[1]
    dec = weight_merging.shape[3]
    low_w, lowp = weight_reduce.shape
    nb, ns = lax.axis_size("band"), lax.axis_size("sect")
    nx = ns // 2
    cs = cols // nx
    assert mb == 2 and ns % 2 == 0 and rows > 2
    live = rows // LAND_BLOCK * LAND_MOST if rows % LAND_BLOCK == 0 else rows
    off = offsets(rows, nb)
    n_off = max(len(off), 1)
    assert dec == br_w
    n_cut = len(pieces(live))
    n_sel = -(-(live - 2) * (rows - 2) // 8) * 8
    pad = -(-max(DILATIONS) // 8) * 8
    vm, dma = pltpu.VMEM, pltpu.SemaphoreType.DMA
    dims = (mb, rows, cols, ch, br_w, live, nb, ns, low_w, lowp)
    args = dict(
        mask_h=land_mask, feat_h=features, low_h=low_level, w1_h=weight_one, wd_h=weight_dilated,
        bbr_h=bias_branch, wpool_h=weight_pool, bpool_h=bias_pool.reshape(1, -1),
        wproj_h=weight_project, bproj_h=bias_project.reshape(1, -1), wr_h=weight_reduce.T,
        br_h=bias_reduce.reshape(1, -1), wm_h=weight_merging, bm_h=bias_merging.reshape(1, -1),
    )
    scratch = dict(
        mask=pltpu.SMEM(land_mask.shape, jnp.int32),
        feat=vm((1, rows, cols, ch), BF16),
        feat_own=vm((rows, cols, ch), BF16),
        low=vm((rows, cols, low_w), BF16),
        low_halo=vm((2, cols, low_w), BF16),
        w1=vm(weight_one.shape, BF16),
        wpool=vm(weight_pool.shape, BF16),
        sel_out=vm((n_sel, br_w), F32),
        sel_in=vm((n_off, n_sel, br_w), F32),
        wd=vm((3 + len(off), 3, ch, br_w), BF16),
        wproj=vm(weight_project.shape, BF16),
        wmp=vm((3, 3 * br_w, dec), BF16),
        wml=vm((3, 3, lowp, dec), BF16),
        wr=vm((lowp, low_w), BF16),
        br=vm((1, lowp), F32),
        vec=vm((3, 1, br_w), F32),
        bbr=vm(bias_branch.shape, F32),
        m_l=vm((rows, cols + 2 * pad, br_w), F32),
        m_r=vm((rows, cols + 2 * pad, br_w), F32),
        part_off=vm((n_off, 2, rows, cols, br_w), BF16),
        crecv_off=vm((n_off, rows, cols, br_w), BF16),
        xsend_off=vm((n_off, nx, live, cs, br_w), BF16),
        xrecv_off=vm((n_off, nx, live, cs, br_w), BF16),
        zsend=vm((n_off, live, cs, br_w), BF16),
        zrecv=vm((n_off, live, cs, br_w), BF16),
        keep_off=vm((n_off, live, cs, br_w), F32),
        part_own=vm((4, 2, live, cols, br_w), BF16),
        crecv_own=vm((4, live, cols, br_w), BF16),
        xsend_own=vm((4, nx, live, cs, br_w), BF16),
        xrecv_own=vm((4, nx, live, cs, br_w), BF16),
        keep_own=vm((4, live, cs, br_w), F32),
        acc=vm((live, cs, br_w), F32),
        pool_s=vm((ns, mb, br_w), F32),
        pool_b=vm((nb, mb, br_w), F32),
        gath=vm((nx, live, cs, br_w), BF16),
        halo=vm((2, nx, cs, br_w), BF16),
        joined=vm((rows + 2, cols, br_w), BF16),
        lowred=vm((rows + 2, cols, lowp), BF16),
        lowacc=vm((live, cols, dec), F32),
        merged=vm((live, cols, dec), BF16),
        merged_in=vm((live, cols, dec), BF16),
        across=pltpu.SemaphoreType.REGULAR,
        above=pltpu.SemaphoreType.REGULAR,
        below=pltpu.SemaphoreType.REGULAR,
        loc_sem=dma((16,)),
        one_s=dma((4,)),
        one_r=dma((3,)),
        lo_s=dma((2,)),
        lo_r=dma((2,)),
        c_s=dma((1 + n_off,)),
        c_r=dma((4 + n_off,)),
        x_s=dma((1 + n_off,)),
        x_r=dma((2 * n_cut + 2 * n_off, max(nx - 1, 1))),
        s_s=dma((n_off,)),
        s_r=dma((n_off,)),
        z_s=dma((n_off,)),
        z_r=dma((n_off, 2)),
        gx_r=dma((n_cut, max(nx - 1, 1))),
        h_s=dma((2,)),
        h_r=dma((2,)),
    )
    names = (*args, "out", *scratch)
    merged_map = pl.pallas_call(
        functools.partial(kernel, dims, names),
        out_shape=jax.ShapeDtypeStruct((mb, rows, cols, dec), BF16),
        in_specs=[pl.BlockSpec(memory_space=pltpu.HBM)] * len(args),
        out_specs=pl.BlockSpec(memory_space=pltpu.VMEM),
        scratch_shapes=list(scratch.values()),
        compiler_params=pltpu.CompilerParams(
            collective_id=0, has_side_effects=True, vmem_limit_bytes=48 * 1024 * 1024
        ),
    )(*[pltpu.with_memory_space_constraint(a, pltpu.HBM) for a in args.values()])
    return jnp.maximum(merged_map, jnp.zeros_like(merged_map))


def solution(mesh):
    in_specs = (
        P("grp", "band", None, "sect"),
        P("grp", "band", None, None),
        P("grp", "band"),
        P("sect", None),
        P(None, None, None, "sect", None),
        P(),
        P("sect", None),
        P(),
        P(),
        P(),
        P(),
        P(),
        P(),
        P(),
    )
    out_specs = P("grp", "band", None, None)
    return jax.shard_map(shards, mesh=mesh, in_specs=in_specs, out_specs=out_specs, check_vma=False)
```

```python
import functools
import types

import jax
import jax.numpy as jnp
from jax import lax
from jax.experimental import pallas as pl
from jax.experimental.pallas import tpu as pltpu
from jax.sharding import PartitionSpec as P

DILATIONS = (12, 24, 36)
LAND_BLOCK = 6
LAND_MOST = 4
MESH = pl.DeviceIdType.MESH
F32 = jnp.float32
BF16 = jnp.bfloat16
ORDER = (0, 3, 2, 1)


def offsets(rows, bands):
    off = []
    for k in (1, 2, 3):
        d = DILATIONS[k - 1]
        assert d % rows == 0
        hop = d // rows
        if hop < bands:
            off.append((k, 0, hop))
            off.append((k, 2, hop))
    return off


def pieces(live):
    inner = live - 2
    cuts = [(0, 2)]
    if inner > 1:
        cuts += [(2, inner - inner // 2), (live - inner // 2, inner // 2)]
    elif inner:
        cuts.append((2, inner))
    return cuts


def kernel(dims, names, *refs):
    r = types.SimpleNamespace(**dict(zip(names, refs, strict=True)))
    mb, rows, cols, ch, br_w, live, nb, ns, low_w, lowp = dims
    nx = ns // 2
    cs = cols // nx
    off = offsets(rows, nb)
    n_off = len(off)
    cuts = pieces(live)
    n_cut = len(cuts)
    need = [(k, 1) for k in ORDER if k] + [(k, i) for k, i, _ in off]
    pad = (r.m_l.shape[1] - cols) // 2
    scope = jax.named_scope

    band = lax.axis_index("band")
    sect = lax.axis_index("sect")
    core = lax.rem(sect, 2)
    xi = lax.div(sect, 2)
    mine, theirs = core, 1 - core
    peer = xi * 2 + 1 - core

    bar = pltpu.get_barrier_semaphore()
    up_ok = band >= 1
    dn_ok = band + 1 < nb

    def hello(b, s):
        pl.semaphore_signal(bar, inc=1, device_id={"band": b, "sect": s}, device_id_type=MESH)

    for e in range(1, ns):
        hello(band, lax.rem(sect + e, ns))
    for ok, step in ((up_ok, -1), (dn_ok, 1)):
        @pl.when(ok)
        def _(step=step):
            hello(band + step, sect)

    waits = {}

    def fetch(name, *copies, whole):
        sem = r.loc_sem.at[len(waits)]
        for src, dst in copies:
            pltpu.make_async_copy(src, dst, sem).start()
        waits[name] = pltpu.make_async_copy(whole, whole, sem)

    def need_now(*which):
        for name in which:
            waits[name].wait()

    def taps_of(k, i):
        return r.wd_h.at[k - 1, i], r.wd.at[need.index((k, i))]

    fetch("mask", (r.mask_h, r.mask), whole=r.mask)
    fetch("theirs", (r.feat_h.at[theirs], r.feat.at[0]), whole=r.feat.at[0])
    fetch("w1", (r.w1_h, r.w1), whole=r.w1)
    fetch("mine", (r.feat_h.at[mine], r.feat_own), whole=r.feat_own)
    if n_off:
        fetch("off", *[taps_of(*n) for n in need[3:]], whole=r.wd.at[pl.ds(3, n_off)])
    def pass_on(sem, step, ok):
        @pl.when(jnp.logical_and(jnp.logical_and(up_ok, dn_ok), ok))
        def _():
            pl.semaphore_signal(
                sem, inc=1, device_id={"band": band + step, "sect": sect}, device_id_type=MESH
            )

    def word_from(sem, ok):
        @pl.when(ok)
        def _():
            pl.semaphore_wait(sem, 1)

    def rcopy(src, dst, s, rs, **where):
        return pltpu.make_async_remote_copy(
            src_ref=src, dst_ref=dst, send_sem=s, recv_sem=rs, device_id=where, device_id_type=MESH
        )

    low_up = rcopy(
        r.low_h.at[mine, 0], r.low_halo.at[1], r.lo_s.at[0], r.lo_r.at[1], band=band - 1, sect=sect
    )
    low_dn = rcopy(
        r.low_h.at[mine, rows - 1], r.low_halo.at[0], r.lo_s.at[1], r.lo_r.at[0],
        band=band + 1, sect=sect,
    )

    def slots(m):
        on = [r.mask[m, y] for y in range(rows)]
        place_of = [0] + [None] * (rows - 2) + [1]
        row_of = [0, rows - 1] + [jnp.int32(0)] * (live - 2)
        hits = {}
        count = jnp.int32(0)
        for y in range(1, rows - 1):
            place_of[y] = jnp.where(on[y] > 0, jnp.minimum(count + 2, live - 1), 0)
            for p in range(2, live):
                hit = jnp.logical_and(on[y] > 0, count == p - 2)
                row_of[p] = jnp.where(hit, y, row_of[p])
                hits[p, y] = jnp.where(hit, 1, 0)
            count = count + on[y]
        return on, place_of, row_of, hits

    for ref in (r.m_l, r.m_r):
        zero = jnp.zeros((ref.shape[0], pad, br_w), F32)
        ref[:, :pad] = zero
        ref[:, pad + cols :] = zero
    for at in (0, rows + 1):
        r.joined[at] = jnp.zeros((cols, br_w), BF16)

    def taps(lhs, n, wref, d):
        mid = jnp.dot(lhs, wref[1], preferred_element_type=F32).reshape(n, cols, br_w)
        r.m_l[:n, pl.ds(pad, cols)] = jnp.dot(
            lhs, wref[0], preferred_element_type=F32
        ).reshape(n, cols, br_w)
        r.m_r[:n, pl.ds(pad, cols)] = jnp.dot(
            lhs, wref[2], preferred_element_type=F32
        ).reshape(n, cols, br_w)
        return mid + r.m_l[:n, pl.ds(pad - d, cols)] + r.m_r[:n, pl.ds(pad + d, cols)]

    def core_copy(t):
        if t < 4:
            src, dst = r.part_own.at[t, 0], r.crecv_own.at[t]
        else:
            src, dst = r.part_off.at[t - 4, 0], r.crecv_off.at[t - 4]
        return rcopy(src, dst, r.c_s.at[max(t - 3, 0)], r.c_r.at[t], sect=peer)

    def run_of(t, g):
        return cuts[g]

    def x_copy(t, g, e, incoming=False):
        lo, n = run_of(t, g)
        at = g * 2 + t // 3 if t < 4 else (t - 2) * n_cut + g
        send, recv, u = (
            (r.xsend_own, r.xrecv_own, t) if t < 4 else (r.xsend_off, r.xrecv_off, t - 4)
        )
        other = lax.rem(xi + e, nx)
        slot = other if incoming else xi
        return rcopy(
            send.at[u, other, pl.ds(lo, n)], recv.at[u, slot, pl.ds(lo, n)],
            r.x_s.at[max(t - 3, 0)], r.x_r.at[at, (e if incoming else nx - e) - 1],
            sect=other * 2 + core,
        )

    def x_arrived(g):
        for e in range(1, nx):
            whole = r.xrecv_own.at[pl.ds(0, 3), lax.rem(xi + e, nx), pl.ds(*cuts[g])]
            arrived(whole, r.x_r.at[g * 2, e - 1])

    def send_x(t, g):
        for e in range(1, nx):
            x_copy(t, g, e).start()

    def first(t, step):
        image = r.feat.at[0] if step == 0 else r.feat_own
        if t < 4:
            k = ORDER[t]
            row_of = facts[step][2]
            lhs = jnp.concatenate([image[row_of[p]] for p in range(live)], axis=0)
            if k:
                val = taps(lhs, live, r.wd.at[need.index((k, 1))], DILATIONS[k - 1])
            else:
                val = jnp.dot(lhs, r.w1[...], preferred_element_type=F32).reshape(live, cols, br_w)
            r.part_own[t, step] = val.astype(BF16)
        else:
            k, i, _ = off[t - 4]
            lhs = image[...].reshape(rows * cols, ch)
            val = taps(lhs, rows, r.wd.at[need.index((k, i))], DILATIONS[k - 1])
            r.part_off[t - 4, step] = val.astype(BF16)

    def second(t):
        core_copy(t).wait_recv()
        for c in range(nx):
            cell = pl.ds(c * cs, cs)
            total = r.part_own[t, 1, :, cell].astype(F32) + r.crecv_own[t, :, cell].astype(F32)
            r.xsend_own[t, c] = total.astype(BF16)

            @pl.when(xi == c)
            def _(total=total):
                r.keep_own[t] = total

    def second_off(t, h):
        u = t - 4
        if h == 0:
            core_copy(t).wait_recv()
        elif h == 1:
            sel_copy(t).wait_recv()
        lo, n = cuts[h]
        for c in range(nx):
            cell = pl.ds(c * cs, cs)

            def row(y, cell=cell):
                return r.part_off[u, 1, y, cell].astype(F32) + r.crecv_off[u, y, cell].astype(F32)

            if h == 0:
                picked = [row(0), row(rows - 1)]
            else:
                inner = [row(y) for y in range(1, rows - 1)]
                picked = []
                for p in range(lo, lo + n):
                    total = jnp.zeros((cs, br_w), F32)
                    for y in range(1, rows - 1):
                        at = (p - 2) * (rows - 2) + y - 1
                        total = total + inner[y - 1] * r.sel_in[u, at : at + 1]
                    picked.append(total)
            for p, total in enumerate(picked):
                r.xsend_off[u, c, lo + p] = total.astype(BF16)

            @pl.when(xi == c)
            def _(picked=picked):
                for p, total in enumerate(picked):
                    r.keep_off[u, lo + p] = total

    def sends_to(t):
        k, i, hop = off[t - 4]
        return band + hop < nb if i == 0 else band - hop >= 0

    def gets_from(t):
        k, i, hop = off[t - 4]
        return band - hop >= 0 if i == 0 else band + hop < nb

    def sel_copy(t):
        k, i, hop = off[t - 4]
        return rcopy(
            r.sel_out, r.sel_in.at[t - 4], r.s_s.at[t - 4], r.s_r.at[t - 4],
            band=band - hop if i == 0 else band + hop, sect=sect,
        )

    def z_copy(t, h):
        k, i, hop = off[t - 4]
        run = pl.ds(*cuts[h])
        return rcopy(
            r.zsend.at[t - 4, run], r.zrecv.at[t - 4, run], r.z_s.at[t - 4], r.z_r.at[t - 4, h],
            band=band + hop if i == 0 else band - hop, sect=sect,
        )

    def forward_off(t, h):
        run = pl.ds(*cuts[h])
        total = r.keep_off[t - 4, run]
        for e in range(1, nx):
            x_copy(t, h, e, True).wait_recv()
            total = total + r.xrecv_off[t - 4, lax.rem(xi + e, nx), run].astype(F32)
        r.zsend[t - 4, run] = total.astype(BF16)
        z_copy(t, h).start()

    def for_off(fn, *rest):
        for t in range(4, 4 + n_off):
            @pl.when(sends_to(t))
            def _(t=t):
                fn(t, *rest)

    def pool_sect(e, incoming=False):
        other = lax.rem(sect + e, ns)
        slot = other if incoming else sect
        return rcopy(
            r.pool_s.at[sect], r.pool_s.at[slot], r.one_s.at[0], r.one_r.at[0], sect=other
        )

    def pool_band(e, incoming=False):
        other = lax.rem(band + e, nb)
        slot = other if incoming else band
        return rcopy(
            r.pool_b.at[band], r.pool_b.at[slot], r.one_s.at[1], r.one_r.at[1], band=other
        )

    def dot_f32(v, w):
        n = v.shape[0]
        high = v.astype(BF16).astype(F32)
        middle = (v - high).astype(BF16).astype(F32)
        terms = jnp.concatenate([high, middle, v - high - middle], axis=0).astype(BF16)
        p = jnp.dot(terms, w, preferred_element_type=F32)
        return p[:n] + p[n : 2 * n] + p[2 * n :]

    def all_of(ref, n):
        return ref.at[pl.ds(0, n)]

    def arrived(whole, sem):
        pltpu.make_async_copy(whole, whole, sem).wait()

    def pool():
        need_now("wpool")
        ones = jnp.ones((8, rows * cols), BF16)
        at = lax.broadcasted_iota(jnp.int32, (8, ch), 0)
        sums = jnp.zeros((8, ch), F32)
        for m, image in ((mine, r.feat_own), (theirs, r.feat.at[0])):
            part = jnp.dot(
                ones, image[...].reshape(rows * cols, ch), preferred_element_type=F32
            )
            sums = jnp.where(at == m, part, sums)
        r.pool_s[sect] = dot_f32(sums, r.wpool[...])[:mb]
        for e in range(1, ns):
            pool_sect(e).start()

    need_now("mask")
    facts = [slots(theirs), slots(mine)]
    on, place_of, row_of, hits = facts[1]

    for p in range(2, live):
        for y in range(1, rows - 1):
            at = (p - 2) * (rows - 2) + y - 1
            r.sel_out[at : at + 1] = jnp.full((1, br_w), hits[p, y].astype(F32))

    def own_half(t, step):
        with scope(f"first{t}{'ab'[step]}"):
            first(t, step)
        if step == 0:
            core_copy(t).start()

    def off_theirs(t):
        first(t, 0)
        core_copy(t).start()

    def off_send(t, h):
        second_off(t, h)
        send_x(t, h)

    with scope("w0"):
        need_now("theirs", "w1")
    fetch("wpool", (r.wpool_h, r.wpool), whole=r.wpool)
    fetch("taps0", taps_of(*need[0]), whole=r.wd.at[0])
    fetch("taps1", *[taps_of(*n) for n in need[1:3]], whole=r.wd.at[pl.ds(1, 2)])
    fetch("low", (r.low_h.at[mine], r.low), whole=r.low)
    fetch("wr", (r.wr_h, r.wr), whole=r.wr)
    fetch("br", (r.br_h, r.br), whole=r.br)
    fetch("wml", (r.wm_h.at[:, :, pl.ds(br_w, lowp)], r.wml), whole=r.wml)
    fetch(
        "vec", (r.bm_h, r.vec.at[0]), (r.bpool_h, r.vec.at[1]), (r.bproj_h, r.vec.at[2]),
        whole=r.vec,
    )
    fetch("wproj", (r.wproj_h, r.wproj), whole=r.wproj)
    fetch("bbr", (r.bbr_h, r.bbr), whole=r.bbr)
    fetch(
        "wmp",
        *[
            (r.wm_h.at[i, j, pl.ds(0, br_w)], r.wmp.at[j, pl.ds(i * br_w, br_w)])
            for i in range(3) for j in range(3)
        ],
        whole=r.wmp,
    )
    with scope("first0a"):
        first(0, 0)
    with scope("bar"):
        sides = jnp.minimum(band, 1) + jnp.minimum(nb - 1 - band, 1)
        pl.semaphore_wait(bar, (ns - 1) + sides)
    core_copy(0).start()
    for e in range(1, nx):
        pl.semaphore_signal(
            r.across, inc=1, device_id={"sect": lax.rem(sect + 2 * e, ns)}, device_id_type=MESH
        )
    pass_on(r.above, 1, band < 2)
    pass_on(r.below, -1, band + 2 >= nb)

    def tell(i, ok):
        for t in range(4, 4 + n_off):
            if off[t - 4][1] == i:
                @pl.when(jnp.logical_and(gets_from(t), ok))
                def _(t=t):
                    sel_copy(t).start()

    @pl.when(up_ok)
    def _():
        low_up.start()

    @pl.when(dn_ok)
    def _():
        low_dn.start()

    need_now("mine")
    own_half(0, 1)
    if n_off:
        need_now("off")
    with scope("offa"):
        for_off(off_theirs)
    with scope("second0"):
        second(0)
    send_x(0, 0)
    with scope("p1"):
        word_from(r.above, band >= 2)
    pass_on(r.above, 1, band >= 2)
    tell(0, band >= 0)
    with scope("pool"):
        pool()
    with scope("p2"):
        word_from(r.below, jnp.logical_and(up_ok, band + 2 < nb))
    pass_on(r.below, -1, band + 2 < nb)
    tell(2, up_ok)
    with scope("offb"):
        for_off(first, 1)
    with scope("offs0"):
        for_off(off_send, 0)
    for g in range(1, n_cut):
        send_x(0, g)
    need_now("taps0", "taps1")
    own_half(1, 0)
    own_half(2, 0)
    with scope("p3"):
        word_from(r.below, jnp.logical_and(jnp.logical_not(up_ok), band + 2 < nb))
    tell(2, jnp.logical_not(up_ok))
    own_half(1, 1)
    with scope("second1"):
        second(1)
    for g in range(n_cut):
        send_x(1, g)
    own_half(3, 0)
    own_half(2, 1)
    with scope("poolb"):
        arrived(all_of(r.pool_s, ns - 1), r.one_r.at[0])
        total = r.pool_s[0]
        for s in range(1, ns):
            total = total + r.pool_s[s]
        r.pool_b[band] = total
    for e in range(1, nb):
        pool_band(e).start()
    with scope("second2"):
        second(2)
    own_half(3, 1)
    with scope("offs1"):
        for g in range(1, n_cut):
            for_off(off_send, g)
    send_x(2, 0)
    with scope("second3"):
        second(3)
    send_x(3, 0)
    for t in (2, 3):
        for g in range(1, n_cut):
            send_x(t, g)
    with scope("fwd0"):
        for_off(forward_off, 0)

    with scope("low"):
        need_now("low", "wr", "br", "wml", "vec")

        def reduced(v):
            return jax.nn.relu(
                lax.dot_general(
                    v, r.wr[...], (((1,), (1,)), ((), ())), preferred_element_type=F32
                )
                + r.br[...]
            ).astype(BF16)

        r.lowred[1 : rows + 1] = reduced(r.low[...].reshape(rows * cols, low_w)).reshape(
            rows, cols, lowp
        )
        for side, at, ok, copy in ((0, 0, up_ok, low_dn), (1, rows + 1, dn_ok, low_up)):
            @pl.when(ok)
            def _(side=side, at=at, copy=copy):
                copy.wait_recv()
                r.lowred[at] = reduced(r.low_halo[side])

            @pl.when(jnp.logical_not(ok))
            def _(at=at):
                r.lowred[at] = jnp.zeros((cols, lowp), BF16)

    def combine(mid, left, right, n):
        r.m_l[:n, pl.ds(pad, cols)] = left.reshape(n, cols, br_w)
        r.m_r[:n, pl.ds(pad, cols)] = right.reshape(n, cols, br_w)
        return (
            mid.reshape(n, cols, br_w)
            + r.m_l[:n, pl.ds(pad - 1, cols)]
            + r.m_r[:n, pl.ds(pad + 1, cols)]
        )

    with scope("lowconv"):
        terms = [None] * 3
        for i in range(3):
            lhs = jnp.concatenate([r.lowred[row_of[p] + i] for p in range(live)], axis=0)
            for j in range(3):
                term = jnp.dot(lhs, r.wml[i, j], preferred_element_type=F32)
                terms[j] = term if i == 0 else terms[j] + term
        r.lowacc[...] = combine(terms[1], terms[0], terms[2], live) + r.vec[0].reshape(1, 1, br_w)

    for g in range(1, n_cut):
        with scope(f"fwd{g}"):
            for_off(forward_off, g)

    need_now("wproj", "bbr")
    with scope("ctx"):
        if nb > 1:
            arrived(all_of(r.pool_b, nb - 1), r.one_r.at[1])
        total = r.pool_b[0]
        for b in range(1, nb):
            total = total + r.pool_b[b]
        pooled = jax.nn.relu(total / (nb * rows * cols) + r.vec[1])
        context = dot_f32(pooled, r.wproj[4 * br_w :])
        own = context[0:1]
        for m in range(1, mb):
            own = jnp.where(mine == m, context[m : m + 1], own)
        base = own + r.vec[2]

    def branch(t, g):
        lo, n = cuts[g]
        k = ORDER[t]
        with scope(f"x{t}{g}"):
            if t == 0:
                x_arrived(g)
            if t == 3:
                for e in range(1, nx):
                    x_copy(t, g, e, True).wait_recv()
        for u in range(4, 4 + n_off):
            if off[u - 4][0] == k:
                @pl.when(gets_from(u))
                def _(u=u):
                    with scope(f"z{g}"):
                        z_copy(u, g).wait_recv()
                    run = pl.ds(lo, n)
                    r.keep_own[t, run] = r.keep_own[t, run] + r.zrecv[u - 4, run].astype(F32)
        total = r.keep_own[t, lo : lo + n]
        for e in range(1, nx):
            total = total + r.xrecv_own[t, lax.rem(xi + e, nx), lo : lo + n].astype(F32)
        total = jax.nn.relu(total + r.bbr[k : k + 1].reshape(1, 1, br_w)).astype(BF16)
        return jnp.dot(
            total.reshape(n * cs, br_w), r.wproj[k * br_w : (k + 1) * br_w],
            preferred_element_type=F32,
        )

    def gather_x(g, e, incoming=False):
        run = pl.ds(*cuts[g])
        other = lax.rem(xi + e, nx)
        slot = other if incoming else xi
        return rcopy(
            r.gath.at[xi, run], r.gath.at[slot, run],
            r.one_s.at[2], r.gx_r.at[g, (e if incoming else nx - e) - 1], sect=other * 2 + core,
        )

    def early(g):
        lo, n = cuts[g]
        acc = branch(0, g)
        for t in (1, 2):
            acc = acc + branch(t, g)
        r.acc[lo : lo + n] = (acc + base).reshape(n, cs, br_w)

    def project(g):
        lo, n = cuts[g]
        last = branch(3, g).reshape(n, cs, br_w)
        done = jax.nn.relu(r.acc[lo : lo + n] + last)
        for p in range(n):
            v = done[p]
            if lo + p < 2:
                v = v * on[(0, rows - 1)[lo + p]].astype(F32)
            r.gath[xi, lo + p] = v.astype(BF16)
        if g == 0:
            if nx > 1:
                pl.semaphore_wait(r.across, nx - 1)
            for e in reversed(range(nx)):
                for side, ok in ((0, dn_ok), (1, up_ok)):
                    @pl.when(ok)
                    def _(side=side, e=e):
                        halo_copy(side, e).start()
        for e in range(1, nx):
            gather_x(g, e).start()

    def halo_copy(side, e):
        other = lax.rem(xi + e, nx)
        return rcopy(
            r.gath.at[xi, 1 - side], r.halo.at[side, xi], r.h_s.at[side], r.h_r.at[side],
            band=band + 1 if side == 0 else band - 1, sect=other * 2 + core,
        )

    early(0)
    project(0)
    for g in range(1, n_cut):
        early(g)
    for g in range(1, n_cut):
        project(g)
    with scope("ga"):
        for e in range(1, nx):
            gather_x(0, e, True).wait_recv()
    for c in range(nx):
        for p, y in ((0, 0), (1, rows - 1)):
            r.joined[y + 1, pl.ds(c * cs, cs)] = r.gath[c, p]
    need_now("wmp")
    def merge_terms(rows_in, first_tap, taps_in):
        lhs = jnp.concatenate(
            [jnp.concatenate([r.joined[y] for y in ys], axis=0) for ys in rows_in], axis=1
        )
        tap = pl.ds(first_tap * br_w, taps_in * br_w)
        return [jnp.dot(lhs, r.wmp[j, tap], preferred_element_type=F32) for j in range(3)]

    for side, at, ok in ((0, 0, up_ok), (1, rows + 1, dn_ok)):
        @pl.when(ok)
        def _(side=side, at=at):
            with scope("hw"):
                arrived(r.halo.at[side], r.h_r.at[side])
            for c in range(nx):
                r.joined[at, pl.ds(c * cs, cs)] = r.halo[side, c]

    with scope("edge"):
        upper = merge_terms([[0], [1]], 0, 2)
        lower = merge_terms([[rows], [rows + 1]], 1, 2)
        left, mid, right = [jnp.concatenate(p, axis=0) for p in zip(upper, lower)]
        r.lowacc[:2] = r.lowacc[:2] + combine(mid, left, right, 2)
    with scope("gb"):
        for g in range(1, n_cut):
            for e in range(1, nx):
                gather_x(g, e, True).wait_recv()
    with scope("join"):
        for y in range(1, rows - 1):
            for c in range(nx):
                r.joined[y + 1, pl.ds(c * cs, cs)] = (
                    r.gath[c, place_of[y]].astype(F32) * on[y].astype(F32)
                ).astype(BF16)

    def merged_copy(h):
        run = pl.ds(*halves[h])
        return rcopy(
            r.merged.at[run], r.merged_in.at[run], r.one_s.at[3], r.one_r.at[2], sect=peer
        )

    halves = [(2, live - 2), (0, 2)] if live > 2 else [(0, 2)]
    for h, (lo, n) in enumerate(halves):
        with scope(f"merge{h}"):
            if lo:
                terms = merge_terms(
                    [[row_of[p] + i for p in range(lo, lo + n)] for i in range(3)], 0, 3
                )
            else:
                terms = [
                    jnp.concatenate(p, axis=0)
                    for p in zip(merge_terms([[2]], 2, 1), merge_terms([[rows - 1]], 0, 1))
                ]
            left, mid, right = terms
            total = combine(mid, left, right, n) + r.lowacc[lo : lo + n]
            r.merged[lo : lo + n] = jax.nn.relu(total).astype(BF16)
        merged_copy(h).start()

    def spread(image, src, flags, places):
        for y in range(rows):
            r.out[image, y] = (src[places[y]].astype(F32) * flags[y].astype(F32)).astype(BF16)

    with scope("spread"):
        spread(mine, r.merged, on, place_of)
    with scope("ow"):
        arrived(r.merged, r.one_r.at[2])
    with scope("spread2"):
        spread(theirs, r.merged_in, facts[0][0], facts[0][1])

    @pl.when(up_ok)
    def _():
        low_up.wait_send()

    @pl.when(dn_ok)
    def _():
        low_dn.wait_send()

    def off_sent(t):
        u = t - 4
        core_copy(t).wait_send()
        if nx > 1:
            arrived(all_of(r.xsend_off.at[u], nx - 1), r.x_s.at[1 + u])
        arrived(r.zsend.at[u], r.z_s.at[u])

    for t in range(4, 4 + n_off):
        @pl.when(gets_from(t))
        def _(t=t):
            sel_copy(t).wait_send()
    for_off(off_sent)
    arrived(r.part_own.at[:, 0], r.c_s.at[0])
    if nx > 1:
        arrived(r.xsend_own.at[:, pl.ds(0, nx - 1)], r.x_s.at[0])
        arrived(all_of(r.gath, nx - 1), r.one_s.at[2])
    arrived(all_of(r.pool_s, ns - 1), r.one_s.at[0])
    if nb > 1:
        arrived(all_of(r.pool_b, nb - 1), r.one_s.at[1])
    for side, ok in ((0, dn_ok), (1, up_ok)):
        @pl.when(ok)
        def _(side=side):
            arrived(r.halo.at[side], r.h_s.at[side])
    arrived(r.merged, r.one_s.at[3])


def shards(
    features, low_level, land_mask, weight_one, weight_dilated, bias_branch, weight_pool,
    bias_pool, weight_project, bias_project, weight_reduce, bias_reduce, weight_merging,
    bias_merging,
):
    mb, rows, cols, ch = features.shape
    br_w = weight_project.shape[1]
    dec = weight_merging.shape[3]
    low_w, lowp = weight_reduce.shape
    nb, ns = lax.axis_size("band"), lax.axis_size("sect")
    nx = ns // 2
    cs = cols // nx
    assert mb == 2 and ns % 2 == 0 and rows > 2
    live = rows // LAND_BLOCK * LAND_MOST if rows % LAND_BLOCK == 0 else rows
    off = offsets(rows, nb)
    n_off = max(len(off), 1)
    assert dec == br_w
    n_cut = len(pieces(live))
    n_sel = -(-(live - 2) * (rows - 2) // 8) * 8
    pad = -(-max(DILATIONS) // 8) * 8
    vm, dma = pltpu.VMEM, pltpu.SemaphoreType.DMA
    dims = (mb, rows, cols, ch, br_w, live, nb, ns, low_w, lowp)
    args = dict(
        mask_h=land_mask, feat_h=features, low_h=low_level, w1_h=weight_one, wd_h=weight_dilated,
        bbr_h=bias_branch, wpool_h=weight_pool, bpool_h=bias_pool.reshape(1, -1),
        wproj_h=weight_project, bproj_h=bias_project.reshape(1, -1), wr_h=weight_reduce.T,
        br_h=bias_reduce.reshape(1, -1), wm_h=weight_merging, bm_h=bias_merging.reshape(1, -1),
    )
    scratch = dict(
        mask=pltpu.SMEM(land_mask.shape, jnp.int32),
        feat=vm((1, rows, cols, ch), BF16),
        feat_own=vm((rows, cols, ch), BF16),
        low=vm((rows, cols, low_w), BF16),
        low_halo=vm((2, cols, low_w), BF16),
        w1=vm(weight_one.shape, BF16),
        wpool=vm(weight_pool.shape, BF16),
        sel_out=vm((n_sel, br_w), F32),
        sel_in=vm((n_off, n_sel, br_w), F32),
        wd=vm((3 + len(off), 3, ch, br_w), BF16),
        wproj=vm(weight_project.shape, BF16),
        wmp=vm((3, 3 * br_w, dec), BF16),
        wml=vm((3, 3, lowp, dec), BF16),
        wr=vm((lowp, low_w), BF16),
        br=vm((1, lowp), F32),
        vec=vm((3, 1, br_w), F32),
        bbr=vm(bias_branch.shape, F32),
        m_l=vm((rows, cols + 2 * pad, br_w), F32),
        m_r=vm((rows, cols + 2 * pad, br_w), F32),
        part_off=vm((n_off, 2, rows, cols, br_w), BF16),
        crecv_off=vm((n_off, rows, cols, br_w), BF16),
        xsend_off=vm((n_off, nx, live, cs, br_w), BF16),
        xrecv_off=vm((n_off, nx, live, cs, br_w), BF16),
        zsend=vm((n_off, live, cs, br_w), BF16),
        zrecv=vm((n_off, live, cs, br_w), BF16),
        keep_off=vm((n_off, live, cs, br_w), F32),
        part_own=vm((4, 2, live, cols, br_w), BF16),
        crecv_own=vm((4, live, cols, br_w), BF16),
        xsend_own=vm((4, nx, live, cs, br_w), BF16),
        xrecv_own=vm((4, nx, live, cs, br_w), BF16),
        keep_own=vm((4, live, cs, br_w), F32),
        acc=vm((live, cs, br_w), F32),
        pool_s=vm((ns, mb, br_w), F32),
        pool_b=vm((nb, mb, br_w), F32),
        gath=vm((nx, live, cs, br_w), BF16),
        halo=vm((2, nx, cs, br_w), BF16),
        joined=vm((rows + 2, cols, br_w), BF16),
        lowred=vm((rows + 2, cols, lowp), BF16),
        lowacc=vm((live, cols, dec), F32),
        merged=vm((live, cols, dec), BF16),
        merged_in=vm((live, cols, dec), BF16),
        across=pltpu.SemaphoreType.REGULAR,
        above=pltpu.SemaphoreType.REGULAR,
        below=pltpu.SemaphoreType.REGULAR,
        loc_sem=dma((16,)),
        one_s=dma((4,)),
        one_r=dma((3,)),
        lo_s=dma((2,)),
        lo_r=dma((2,)),
        c_s=dma((1 + n_off,)),
        c_r=dma((4 + n_off,)),
        x_s=dma((1 + n_off,)),
        x_r=dma(((2 + n_off) * n_cut, max(nx - 1, 1))),
        s_s=dma((n_off,)),
        s_r=dma((n_off,)),
        z_s=dma((n_off,)),
        z_r=dma((n_off, n_cut)),
        gx_r=dma((n_cut, max(nx - 1, 1))),
        h_s=dma((2,)),
        h_r=dma((2,)),
    )
    names = (*args, "out", *scratch)
    merged_map = pl.pallas_call(
        functools.partial(kernel, dims, names),
        out_shape=jax.ShapeDtypeStruct((mb, rows, cols, dec), BF16),
        in_specs=[pl.BlockSpec(memory_space=pltpu.HBM)] * len(args),
        out_specs=pl.BlockSpec(memory_space=pltpu.VMEM),
        scratch_shapes=list(scratch.values()),
        compiler_params=pltpu.CompilerParams(
            collective_id=0, has_side_effects=True, vmem_limit_bytes=48 * 1024 * 1024
        ),
    )(*[pltpu.with_memory_space_constraint(a, pltpu.HBM) for a in args.values()])
    return jnp.maximum(merged_map, jnp.zeros_like(merged_map))


def solution(mesh):
    in_specs = (
        P("grp", "band", None, "sect"),
        P("grp", "band", None, None),
        P("grp", "band"),
        P("sect", None),
        P(None, None, None, "sect", None),
        P(),
        P("sect", None),
        P(),
        P(),
        P(),
        P(),
        P(),
        P(),
        P(),
    )
    out_specs = P("grp", "band", None, None)
    return jax.shard_map(shards, mesh=mesh, in_specs=in_specs, out_specs=out_specs, check_vma=False)
```

```python
import functools
import types

import jax
import jax.numpy as jnp
from jax import lax
from jax.experimental import pallas as pl
from jax.experimental.pallas import tpu as pltpu
from jax.sharding import PartitionSpec as P

DILATIONS = (12, 24, 36)
LAND_BLOCK = 6
LAND_MOST = 4
MESH = pl.DeviceIdType.MESH
F32 = jnp.float32
BF16 = jnp.bfloat16
ORDER = (0, 3, 2, 1)


def offsets(rows, bands):
    off = []
    for k in (1, 2, 3):
        d = DILATIONS[k - 1]
        assert d % rows == 0
        hop = d // rows
        if hop < bands:
            off.append((k, 0, hop))
            off.append((k, 2, hop))
    return off


def off_slots(off, bands):
    slots = []
    for n, (k, i, hop) in enumerate(off):
        shared = n and off[n - 1][0] == k and 2 * hop >= bands
        slots.append(slots[-1] if shared else (slots[-1] + 1 if slots else 0))
    return slots


def pieces(live):
    inner = live - 2
    cuts = [(0, 2)]
    if inner > 1:
        cuts += [(2, inner - inner // 2), (live - inner // 2, inner // 2)]
    elif inner:
        cuts.append((2, inner))
    return cuts


def kernel(dims, names, *refs):
    r = types.SimpleNamespace(**dict(zip(names, refs, strict=True)))
    mb, rows, cols, ch, br_w, live, nb, ns, low_w, lowp = dims
    nx = ns // 2
    cs = cols // nx
    off = offsets(rows, nb)
    n_off = len(off)
    cuts = pieces(live)
    n_cut = len(cuts)
    slot_of = off_slots(off, nb)
    need = [(k, 1) for k in ORDER if k] + [(k, i) for k, i, _ in off]
    pad = (r.m_l.shape[1] - cols) // 2
    scope = jax.named_scope

    band = lax.axis_index("band")
    sect = lax.axis_index("sect")
    core = lax.rem(sect, 2)
    xi = lax.div(sect, 2)
    mine, theirs = core, 1 - core
    peer = xi * 2 + 1 - core

    bar = pltpu.get_barrier_semaphore()
    up_ok = band >= 1
    dn_ok = band + 1 < nb

    def hello(b, s):
        pl.semaphore_signal(bar, inc=1, device_id={"band": b, "sect": s}, device_id_type=MESH)

    for e in range(1, ns):
        hello(band, lax.rem(sect + e, ns))
    for ok, step in ((up_ok, -1), (dn_ok, 1)):
        @pl.when(ok)
        def _(step=step):
            hello(band + step, sect)

    waits = {}

    def fetch(name, *copies, whole):
        sem = r.loc_sem.at[len(waits)]
        for src, dst in copies:
            pltpu.make_async_copy(src, dst, sem).start()
        waits[name] = pltpu.make_async_copy(whole, whole, sem)

    def need_now(*which):
        for name in which:
            waits[name].wait()

    def taps_of(k, i):
        return r.wd_h.at[k - 1, i], r.wd.at[need.index((k, i))]

    fetch("mask", (r.mask_h, r.mask), whole=r.mask)
    fetch("theirs", (r.feat_h.at[theirs], r.feat.at[0]), whole=r.feat.at[0])
    fetch("w1", (r.w1_h, r.w1), whole=r.w1)
    fetch("mine", (r.feat_h.at[mine], r.feat_own), whole=r.feat_own)
    if n_off:
        fetch("off", *[taps_of(*n) for n in need[3:]], whole=r.wd.at[pl.ds(3, n_off)])
    def pass_on(sem, step, ok):
        @pl.when(jnp.logical_and(jnp.logical_and(up_ok, dn_ok), ok))
        def _():
            pl.semaphore_signal(
                sem, inc=1, device_id={"band": band + step, "sect": sect}, device_id_type=MESH
            )

    def word_from(sem, ok):
        @pl.when(ok)
        def _():
            pl.semaphore_wait(sem, 1)

    def rcopy(src, dst, s, rs, **where):
        return pltpu.make_async_remote_copy(
            src_ref=src, dst_ref=dst, send_sem=s, recv_sem=rs, device_id=where, device_id_type=MESH
        )

    low_up = rcopy(
        r.low_h.at[mine, 0], r.low_halo.at[1], r.lo_s.at[0], r.lo_r.at[1], band=band - 1, sect=sect
    )
    low_dn = rcopy(
        r.low_h.at[mine, rows - 1], r.low_halo.at[0], r.lo_s.at[1], r.lo_r.at[0],
        band=band + 1, sect=sect,
    )

    def slots(m):
        on = [r.mask[m, y] for y in range(rows)]
        place_of = [0] + [None] * (rows - 2) + [1]
        row_of = [0, rows - 1] + [jnp.int32(0)] * (live - 2)
        hits = {}
        count = jnp.int32(0)
        for y in range(1, rows - 1):
            place_of[y] = jnp.where(on[y] > 0, jnp.minimum(count + 2, live - 1), 0)
            for p in range(2, live):
                hit = jnp.logical_and(on[y] > 0, count == p - 2)
                row_of[p] = jnp.where(hit, y, row_of[p])
                hits[p, y] = jnp.where(hit, 1, 0)
            count = count + on[y]
        return on, place_of, row_of, hits

    for ref in (r.m_l, r.m_r):
        zero = jnp.zeros((ref.shape[0], pad, br_w), F32)
        ref[:, :pad] = zero
        ref[:, pad + cols :] = zero
    for at in (0, rows + 1):
        r.joined[at] = jnp.zeros((cols, br_w), BF16)

    def taps(lhs, n, wref, d):
        mid = jnp.dot(lhs, wref[1], preferred_element_type=F32).reshape(n, cols, br_w)
        r.m_l[:n, pl.ds(pad, cols)] = jnp.dot(
            lhs, wref[0], preferred_element_type=F32
        ).reshape(n, cols, br_w)
        r.m_r[:n, pl.ds(pad, cols)] = jnp.dot(
            lhs, wref[2], preferred_element_type=F32
        ).reshape(n, cols, br_w)
        return mid + r.m_l[:n, pl.ds(pad - d, cols)] + r.m_r[:n, pl.ds(pad + d, cols)]

    def core_copy(t):
        if t < 4:
            src, dst = r.part_own.at[t, 0], r.crecv_own.at[t]
        else:
            src, dst = r.part_off.at[slot_of[t - 4], 0], r.crecv_off.at[slot_of[t - 4]]
        return rcopy(src, dst, r.c_s.at[0 if t < 4 else 1 + slot_of[t - 4]], r.c_r.at[t if t < 4 else 4 + slot_of[t - 4]], sect=peer)

    def run_of(t, g):
        return cuts[g]

    def x_copy(t, g, e, incoming=False):
        lo, n = run_of(t, g)
        at = g * 2 + t // 3 if t < 4 else (2 + slot_of[t - 4]) * n_cut + g
        send, recv, u = (
            (r.xsend_own, r.xrecv_own, t) if t < 4 else (r.xsend_off, r.xrecv_off, slot_of[t - 4])
        )
        other = lax.rem(xi + e, nx)
        slot = other if incoming else xi
        return rcopy(
            send.at[u, other, pl.ds(lo, n)], recv.at[u, slot, pl.ds(lo, n)],
            r.x_s.at[0 if t < 4 else 1 + slot_of[t - 4]], r.x_r.at[at, (e if incoming else nx - e) - 1],
            sect=other * 2 + core,
        )

    def x_arrived(g):
        for e in range(1, nx):
            whole = r.xrecv_own.at[pl.ds(0, 3), lax.rem(xi + e, nx), pl.ds(*cuts[g])]
            arrived(whole, r.x_r.at[g * 2, e - 1])

    def send_x(t, g):
        for e in range(1, nx):
            x_copy(t, g, e).start()

    def first(t, step):
        image = r.feat.at[0] if step == 0 else r.feat_own
        if t < 4:
            k = ORDER[t]
            row_of = facts[step][2]
            lhs = jnp.concatenate([image[row_of[p]] for p in range(live)], axis=0)
            if k:
                val = taps(lhs, live, r.wd.at[need.index((k, 1))], DILATIONS[k - 1])
            else:
                val = jnp.dot(lhs, r.w1[...], preferred_element_type=F32).reshape(live, cols, br_w)
            r.part_own[t, step] = val.astype(BF16)
        else:
            k, i, _ = off[t - 4]
            lhs = image[...].reshape(rows * cols, ch)
            val = taps(lhs, rows, r.wd.at[need.index((k, i))], DILATIONS[k - 1])
            r.part_off[slot_of[t - 4], step] = val.astype(BF16)

    def second(t):
        core_copy(t).wait_recv()
        for c in range(nx):
            cell = pl.ds(c * cs, cs)
            total = r.part_own[t, 1, :, cell].astype(F32) + r.crecv_own[t, :, cell].astype(F32)
            r.xsend_own[t, c] = total.astype(BF16)

            @pl.when(xi == c)
            def _(total=total):
                r.keep_own[t] = total

    def second_off(t, h):
        u = slot_of[t - 4]
        if h == 0:
            core_copy(t).wait_recv()
        elif h == 1:
            sel_copy(t).wait_recv()
        lo, n = cuts[h]
        for c in range(nx):
            cell = pl.ds(c * cs, cs)

            def row(y, cell=cell):
                return r.part_off[u, 1, y, cell].astype(F32) + r.crecv_off[u, y, cell].astype(F32)

            if h == 0:
                picked = [row(0), row(rows - 1)]
            else:
                inner = [row(y) for y in range(1, rows - 1)]
                picked = []
                for p in range(lo, lo + n):
                    total = jnp.zeros((cs, br_w), F32)
                    for y in range(1, rows - 1):
                        at = (p - 2) * (rows - 2) + y - 1
                        total = total + inner[y - 1] * r.sel_in[u, at : at + 1]
                    picked.append(total)
            for p, total in enumerate(picked):
                r.xsend_off[u, c, lo + p] = total.astype(BF16)

            @pl.when(xi == c)
            def _(picked=picked):
                for p, total in enumerate(picked):
                    r.keep_off[u, lo + p] = total

    def sends_to(t):
        k, i, hop = off[t - 4]
        return band + hop < nb if i == 0 else band - hop >= 0

    def gets_from(t):
        k, i, hop = off[t - 4]
        return band - hop >= 0 if i == 0 else band + hop < nb

    def sel_copy(t):
        k, i, hop = off[t - 4]
        return rcopy(
            r.sel_out, r.sel_in.at[slot_of[t - 4]], r.s_s.at[slot_of[t - 4]], r.s_r.at[slot_of[t - 4]],
            band=band - hop if i == 0 else band + hop, sect=sect,
        )

    def z_copy(t, h):
        k, i, hop = off[t - 4]
        run = pl.ds(*cuts[h])
        return rcopy(
            r.zsend.at[slot_of[t - 4], run], r.zrecv.at[slot_of[t - 4], run], r.z_s.at[slot_of[t - 4]], r.z_r.at[slot_of[t - 4], h],
            band=band + hop if i == 0 else band - hop, sect=sect,
        )

    def forward_off(t, h):
        run = pl.ds(*cuts[h])
        total = r.keep_off[slot_of[t - 4], run]
        for e in range(1, nx):
            x_copy(t, h, e, True).wait_recv()
            total = total + r.xrecv_off[slot_of[t - 4], lax.rem(xi + e, nx), run].astype(F32)
        r.zsend[slot_of[t - 4], run] = total.astype(BF16)
        z_copy(t, h).start()

    def for_off(fn, *rest):
        for t in range(4, 4 + n_off):
            @pl.when(sends_to(t))
            def _(t=t):
                fn(t, *rest)

    def pool_sect(e, incoming=False):
        other = lax.rem(sect + e, ns)
        slot = other if incoming else sect
        return rcopy(
            r.pool_s.at[sect], r.pool_s.at[slot], r.one_s.at[0], r.one_r.at[0], sect=other
        )

    def pool_band(e, incoming=False):
        other = lax.rem(band + e, nb)
        slot = other if incoming else band
        return rcopy(
            r.pool_b.at[band], r.pool_b.at[slot], r.one_s.at[1], r.one_r.at[1], band=other
        )

    def dot_f32(v, w):
        n = v.shape[0]
        high = v.astype(BF16).astype(F32)
        middle = (v - high).astype(BF16).astype(F32)
        terms = jnp.concatenate([high, middle, v - high - middle], axis=0).astype(BF16)
        p = jnp.dot(terms, w, preferred_element_type=F32)
        return p[:n] + p[n : 2 * n] + p[2 * n :]

    def all_of(ref, n):
        return ref.at[pl.ds(0, n)]

    def arrived(whole, sem):
        pltpu.make_async_copy(whole, whole, sem).wait()

    def pool():
        need_now("wpool")
        ones = jnp.ones((8, rows * cols), BF16)
        at = lax.broadcasted_iota(jnp.int32, (8, ch), 0)
        sums = jnp.zeros((8, ch), F32)
        for m, image in ((mine, r.feat_own), (theirs, r.feat.at[0])):
            part = jnp.dot(
                ones, image[...].reshape(rows * cols, ch), preferred_element_type=F32
            )
            sums = jnp.where(at == m, part, sums)
        r.pool_s[sect] = dot_f32(sums, r.wpool[...])[:mb]
        for e in range(1, ns):
            pool_sect(e).start()

    need_now("mask")
    facts = [slots(theirs), slots(mine)]
    on, place_of, row_of, hits = facts[1]

    for p in range(2, live):
        for y in range(1, rows - 1):
            at = (p - 2) * (rows - 2) + y - 1
            r.sel_out[at : at + 1] = jnp.full((1, br_w), hits[p, y].astype(F32))

    def own_half(t, step):
        with scope(f"first{t}{'ab'[step]}"):
            first(t, step)
        if step == 0:
            core_copy(t).start()

    def off_theirs(t):
        first(t, 0)
        core_copy(t).start()

    def off_send(t, h):
        second_off(t, h)
        send_x(t, h)

    with scope("w0"):
        need_now("theirs", "w1")
    fetch("wpool", (r.wpool_h, r.wpool), whole=r.wpool)
    fetch("taps0", taps_of(*need[0]), whole=r.wd.at[0])
    fetch("taps1", *[taps_of(*n) for n in need[1:3]], whole=r.wd.at[pl.ds(1, 2)])
    fetch("low", (r.low_h.at[mine], r.low), whole=r.low)
    fetch("wr", (r.wr_h, r.wr), whole=r.wr)
    fetch("br", (r.br_h, r.br), whole=r.br)
    fetch("wml", (r.wm_h.at[:, :, pl.ds(br_w, lowp)], r.wml), whole=r.wml)
    fetch(
        "vec", (r.bm_h, r.vec.at[0]), (r.bpool_h, r.vec.at[1]), (r.bproj_h, r.vec.at[2]),
        whole=r.vec,
    )
    fetch("wproj", (r.wproj_h, r.wproj), whole=r.wproj)
    fetch("bbr", (r.bbr_h, r.bbr), whole=r.bbr)
    fetch(
        "wmp",
        *[
            (r.wm_h.at[i, j, pl.ds(0, br_w)], r.wmp.at[j, pl.ds(i * br_w, br_w)])
            for i in range(3) for j in range(3)
        ],
        whole=r.wmp,
    )
    with scope("first0a"):
        first(0, 0)
    with scope("bar"):
        sides = jnp.minimum(band, 1) + jnp.minimum(nb - 1 - band, 1)
        pl.semaphore_wait(bar, (ns - 1) + sides)
    core_copy(0).start()
    for e in range(1, nx):
        pl.semaphore_signal(
            r.across, inc=1, device_id={"sect": lax.rem(sect + 2 * e, ns)}, device_id_type=MESH
        )
    pass_on(r.above, 1, band < 2)
    pass_on(r.below, -1, band + 2 >= nb)

    def tell(i, ok):
        for t in range(4, 4 + n_off):
            if off[t - 4][1] == i:
                @pl.when(jnp.logical_and(gets_from(t), ok))
                def _(t=t):
                    sel_copy(t).start()

    @pl.when(up_ok)
    def _():
        low_up.start()

    @pl.when(dn_ok)
    def _():
        low_dn.start()

    need_now("mine")
    own_half(0, 1)
    if n_off:
        need_now("off")
    with scope("offa"):
        for_off(off_theirs)
    with scope("second0"):
        second(0)
    send_x(0, 0)
    with scope("p1"):
        word_from(r.above, band >= 2)
    pass_on(r.above, 1, band >= 2)
    tell(0, band >= 0)
    with scope("pool"):
        pool()
    with scope("p2"):
        word_from(r.below, jnp.logical_and(up_ok, band + 2 < nb))
    pass_on(r.below, -1, band + 2 < nb)
    tell(2, up_ok)
    with scope("offb"):
        for_off(first, 1)
    with scope("offs0"):
        for_off(off_send, 0)
    for g in range(1, n_cut):
        send_x(0, g)
    need_now("taps0", "taps1")
    own_half(1, 0)
    own_half(2, 0)
    with scope("p3"):
        word_from(r.below, jnp.logical_and(jnp.logical_not(up_ok), band + 2 < nb))
    tell(2, jnp.logical_not(up_ok))
    own_half(1, 1)
    with scope("second1"):
        second(1)
    for g in range(n_cut):
        send_x(1, g)
    own_half(3, 0)
    own_half(2, 1)
    with scope("poolb"):
        arrived(all_of(r.pool_s, ns - 1), r.one_r.at[0])
        total = r.pool_s[0]
        for s in range(1, ns):
            total = total + r.pool_s[s]
        r.pool_b[band] = total
    for e in range(1, nb):
        pool_band(e).start()
    with scope("second2"):
        second(2)
    own_half(3, 1)
    with scope("offs1"):
        for g in range(1, n_cut):
            for_off(off_send, g)
    send_x(2, 0)
    with scope("second3"):
        second(3)
    send_x(3, 0)
    for t in (2, 3):
        for g in range(1, n_cut):
            send_x(t, g)
    with scope("fwd0"):
        for_off(forward_off, 0)

    with scope("low"):
        need_now("low", "wr", "br", "wml", "vec")

        def reduced(v):
            return jax.nn.relu(
                lax.dot_general(
                    v, r.wr[...], (((1,), (1,)), ((), ())), preferred_element_type=F32
                )
                + r.br[...]
            ).astype(BF16)

        r.lowred[1 : rows + 1] = reduced(r.low[...].reshape(rows * cols, low_w)).reshape(
            rows, cols, lowp
        )
        for side, at, ok, copy in ((0, 0, up_ok, low_dn), (1, rows + 1, dn_ok, low_up)):
            @pl.when(ok)
            def _(side=side, at=at, copy=copy):
                copy.wait_recv()
                r.lowred[at] = reduced(r.low_halo[side])

            @pl.when(jnp.logical_not(ok))
            def _(at=at):
                r.lowred[at] = jnp.zeros((cols, lowp), BF16)

    def combine(mid, left, right, n):
        r.m_l[:n, pl.ds(pad, cols)] = left.reshape(n, cols, br_w)
        r.m_r[:n, pl.ds(pad, cols)] = right.reshape(n, cols, br_w)
        return (
            mid.reshape(n, cols, br_w)
            + r.m_l[:n, pl.ds(pad - 1, cols)]
            + r.m_r[:n, pl.ds(pad + 1, cols)]
        )

    with scope("lowconv"):
        terms = [None] * 3
        for i in range(3):
            lhs = jnp.concatenate([r.lowred[row_of[p] + i] for p in range(live)], axis=0)
            for j in range(3):
                term = jnp.dot(lhs, r.wml[i, j], preferred_element_type=F32)
                terms[j] = term if i == 0 else terms[j] + term
        r.lowacc[...] = combine(terms[1], terms[0], terms[2], live) + r.vec[0].reshape(1, 1, br_w)

    for g in range(1, n_cut):
        with scope(f"fwd{g}"):
            for_off(forward_off, g)

    need_now("wproj", "bbr")
    with scope("ctx"):
        if nb > 1:
            arrived(all_of(r.pool_b, nb - 1), r.one_r.at[1])
        total = r.pool_b[0]
        for b in range(1, nb):
            total = total + r.pool_b[b]
        pooled = jax.nn.relu(total / (nb * rows * cols) + r.vec[1])
        context = dot_f32(pooled, r.wproj[4 * br_w :])
        own = context[0:1]
        for m in range(1, mb):
            own = jnp.where(mine == m, context[m : m + 1], own)
        base = own + r.vec[2]

    def branch(t, g):
        lo, n = cuts[g]
        k = ORDER[t]
        with scope(f"x{t}{g}"):
            if t == 0:
                x_arrived(g)
            if t == 3:
                for e in range(1, nx):
                    x_copy(t, g, e, True).wait_recv()
        for u in range(4, 4 + n_off):
            if off[u - 4][0] == k:
                @pl.when(gets_from(u))
                def _(u=u):
                    with scope(f"z{g}"):
                        z_copy(u, g).wait_recv()
                    run = pl.ds(lo, n)
                    r.keep_own[t, run] = r.keep_own[t, run] + r.zrecv[slot_of[u - 4], run].astype(F32)
        total = r.keep_own[t, lo : lo + n]
        for e in range(1, nx):
            total = total + r.xrecv_own[t, lax.rem(xi + e, nx), lo : lo + n].astype(F32)
        total = jax.nn.relu(total + r.bbr[k : k + 1].reshape(1, 1, br_w)).astype(BF16)
        return jnp.dot(
            total.reshape(n * cs, br_w), r.wproj[k * br_w : (k + 1) * br_w],
            preferred_element_type=F32,
        )

    def gather_x(g, e, incoming=False):
        run = pl.ds(*cuts[g])
        other = lax.rem(xi + e, nx)
        slot = other if incoming else xi
        return rcopy(
            r.gath.at[xi, run], r.gath.at[slot, run],
            r.one_s.at[2], r.gx_r.at[g, (e if incoming else nx - e) - 1], sect=other * 2 + core,
        )

    def early(g):
        lo, n = cuts[g]
        acc = branch(0, g)
        for t in (1, 2):
            acc = acc + branch(t, g)
        r.acc[lo : lo + n] = (acc + base).reshape(n, cs, br_w)

    def project(g):
        lo, n = cuts[g]
        last = branch(3, g).reshape(n, cs, br_w)
        done = jax.nn.relu(r.acc[lo : lo + n] + last)
        for p in range(n):
            v = done[p]
            if lo + p < 2:
                v = v * on[(0, rows - 1)[lo + p]].astype(F32)
            r.gath[xi, lo + p] = v.astype(BF16)
        if g == 0:
            if nx > 1:
                pl.semaphore_wait(r.across, nx - 1)
            for e in reversed(range(nx)):
                for side, ok in ((0, dn_ok), (1, up_ok)):
                    @pl.when(ok)
                    def _(side=side, e=e):
                        halo_copy(side, e).start()
        for e in range(1, nx):
            gather_x(g, e).start()

    def halo_copy(side, e):
        other = lax.rem(xi + e, nx)
        return rcopy(
            r.gath.at[xi, 1 - side], r.halo.at[side, xi], r.h_s.at[side], r.h_r.at[side],
            band=band + 1 if side == 0 else band - 1, sect=other * 2 + core,
        )

    early(0)
    project(0)
    for g in range(1, n_cut):
        early(g)
    for g in range(1, n_cut):
        project(g)
    with scope("ga"):
        for e in range(1, nx):
            gather_x(0, e, True).wait_recv()
    for c in range(nx):
        for p, y in ((0, 0), (1, rows - 1)):
            r.joined[y + 1, pl.ds(c * cs, cs)] = r.gath[c, p]
    need_now("wmp")
    def merge_terms(rows_in, first_tap, taps_in):
        lhs = jnp.concatenate(
            [jnp.concatenate([r.joined[y] for y in ys], axis=0) for ys in rows_in], axis=1
        )
        tap = pl.ds(first_tap * br_w, taps_in * br_w)
        return [jnp.dot(lhs, r.wmp[j, tap], preferred_element_type=F32) for j in range(3)]

    for side, at, ok in ((0, 0, up_ok), (1, rows + 1, dn_ok)):
        @pl.when(ok)
        def _(side=side, at=at):
            with scope("hw"):
                arrived(r.halo.at[side], r.h_r.at[side])
            for c in range(nx):
                r.joined[at, pl.ds(c * cs, cs)] = r.halo[side, c]

    with scope("edge"):
        upper = merge_terms([[0], [1]], 0, 2)
        lower = merge_terms([[rows], [rows + 1]], 1, 2)
        left, mid, right = [jnp.concatenate(p, axis=0) for p in zip(upper, lower)]
        r.lowacc[:2] = r.lowacc[:2] + combine(mid, left, right, 2)
    def merged_copy(lo, n):
        run = pl.ds(lo, n)
        return rcopy(
            r.merged.at[run], r.merged_in.at[run], r.one_s.at[3], r.one_r.at[2], sect=peer
        )

    def finish(lo, n, terms):
        left, mid, right = terms
        total = combine(mid, left, right, n) + r.lowacc[lo : lo + n]
        r.merged[lo : lo + n] = jax.nn.relu(total).astype(BF16)
        merged_copy(lo, n).start()

    def gathered(g):
        with scope(f"gb{g}"):
            for e in range(1, nx):
                gather_x(g, e, True).wait_recv()

    def join(y, c, p):
        r.joined[y + 1, pl.ds(c * cs, cs)] = (
            r.gath[c, p].astype(F32) * on[y].astype(F32)
        ).astype(BF16)

    if n_cut > 1:
        gathered(1)
    for c in range(nx):
        join(1, c, min(2, live - 1))
    with scope("merge0"):
        finish(0, 1, merge_terms([[2]], 2, 1))
    for g in range(2, n_cut):
        gathered(g)
    with scope("join"):
        for y in range(2, rows - 1):
            for c in range(nx):
                join(y, c, place_of[y])
    if live > 2:
        with scope("merge1"):
            inner = range(2, live)
            finish(
                2, live - 2, merge_terms([[row_of[p] + i for p in inner] for i in range(3)], 0, 3)
            )
    with scope("merge2"):
        finish(1, 1, merge_terms([[rows - 1]], 0, 1))

    def spread(image, src, flags, places):
        for y in range(rows):
            r.out[image, y] = (src[places[y]].astype(F32) * flags[y].astype(F32)).astype(BF16)

    with scope("spread"):
        spread(mine, r.merged, on, place_of)
    with scope("ow"):
        arrived(r.merged, r.one_r.at[2])
    with scope("spread2"):
        spread(theirs, r.merged_in, facts[0][0], facts[0][1])

    @pl.when(up_ok)
    def _():
        low_up.wait_send()

    @pl.when(dn_ok)
    def _():
        low_dn.wait_send()

    def off_sent(t):
        u = slot_of[t - 4]
        core_copy(t).wait_send()
        if nx > 1:
            arrived(all_of(r.xsend_off.at[u], nx - 1), r.x_s.at[1 + u])
        arrived(r.zsend.at[u], r.z_s.at[u])

    for t in range(4, 4 + n_off):
        @pl.when(gets_from(t))
        def _(t=t):
            sel_copy(t).wait_send()
    for_off(off_sent)
    arrived(r.part_own.at[:, 0], r.c_s.at[0])
    if nx > 1:
        arrived(r.xsend_own.at[:, pl.ds(0, nx - 1)], r.x_s.at[0])
        arrived(all_of(r.gath, nx - 1), r.one_s.at[2])
    arrived(all_of(r.pool_s, ns - 1), r.one_s.at[0])
    if nb > 1:
        arrived(all_of(r.pool_b, nb - 1), r.one_s.at[1])
    for side, ok in ((0, dn_ok), (1, up_ok)):
        @pl.when(ok)
        def _(side=side):
            arrived(r.halo.at[side], r.h_s.at[side])
    arrived(r.merged, r.one_s.at[3])


def shards(
    features, low_level, land_mask, weight_one, weight_dilated, bias_branch, weight_pool,
    bias_pool, weight_project, bias_project, weight_reduce, bias_reduce, weight_merging,
    bias_merging,
):
    mb, rows, cols, ch = features.shape
    br_w = weight_project.shape[1]
    dec = weight_merging.shape[3]
    low_w, lowp = weight_reduce.shape
    nb, ns = lax.axis_size("band"), lax.axis_size("sect")
    nx = ns // 2
    cs = cols // nx
    assert mb == 2 and ns % 2 == 0 and rows > 2
    live = rows // LAND_BLOCK * LAND_MOST if rows % LAND_BLOCK == 0 else rows
    off = offsets(rows, nb)
    n_off = max(off_slots(off, nb), default=0) + 1
    assert dec == br_w
    n_cut = len(pieces(live))
    n_sel = -(-(live - 2) * (rows - 2) // 8) * 8
    pad = -(-max(DILATIONS) // 8) * 8
    vm, dma = pltpu.VMEM, pltpu.SemaphoreType.DMA
    dims = (mb, rows, cols, ch, br_w, live, nb, ns, low_w, lowp)
    args = dict(
        mask_h=land_mask, feat_h=features, low_h=low_level, w1_h=weight_one, wd_h=weight_dilated,
        bbr_h=bias_branch, wpool_h=weight_pool, bpool_h=bias_pool.reshape(1, -1),
        wproj_h=weight_project, bproj_h=bias_project.reshape(1, -1), wr_h=weight_reduce.T,
        br_h=bias_reduce.reshape(1, -1), wm_h=weight_merging, bm_h=bias_merging.reshape(1, -1),
    )
    scratch = dict(
        mask=pltpu.SMEM(land_mask.shape, jnp.int32),
        feat=vm((1, rows, cols, ch), BF16),
        feat_own=vm((rows, cols, ch), BF16),
        low=vm((rows, cols, low_w), BF16),
        low_halo=vm((2, cols, low_w), BF16),
        w1=vm(weight_one.shape, BF16),
        wpool=vm(weight_pool.shape, BF16),
        sel_out=vm((n_sel, br_w), F32),
        sel_in=vm((n_off, n_sel, br_w), F32),
        wd=vm((3 + len(off), 3, ch, br_w), BF16),
        wproj=vm(weight_project.shape, BF16),
        wmp=vm((3, 3 * br_w, dec), BF16),
        wml=vm((3, 3, lowp, dec), BF16),
        wr=vm((lowp, low_w), BF16),
        br=vm((1, lowp), F32),
        vec=vm((3, 1, br_w), F32),
        bbr=vm(bias_branch.shape, F32),
        m_l=vm((rows, cols + 2 * pad, br_w), F32),
        m_r=vm((rows, cols + 2 * pad, br_w), F32),
        part_off=vm((n_off, 2, rows, cols, br_w), BF16),
        crecv_off=vm((n_off, rows, cols, br_w), BF16),
        xsend_off=vm((n_off, nx, live, cs, br_w), BF16),
        xrecv_off=vm((n_off, nx, live, cs, br_w), BF16),
        zsend=vm((n_off, live, cs, br_w), BF16),
        zrecv=vm((n_off, live, cs, br_w), BF16),
        keep_off=vm((n_off, live, cs, br_w), F32),
        part_own=vm((4, 2, live, cols, br_w), BF16),
        crecv_own=vm((4, live, cols, br_w), BF16),
        xsend_own=vm((4, nx, live, cs, br_w), BF16),
        xrecv_own=vm((4, nx, live, cs, br_w), BF16),
        keep_own=vm((4, live, cs, br_w), F32),
        acc=vm((live, cs, br_w), F32),
        pool_s=vm((ns, mb, br_w), F32),
        pool_b=vm((nb, mb, br_w), F32),
        gath=vm((nx, live, cs, br_w), BF16),
        halo=vm((2, nx, cs, br_w), BF16),
        joined=vm((rows + 2, cols, br_w), BF16),
        lowred=vm((rows + 2, cols, lowp), BF16),
        lowacc=vm((live, cols, dec), F32),
        merged=vm((live, cols, dec), BF16),
        merged_in=vm((live, cols, dec), BF16),
        across=pltpu.SemaphoreType.REGULAR,
        above=pltpu.SemaphoreType.REGULAR,
        below=pltpu.SemaphoreType.REGULAR,
        loc_sem=dma((16,)),
        one_s=dma((4,)),
        one_r=dma((3,)),
        lo_s=dma((2,)),
        lo_r=dma((2,)),
        c_s=dma((1 + n_off,)),
        c_r=dma((4 + n_off,)),
        x_s=dma((1 + n_off,)),
        x_r=dma(((2 + n_off) * n_cut, max(nx - 1, 1))),
        s_s=dma((n_off,)),
        s_r=dma((n_off,)),
        z_s=dma((n_off,)),
        z_r=dma((n_off, n_cut)),
        gx_r=dma((n_cut, max(nx - 1, 1))),
        h_s=dma((2,)),
        h_r=dma((2,)),
    )
    names = (*args, "out", *scratch)
    merged_map = pl.pallas_call(
        functools.partial(kernel, dims, names),
        out_shape=jax.ShapeDtypeStruct((mb, rows, cols, dec), BF16),
        in_specs=[pl.BlockSpec(memory_space=pltpu.HBM)] * len(args),
        out_specs=pl.BlockSpec(memory_space=pltpu.VMEM),
        scratch_shapes=list(scratch.values()),
        compiler_params=pltpu.CompilerParams(
            collective_id=0, has_side_effects=True, vmem_limit_bytes=48 * 1024 * 1024
        ),
    )(*[pltpu.with_memory_space_constraint(a, pltpu.HBM) for a in args.values()])
    return jnp.maximum(merged_map, jnp.zeros_like(merged_map))


def solution(mesh):
    in_specs = (
        P("grp", "band", None, "sect"),
        P("grp", "band", None, None),
        P("grp", "band"),
        P("sect", None),
        P(None, None, None, "sect", None),
        P(),
        P("sect", None),
        P(),
        P(),
        P(),
        P(),
        P(),
        P(),
        P(),
    )
    out_specs = P("grp", "band", None, None)
    return jax.shard_map(shards, mesh=mesh, in_specs=in_specs, out_specs=out_specs, check_vma=False)
```

```python
import functools
import types

import jax
import jax.numpy as jnp
from jax import lax
from jax.experimental import pallas as pl
from jax.experimental.pallas import tpu as pltpu
from jax.sharding import PartitionSpec as P

DILATIONS = (12, 24, 36)
LAND_BLOCK = 6
LAND_MOST = 4
MESH = pl.DeviceIdType.MESH
F32 = jnp.float32
BF16 = jnp.bfloat16
ORDER = (0, 3, 2, 1)


def offsets(rows, bands):
    off = []
    for k in (1, 2, 3):
        d = DILATIONS[k - 1]
        assert d % rows == 0
        hop = d // rows
        if hop < bands:
            off.append((k, 0, hop))
            off.append((k, 2, hop))
    return off


def off_slots(off, bands):
    slots = []
    for n, (k, i, hop) in enumerate(off):
        shared = n and off[n - 1][0] == k and 2 * hop >= bands
        slots.append(slots[-1] if shared else (slots[-1] + 1 if slots else 0))
    return slots


def pieces(live):
    inner = live - 2
    cuts = [(0, 2)]
    if inner > 1:
        cuts += [(2, inner - inner // 2), (live - inner // 2, inner // 2)]
    elif inner:
        cuts.append((2, inner))
    return cuts


def kernel(dims, names, *refs):
    r = types.SimpleNamespace(**dict(zip(names, refs, strict=True)))
    mb, rows, cols, ch, br_w, live, nb, ns, low_w, lowp = dims
    nx = ns // 2
    cs = cols // nx
    off = offsets(rows, nb)
    n_off = len(off)
    cuts = pieces(live)
    n_cut = len(cuts)
    slot_of = off_slots(off, nb)
    need = [(k, 1) for k in ORDER if k] + [(k, i) for k, i, _ in off]
    pad = (r.m_l.shape[1] - cols) // 2
    scope = jax.named_scope

    band = lax.axis_index("band")
    sect = lax.axis_index("sect")
    core = lax.rem(sect, 2)
    xi = lax.div(sect, 2)
    mine, theirs = core, 1 - core
    peer = xi * 2 + 1 - core

    bar = pltpu.get_barrier_semaphore()
    up_ok = band >= 1
    dn_ok = band + 1 < nb

    def hello(b, s):
        pl.semaphore_signal(bar, inc=1, device_id={"band": b, "sect": s}, device_id_type=MESH)

    for e in range(1, ns):
        hello(band, lax.rem(sect + e, ns))
    for ok, step in ((up_ok, -1), (dn_ok, 1)):
        @pl.when(ok)
        def _(step=step):
            hello(band + step, sect)

    waits = {}
    free = list(range(r.loc_sem.shape[0]))

    def fetch(name, *copies, whole):
        sem = r.loc_sem.at[free.pop(0)]
        for src, dst in copies:
            pltpu.make_async_copy(src, dst, sem).start()
        waits[name] = pltpu.make_async_copy(whole, whole, sem)

    def need_now(*which):
        for name in which:
            waits[name].wait()

    def taps_of(k, i):
        return r.wd_h.at[k - 1, i], r.wd.at[need.index((k, i))]

    fetch("mask", (r.mask_h, r.mask), whole=r.mask)
    fetch("theirs", (r.feat_h.at[theirs], r.feat.at[0]), whole=r.feat.at[0])
    fetch("w1", (r.w1_h, r.w1), whole=r.w1)
    fetch("mine", (r.feat_h.at[mine], r.feat_own), whole=r.feat_own)
    if n_off:
        fetch("off", *[taps_of(*n) for n in need[3:]], whole=r.wd.at[pl.ds(3, n_off)])
    def pass_on(sem, step, ok):
        @pl.when(jnp.logical_and(jnp.logical_and(up_ok, dn_ok), ok))
        def _():
            pl.semaphore_signal(
                sem, inc=1, device_id={"band": band + step, "sect": sect}, device_id_type=MESH
            )

    def word_from(sem, ok):
        @pl.when(ok)
        def _():
            pl.semaphore_wait(sem, 1)

    def rcopy(src, dst, s, rs, **where):
        return pltpu.make_async_remote_copy(
            src_ref=src, dst_ref=dst, send_sem=s, recv_sem=rs, device_id=where, device_id_type=MESH
        )

    low_up = rcopy(
        r.low_h.at[mine, 0], r.low_halo.at[1], r.lo_s.at[0], r.lo_r.at[1], band=band - 1, sect=sect
    )
    low_dn = rcopy(
        r.low_h.at[mine, rows - 1], r.low_halo.at[0], r.lo_s.at[1], r.lo_r.at[0],
        band=band + 1, sect=sect,
    )

    def slots(m):
        on = [r.mask[m, y] for y in range(rows)]
        place_of = [0] + [None] * (rows - 2) + [1]
        row_of = [0, rows - 1] + [jnp.int32(0)] * (live - 2)
        hits = {}
        count = jnp.int32(0)
        for y in range(1, rows - 1):
            place_of[y] = jnp.where(on[y] > 0, jnp.minimum(count + 2, live - 1), 0)
            for p in range(2, live):
                hit = jnp.logical_and(on[y] > 0, count == p - 2)
                row_of[p] = jnp.where(hit, y, row_of[p])
                hits[p, y] = jnp.where(hit, 1, 0)
            count = count + on[y]
        return on, place_of, row_of, hits

    for ref in (r.m_l, r.m_r):
        zero = jnp.zeros((ref.shape[0], pad, br_w), F32)
        ref[:, :pad] = zero
        ref[:, pad + cols :] = zero
    for at in (0, rows + 1):
        r.joined[at] = jnp.zeros((cols, br_w), BF16)

    def taps(lhs, n, wref, d):
        mid = jnp.dot(lhs, wref[1], preferred_element_type=F32).reshape(n, cols, br_w)
        r.m_l[:n, pl.ds(pad, cols)] = jnp.dot(
            lhs, wref[0], preferred_element_type=F32
        ).reshape(n, cols, br_w)
        r.m_r[:n, pl.ds(pad, cols)] = jnp.dot(
            lhs, wref[2], preferred_element_type=F32
        ).reshape(n, cols, br_w)
        return mid + r.m_l[:n, pl.ds(pad - d, cols)] + r.m_r[:n, pl.ds(pad + d, cols)]

    def core_copy(t):
        if t < 4:
            src, dst = r.part_own.at[t, 0], r.crecv_own.at[t]
        else:
            src, dst = r.part_off.at[slot_of[t - 4], 0], r.crecv_off.at[slot_of[t - 4]]
        return rcopy(src, dst, r.c_s.at[0 if t < 4 else 1 + slot_of[t - 4]], r.c_r.at[t if t < 4 else 4 + slot_of[t - 4]], sect=peer)

    def run_of(t, g):
        return cuts[g]

    def x_copy(t, g, e, incoming=False):
        lo, n = run_of(t, g)
        at = g * 2 + t // 3 if t < 4 else (2 + slot_of[t - 4]) * n_cut + g
        send, recv, u = (
            (r.xsend_own, r.xrecv_own, t) if t < 4 else (r.xsend_off, r.xrecv_off, slot_of[t - 4])
        )
        other = lax.rem(xi + e, nx)
        slot = other if incoming else xi
        return rcopy(
            send.at[u, other, pl.ds(lo, n)], recv.at[u, slot, pl.ds(lo, n)],
            r.x_s.at[0 if t < 4 else 1 + slot_of[t - 4]], r.x_r.at[at, (e if incoming else nx - e) - 1],
            sect=other * 2 + core,
        )

    def x_arrived(g):
        for e in range(1, nx):
            whole = r.xrecv_own.at[pl.ds(0, 3), lax.rem(xi + e, nx), pl.ds(*cuts[g])]
            arrived(whole, r.x_r.at[g * 2, e - 1])

    def send_x(t, g):
        for e in range(1, nx):
            x_copy(t, g, e).start()

    def first(t, step):
        image = r.feat.at[0] if step == 0 else r.feat_own
        if t < 4:
            k = ORDER[t]
            row_of = facts[step][2]
            lhs = jnp.concatenate([image[row_of[p]] for p in range(live)], axis=0)
            if k:
                val = taps(lhs, live, r.wd.at[need.index((k, 1))], DILATIONS[k - 1])
            else:
                val = jnp.dot(lhs, r.w1[...], preferred_element_type=F32).reshape(live, cols, br_w)
            r.part_own[t, step] = val.astype(BF16)
        else:
            k, i, _ = off[t - 4]
            lhs = image[...].reshape(rows * cols, ch)
            val = taps(lhs, rows, r.wd.at[need.index((k, i))], DILATIONS[k - 1])
            r.part_off[slot_of[t - 4], step] = val.astype(BF16)

    def second(t):
        core_copy(t).wait_recv()
        for c in range(nx):
            cell = pl.ds(c * cs, cs)
            total = r.part_own[t, 1, :, cell].astype(F32) + r.crecv_own[t, :, cell].astype(F32)
            r.xsend_own[t, c] = total.astype(BF16)

            @pl.when(xi == c)
            def _(total=total):
                r.keep_own[t] = total

    def second_off(t, h):
        u = slot_of[t - 4]
        if h == 0:
            core_copy(t).wait_recv()
        elif h == 1:
            sel_copy(t).wait_recv()
        lo, n = cuts[h]
        for c in range(nx):
            cell = pl.ds(c * cs, cs)

            def row(y, cell=cell):
                return r.part_off[u, 1, y, cell].astype(F32) + r.crecv_off[u, y, cell].astype(F32)

            if h == 0:
                picked = [row(0), row(rows - 1)]
            else:
                inner = [row(y) for y in range(1, rows - 1)]
                picked = []
                for p in range(lo, lo + n):
                    total = jnp.zeros((cs, br_w), F32)
                    for y in range(1, rows - 1):
                        at = (p - 2) * (rows - 2) + y - 1
                        total = total + inner[y - 1] * r.sel_in[u, at : at + 1]
                    picked.append(total)
            for p, total in enumerate(picked):
                r.xsend_off[u, c, lo + p] = total.astype(BF16)

            @pl.when(xi == c)
            def _(picked=picked):
                for p, total in enumerate(picked):
                    r.keep_off[u, lo + p] = total

    def sends_to(t):
        k, i, hop = off[t - 4]
        return band + hop < nb if i == 0 else band - hop >= 0

    def gets_from(t):
        k, i, hop = off[t - 4]
        return band - hop >= 0 if i == 0 else band + hop < nb

    def sel_copy(t):
        k, i, hop = off[t - 4]
        return rcopy(
            r.sel_out, r.sel_in.at[slot_of[t - 4]], r.s_s.at[slot_of[t - 4]], r.s_r.at[slot_of[t - 4]],
            band=band - hop if i == 0 else band + hop, sect=sect,
        )

    def z_copy(t, h):
        k, i, hop = off[t - 4]
        run = pl.ds(*cuts[h])
        return rcopy(
            r.zsend.at[slot_of[t - 4], run], r.zrecv.at[slot_of[t - 4], run], r.z_s.at[slot_of[t - 4]], r.z_r.at[slot_of[t - 4], h],
            band=band + hop if i == 0 else band - hop, sect=sect,
        )

    def forward_off(t, h):
        run = pl.ds(*cuts[h])
        total = r.keep_off[slot_of[t - 4], run]
        for e in range(1, nx):
            x_copy(t, h, e, True).wait_recv()
            total = total + r.xrecv_off[slot_of[t - 4], lax.rem(xi + e, nx), run].astype(F32)
        r.zsend[slot_of[t - 4], run] = total.astype(BF16)
        z_copy(t, h).start()

    def for_off(fn, *rest):
        for t in range(4, 4 + n_off):
            @pl.when(sends_to(t))
            def _(t=t):
                fn(t, *rest)

    def pool_sect(e, incoming=False):
        other = lax.rem(sect + e, ns)
        slot = other if incoming else sect
        return rcopy(
            r.pool_s.at[sect], r.pool_s.at[slot], r.one_s.at[0], r.one_r.at[0], sect=other
        )

    def pool_band(e, incoming=False):
        other = lax.rem(band + e, nb)
        slot = other if incoming else band
        return rcopy(
            r.pool_b.at[band], r.pool_b.at[slot], r.one_s.at[1], r.one_r.at[1], band=other
        )

    def dot_f32(v, w):
        n = v.shape[0]
        high = v.astype(BF16).astype(F32)
        middle = (v - high).astype(BF16).astype(F32)
        terms = jnp.concatenate([high, middle, v - high - middle], axis=0).astype(BF16)
        p = jnp.dot(terms, w, preferred_element_type=F32)
        return p[:n] + p[n : 2 * n] + p[2 * n :]

    def all_of(ref, n):
        return ref.at[pl.ds(0, n)]

    def arrived(whole, sem):
        pltpu.make_async_copy(whole, whole, sem).wait()

    def pool():
        need_now("wpool")
        ones = jnp.ones((8, rows * cols), BF16)
        at = lax.broadcasted_iota(jnp.int32, (8, ch), 0)
        sums = jnp.zeros((8, ch), F32)
        for m, image in ((mine, r.feat_own), (theirs, r.feat.at[0])):
            part = jnp.dot(
                ones, image[...].reshape(rows * cols, ch), preferred_element_type=F32
            )
            sums = jnp.where(at == m, part, sums)
        r.pool_s[sect] = dot_f32(sums, r.wpool[...])[:mb]
        for e in range(1, ns):
            pool_sect(e).start()

    need_now("mask")
    facts = [slots(theirs), slots(mine)]
    on, place_of, row_of, hits = facts[1]

    for p in range(2, live):
        for y in range(1, rows - 1):
            at = (p - 2) * (rows - 2) + y - 1
            r.sel_out[at : at + 1] = jnp.full((1, br_w), hits[p, y].astype(F32))

    def own_half(t, step):
        with scope(f"first{t}{'ab'[step]}"):
            first(t, step)
        if step == 0:
            core_copy(t).start()

    def off_theirs(t):
        first(t, 0)
        core_copy(t).start()

    def off_send(t, h):
        second_off(t, h)
        send_x(t, h)

    with scope("w0"):
        need_now("theirs", "w1")
    free[:0] = range(3)
    fetch("wpool", (r.wpool_h, r.wpool), whole=r.wpool)
    fetch("taps", *[taps_of(*n) for n in need[:3]], whole=r.wd.at[pl.ds(0, 3)])
    fetch("low", (r.low_h.at[mine], r.low), whole=r.low)
    fetch("wr", (r.wr_h, r.wr), whole=r.wr)
    fetch("br", (r.br_h, r.br), whole=r.br)
    fetch("wml", (r.wm_h.at[:, :, pl.ds(br_w, lowp)], r.wml), whole=r.wml)
    fetch(
        "vec", (r.bm_h, r.vec.at[0]), (r.bpool_h, r.vec.at[1]), (r.bproj_h, r.vec.at[2]),
        whole=r.vec,
    )
    fetch("wproj", (r.wproj_h, r.wproj), whole=r.wproj)
    fetch("bbr", (r.bbr_h, r.bbr), whole=r.bbr)
    fetch(
        "wmp",
        *[
            (r.wm_h.at[i, j, pl.ds(0, br_w)], r.wmp.at[j, pl.ds(i * br_w, br_w)])
            for i in range(3) for j in range(3)
        ],
        whole=r.wmp,
    )
    with scope("first0a"):
        first(0, 0)
    with scope("bar"):
        sides = jnp.minimum(band, 1) + jnp.minimum(nb - 1 - band, 1)
        pl.semaphore_wait(bar, (ns - 1) + sides)
    core_copy(0).start()
    for e in range(1, nx):
        pl.semaphore_signal(
            r.across, inc=1, device_id={"sect": lax.rem(sect + 2 * e, ns)}, device_id_type=MESH
        )
    pass_on(r.above, 1, band < 2)
    pass_on(r.below, -1, band + 2 >= nb)

    def tell(i, ok):
        for t in range(4, 4 + n_off):
            if off[t - 4][1] == i:
                @pl.when(jnp.logical_and(gets_from(t), ok))
                def _(t=t):
                    sel_copy(t).start()

    @pl.when(up_ok)
    def _():
        low_up.start()

    @pl.when(dn_ok)
    def _():
        low_dn.start()

    need_now("mine")
    own_half(0, 1)
    if n_off:
        need_now("off")
    with scope("offa"):
        for_off(off_theirs)
    with scope("second0"):
        second(0)
    send_x(0, 0)
    with scope("p1"):
        word_from(r.above, band >= 2)
    pass_on(r.above, 1, band >= 2)
    tell(0, band >= 0)
    with scope("pool"):
        pool()
    with scope("p2"):
        word_from(r.below, jnp.logical_and(up_ok, band + 2 < nb))
    pass_on(r.below, -1, band + 2 < nb)
    tell(2, up_ok)
    with scope("offb"):
        for_off(first, 1)
    with scope("offs0"):
        for_off(off_send, 0)
    for g in range(1, n_cut):
        send_x(0, g)
    need_now("taps")
    own_half(1, 0)
    own_half(2, 0)
    with scope("p3"):
        word_from(r.below, jnp.logical_and(jnp.logical_not(up_ok), band + 2 < nb))
    tell(2, jnp.logical_not(up_ok))
    own_half(1, 1)
    with scope("second1"):
        second(1)
    for g in range(n_cut):
        send_x(1, g)
    own_half(3, 0)
    own_half(2, 1)
    with scope("poolb"):
        arrived(all_of(r.pool_s, ns - 1), r.one_r.at[0])
        total = r.pool_s[0]
        for s in range(1, ns):
            total = total + r.pool_s[s]
        r.pool_b[band] = total
    for e in range(1, nb):
        pool_band(e).start()
    with scope("second2"):
        second(2)
    own_half(3, 1)
    with scope("offs1"):
        for g in range(1, n_cut):
            for_off(off_send, g)
    send_x(2, 0)
    with scope("second3"):
        second(3)
    send_x(3, 0)
    for t in (2, 3):
        for g in range(1, n_cut):
            send_x(t, g)
    with scope("fwd0"):
        for_off(forward_off, 0)

    with scope("low"):
        need_now("low", "wr", "br", "wml", "vec")

        def reduced(v):
            return jax.nn.relu(
                lax.dot_general(
                    v, r.wr[...], (((1,), (1,)), ((), ())), preferred_element_type=F32
                )
                + r.br[...]
            ).astype(BF16)

        r.lowred[1 : rows + 1] = reduced(r.low[...].reshape(rows * cols, low_w)).reshape(
            rows, cols, lowp
        )
        for side, at, ok, copy in ((0, 0, up_ok, low_dn), (1, rows + 1, dn_ok, low_up)):
            @pl.when(ok)
            def _(side=side, at=at, copy=copy):
                copy.wait_recv()
                r.lowred[at] = reduced(r.low_halo[side])

            @pl.when(jnp.logical_not(ok))
            def _(at=at):
                r.lowred[at] = jnp.zeros((cols, lowp), BF16)

    def combine(mid, left, right, n):
        r.m_l[:n, pl.ds(pad, cols)] = left.reshape(n, cols, br_w)
        r.m_r[:n, pl.ds(pad, cols)] = right.reshape(n, cols, br_w)
        return (
            mid.reshape(n, cols, br_w)
            + r.m_l[:n, pl.ds(pad - 1, cols)]
            + r.m_r[:n, pl.ds(pad + 1, cols)]
        )

    with scope("lowconv"):
        terms = [None] * 3
        for i in range(3):
            lhs = jnp.concatenate([r.lowred[row_of[p] + i] for p in range(live)], axis=0)
            for j in range(3):
                term = jnp.dot(lhs, r.wml[i, j], preferred_element_type=F32)
                terms[j] = term if i == 0 else terms[j] + term
        r.lowacc[...] = combine(terms[1], terms[0], terms[2], live) + r.vec[0].reshape(1, 1, br_w)

    for g in range(1, n_cut):
        with scope(f"fwd{g}"):
            for_off(forward_off, g)

    need_now("wproj", "bbr")
    with scope("ctx"):
        if nb > 1:
            arrived(all_of(r.pool_b, nb - 1), r.one_r.at[1])
        total = r.pool_b[0]
        for b in range(1, nb):
            total = total + r.pool_b[b]
        pooled = jax.nn.relu(total / (nb * rows * cols) + r.vec[1])
        context = dot_f32(pooled, r.wproj[4 * br_w :])
        own = context[0:1]
        for m in range(1, mb):
            own = jnp.where(mine == m, context[m : m + 1], own)
        base = own + r.vec[2]

    def branch(t, g):
        lo, n = cuts[g]
        k = ORDER[t]
        with scope(f"x{t}{g}"):
            if t == 0:
                x_arrived(g)
            if t == 3:
                for e in range(1, nx):
                    x_copy(t, g, e, True).wait_recv()
        for u in range(4, 4 + n_off):
            if off[u - 4][0] == k:
                @pl.when(gets_from(u))
                def _(u=u):
                    with scope(f"z{g}"):
                        z_copy(u, g).wait_recv()
                    run = pl.ds(lo, n)
                    r.keep_own[t, run] = r.keep_own[t, run] + r.zrecv[slot_of[u - 4], run].astype(F32)
        total = r.keep_own[t, lo : lo + n]
        for e in range(1, nx):
            total = total + r.xrecv_own[t, lax.rem(xi + e, nx), lo : lo + n].astype(F32)
        total = jax.nn.relu(total + r.bbr[k : k + 1].reshape(1, 1, br_w)).astype(BF16)
        return jnp.dot(
            total.reshape(n * cs, br_w), r.wproj[k * br_w : (k + 1) * br_w],
            preferred_element_type=F32,
        )

    def gather_x(g, e, incoming=False):
        run = pl.ds(*cuts[g])
        other = lax.rem(xi + e, nx)
        slot = other if incoming else xi
        return rcopy(
            r.gath.at[xi, run], r.gath.at[slot, run],
            r.x_s.at[0], r.gx_r.at[g, (e if incoming else nx - e) - 1], sect=other * 2 + core,
        )

    def early(g):
        lo, n = cuts[g]
        acc = branch(0, g)
        for t in (1, 2):
            acc = acc + branch(t, g)
        r.acc[lo : lo + n] = (acc + base).reshape(n, cs, br_w)

    def project(g):
        lo, n = cuts[g]
        last = branch(3, g).reshape(n, cs, br_w)
        done = jax.nn.relu(r.acc[lo : lo + n] + last)
        for p in range(n):
            v = done[p]
            if lo + p < 2:
                v = v * on[(0, rows - 1)[lo + p]].astype(F32)
            r.gath[xi, lo + p] = v.astype(BF16)
        if g == 0:
            if nx > 1:
                pl.semaphore_wait(r.across, nx - 1)
            for e in reversed(range(nx)):
                for side, ok in ((0, dn_ok), (1, up_ok)):
                    @pl.when(ok)
                    def _(side=side, e=e):
                        halo_copy(side, e).start()
        for e in range(1, nx):
            gather_x(g, e).start()

    def halo_copy(side, e):
        other = lax.rem(xi + e, nx)
        return rcopy(
            r.gath.at[xi, 1 - side], r.halo.at[side, xi], r.lo_s.at[1 - side], r.h_r.at[side],
            band=band + 1 if side == 0 else band - 1, sect=other * 2 + core,
        )

    @pl.when(up_ok)
    def _():
        low_up.wait_send()

    @pl.when(dn_ok)
    def _():
        low_dn.wait_send()

    early(0)
    project(0)
    for g in range(1, n_cut):
        early(g)
    for g in range(1, n_cut):
        project(g)
    with scope("ga"):
        for e in range(1, nx):
            gather_x(0, e, True).wait_recv()
    for c in range(nx):
        for p, y in ((0, 0), (1, rows - 1)):
            r.joined[y + 1, pl.ds(c * cs, cs)] = r.gath[c, p]
    need_now("wmp")
    def merge_terms(rows_in, first_tap, taps_in):
        lhs = jnp.concatenate(
            [jnp.concatenate([r.joined[y] for y in ys], axis=0) for ys in rows_in], axis=1
        )
        tap = pl.ds(first_tap * br_w, taps_in * br_w)
        return [jnp.dot(lhs, r.wmp[j, tap], preferred_element_type=F32) for j in range(3)]

    for side, at, ok in ((0, 0, up_ok), (1, rows + 1, dn_ok)):
        @pl.when(ok)
        def _(side=side, at=at):
            with scope("hw"):
                arrived(r.halo.at[side], r.h_r.at[side])
            for c in range(nx):
                r.joined[at, pl.ds(c * cs, cs)] = r.halo[side, c]

    with scope("edge"):
        upper = merge_terms([[0], [1]], 0, 2)
        lower = merge_terms([[rows], [rows + 1]], 1, 2)
        left, mid, right = [jnp.concatenate(p, axis=0) for p in zip(upper, lower)]
        r.lowacc[:2] = r.lowacc[:2] + combine(mid, left, right, 2)
    def merged_copy(lo, n):
        run = pl.ds(lo, n)
        return rcopy(
            r.merged.at[run], r.merged_in.at[run], r.c_s.at[0], r.c_r.at[0], sect=peer
        )

    def finish(lo, n, terms):
        left, mid, right = terms
        total = combine(mid, left, right, n) + r.lowacc[lo : lo + n]
        r.merged[lo : lo + n] = jax.nn.relu(total).astype(BF16)
        merged_copy(lo, n).start()

    def gathered(g):
        with scope(f"gb{g}"):
            for e in range(1, nx):
                gather_x(g, e, True).wait_recv()

    def join(y, c, p):
        r.joined[y + 1, pl.ds(c * cs, cs)] = (
            r.gath[c, p].astype(F32) * on[y].astype(F32)
        ).astype(BF16)

    if n_cut > 1:
        gathered(1)
    for c in range(nx):
        join(1, c, min(2, live - 1))
    with scope("merge0"):
        finish(0, 1, merge_terms([[2]], 2, 1))
    for g in range(2, n_cut):
        gathered(g)
    with scope("join"):
        for y in range(2, rows - 1):
            for c in range(nx):
                join(y, c, place_of[y])
    if live > 2:
        with scope("merge1"):
            inner = range(2, live)
            finish(
                2, live - 2, merge_terms([[row_of[p] + i for p in inner] for i in range(3)], 0, 3)
            )
    with scope("merge2"):
        finish(1, 1, merge_terms([[rows - 1]], 0, 1))

    def spread(image, src, flags, places):
        for y in range(rows):
            r.out[image, y] = (src[places[y]].astype(F32) * flags[y].astype(F32)).astype(BF16)

    with scope("spread"):
        spread(mine, r.merged, on, place_of)
    with scope("ow"):
        arrived(r.merged, r.c_r.at[0])
    with scope("spread2"):
        spread(theirs, r.merged_in, facts[0][0], facts[0][1])

    def off_sent(t):
        u = slot_of[t - 4]
        core_copy(t).wait_send()
        if nx > 1:
            arrived(all_of(r.xsend_off.at[u], nx - 1), r.x_s.at[1 + u])
        arrived(r.zsend.at[u], r.z_s.at[u])

    for t in range(4, 4 + n_off):
        @pl.when(gets_from(t))
        def _(t=t):
            sel_copy(t).wait_send()
    for_off(off_sent)
    arrived(r.part_own.at[:, 0], r.c_s.at[0])
    if nx > 1:
        arrived(r.xsend_own.at[:, pl.ds(0, nx - 1)], r.x_s.at[0])
    arrived(all_of(r.pool_s, ns - 1), r.one_s.at[0])
    if nb > 1:
        arrived(all_of(r.pool_b, nb - 1), r.one_s.at[1])
    for side, ok in ((0, dn_ok), (1, up_ok)):
        @pl.when(ok)
        def _(side=side):
            arrived(r.halo.at[side], r.lo_s.at[1 - side])


def shards(
    features, low_level, land_mask, weight_one, weight_dilated, bias_branch, weight_pool,
    bias_pool, weight_project, bias_project, weight_reduce, bias_reduce, weight_merging,
    bias_merging,
):
    mb, rows, cols, ch = features.shape
    br_w = weight_project.shape[1]
    dec = weight_merging.shape[3]
    low_w, lowp = weight_reduce.shape
    nb, ns = lax.axis_size("band"), lax.axis_size("sect")
    nx = ns // 2
    cs = cols // nx
    assert mb == 2 and ns % 2 == 0 and rows > 2
    live = rows // LAND_BLOCK * LAND_MOST if rows % LAND_BLOCK == 0 else rows
    off = offsets(rows, nb)
    n_off = max(off_slots(off, nb), default=0) + 1
    assert dec == br_w
    n_cut = len(pieces(live))
    n_sel = -(-(live - 2) * (rows - 2) // 8) * 8
    pad = -(-max(DILATIONS) // 8) * 8
    vm, dma = pltpu.VMEM, pltpu.SemaphoreType.DMA
    dims = (mb, rows, cols, ch, br_w, live, nb, ns, low_w, lowp)
    args = dict(
        mask_h=land_mask, feat_h=features, low_h=low_level, w1_h=weight_one, wd_h=weight_dilated,
        bbr_h=bias_branch, wpool_h=weight_pool, bpool_h=bias_pool.reshape(1, -1),
        wproj_h=weight_project, bproj_h=bias_project.reshape(1, -1), wr_h=weight_reduce.T,
        br_h=bias_reduce.reshape(1, -1), wm_h=weight_merging, bm_h=bias_merging.reshape(1, -1),
    )
    scratch = dict(
        mask=pltpu.SMEM(land_mask.shape, jnp.int32),
        feat=vm((1, rows, cols, ch), BF16),
        feat_own=vm((rows, cols, ch), BF16),
        low=vm((rows, cols, low_w), BF16),
        low_halo=vm((2, cols, low_w), BF16),
        w1=vm(weight_one.shape, BF16),
        wpool=vm(weight_pool.shape, BF16),
        sel_out=vm((n_sel, br_w), F32),
        sel_in=vm((n_off, n_sel, br_w), F32),
        wd=vm((3 + len(off), 3, ch, br_w), BF16),
        wproj=vm(weight_project.shape, BF16),
        wmp=vm((3, 3 * br_w, dec), BF16),
        wml=vm((3, 3, lowp, dec), BF16),
        wr=vm((lowp, low_w), BF16),
        br=vm((1, lowp), F32),
        vec=vm((3, 1, br_w), F32),
        bbr=vm(bias_branch.shape, F32),
        m_l=vm((rows, cols + 2 * pad, br_w), F32),
        m_r=vm((rows, cols + 2 * pad, br_w), F32),
        part_off=vm((n_off, 2, rows, cols, br_w), BF16),
        crecv_off=vm((n_off, rows, cols, br_w), BF16),
        xsend_off=vm((n_off, nx, live, cs, br_w), BF16),
        xrecv_off=vm((n_off, nx, live, cs, br_w), BF16),
        zsend=vm((n_off, live, cs, br_w), BF16),
        zrecv=vm((n_off, live, cs, br_w), BF16),
        keep_off=vm((n_off, live, cs, br_w), F32),
        part_own=vm((5, 2, live, cols, br_w), BF16),
        crecv_own=vm((4, live, cols, br_w), BF16),
        xsend_own=vm((5, nx, live, cs, br_w), BF16),
        xrecv_own=vm((4, nx, live, cs, br_w), BF16),
        keep_own=vm((4, live, cs, br_w), F32),
        acc=vm((live, cs, br_w), F32),
        pool_s=vm((ns, mb, br_w), F32),
        pool_b=vm((nb, mb, br_w), F32),
        gath=vm((nx, live, cs, br_w), BF16),
        halo=vm((2, nx, cs, br_w), BF16),
        joined=vm((rows + 2, cols, br_w), BF16),
        lowred=vm((rows + 2, cols, lowp), BF16),
        lowacc=vm((live, cols, dec), F32),
        merged=vm((live, cols, dec), BF16),
        merged_in=vm((live, cols, dec), BF16),
        across=pltpu.SemaphoreType.REGULAR,
        above=pltpu.SemaphoreType.REGULAR,
        below=pltpu.SemaphoreType.REGULAR,
        loc_sem=dma((12,)),
        one_s=dma((2,)),
        one_r=dma((2,)),
        lo_s=dma((2,)),
        lo_r=dma((2,)),
        c_s=dma((1 + n_off,)),
        c_r=dma((4 + n_off,)),
        x_s=dma((1 + n_off,)),
        x_r=dma(((2 + n_off) * n_cut, max(nx - 1, 1))),
        s_s=dma((n_off,)),
        s_r=dma((n_off,)),
        z_s=dma((n_off,)),
        z_r=dma((n_off, n_cut)),
        gx_r=dma((n_cut, max(nx - 1, 1))),
        h_r=dma((2,)),
    )
    names = (*args, "out", *scratch)
    merged_map = pl.pallas_call(
        functools.partial(kernel, dims, names),
        out_shape=jax.ShapeDtypeStruct((mb, rows, cols, dec), BF16),
        in_specs=[pl.BlockSpec(memory_space=pltpu.HBM)] * len(args),
        out_specs=pl.BlockSpec(memory_space=pltpu.VMEM),
        scratch_shapes=list(scratch.values()),
        compiler_params=pltpu.CompilerParams(
            collective_id=0, has_side_effects=True, vmem_limit_bytes=48 * 1024 * 1024
        ),
    )(*[pltpu.with_memory_space_constraint(a, pltpu.HBM) for a in args.values()])
    return jnp.maximum(merged_map, jnp.zeros_like(merged_map))


def solution(mesh):
    in_specs = (
        P("grp", "band", None, "sect"),
        P("grp", "band", None, None),
        P("grp", "band"),
        P("sect", None),
        P(None, None, None, "sect", None),
        P(),
        P("sect", None),
        P(),
        P(),
        P(),
        P(),
        P(),
        P(),
        P(),
    )
    out_specs = P("grp", "band", None, None)
    return jax.shard_map(shards, mesh=mesh, in_specs=in_specs, out_specs=out_specs, check_vma=False)
```

```python
import functools
import types

import jax
import jax.numpy as jnp
from jax import lax
from jax.experimental import pallas as pl
from jax.experimental.pallas import tpu as pltpu
from jax.sharding import PartitionSpec as P

DILATIONS = (12, 24, 36)
LAND_BLOCK = 6
LAND_MOST = 4
MESH = pl.DeviceIdType.MESH
F32 = jnp.float32
BF16 = jnp.bfloat16
ORDER = (0, 3, 2, 1)


def offsets(rows, bands):
    off = []
    for k in (1, 2, 3):
        d = DILATIONS[k - 1]
        assert d % rows == 0
        hop = d // rows
        if hop < bands:
            off.append((k, 0, hop))
            off.append((k, 2, hop))
    return off


def off_slots(off, bands):
    slots = []
    for n, (k, i, hop) in enumerate(off):
        shared = n and off[n - 1][0] == k and 2 * hop >= bands
        slots.append(slots[-1] if shared else (slots[-1] + 1 if slots else 0))
    return slots


def pieces(live):
    inner = live - 2
    cuts = [(0, 2)]
    if inner > 1:
        cuts += [(2, inner - inner // 2), (live - inner // 2, inner // 2)]
    elif inner:
        cuts.append((2, inner))
    return cuts


def kernel(dims, names, *refs):
    r = types.SimpleNamespace(**dict(zip(names, refs, strict=True)))
    mb, rows, cols, ch, br_w, live, nb, ns, low_w, lowp = dims
    nx = ns // 2
    cs = cols // nx
    off = offsets(rows, nb)
    n_off = len(off)
    cuts = pieces(live)
    n_cut = len(cuts)
    slot_of = off_slots(off, nb)
    need = [(k, 1) for k in ORDER if k] + [(k, i) for k, i, _ in off]
    pad = (r.m_l.shape[1] - cols) // 2
    scope = jax.named_scope

    band = lax.axis_index("band")
    sect = lax.axis_index("sect")
    core = lax.rem(sect, 2)
    xi = lax.div(sect, 2)
    mine, theirs = core, 1 - core
    peer = xi * 2 + 1 - core

    bar = pltpu.get_barrier_semaphore()
    up_ok = band >= 1
    dn_ok = band + 1 < nb

    def hello(b, s):
        pl.semaphore_signal(bar, inc=1, device_id={"band": b, "sect": s}, device_id_type=MESH)

    for e in range(1, ns):
        hello(band, lax.rem(sect + e, ns))
    for ok, step in ((up_ok, -1), (dn_ok, 1)):
        @pl.when(ok)
        def _(step=step):
            hello(band + step, sect)

    waits = {}
    free = list(range(r.loc_sem.shape[0]))

    def fetch(name, *copies, whole):
        sem = r.loc_sem.at[free.pop(0)]
        for src, dst in copies:
            pltpu.make_async_copy(src, dst, sem).start()
        waits[name] = pltpu.make_async_copy(whole, whole, sem)

    def need_now(*which):
        for name in which:
            waits[name].wait()

    def taps_of(k, i):
        return r.wd_h.at[k - 1, i], r.wd.at[need.index((k, i))]

    fetch("mask", (r.mask_h, r.mask), whole=r.mask)
    fetch("theirs", (r.feat_h.at[theirs], r.feat.at[0]), whole=r.feat.at[0])
    fetch("w1", (r.w1_h, r.w1), whole=r.w1)
    fetch("mine", (r.feat_h.at[mine], r.feat_own), whole=r.feat_own)
    if n_off:
        fetch("off", *[taps_of(*n) for n in need[3:]], whole=r.wd.at[pl.ds(3, n_off)])
    def pass_on(sem, step, ok):
        @pl.when(jnp.logical_and(jnp.logical_and(up_ok, dn_ok), ok))
        def _():
            pl.semaphore_signal(
                sem, inc=1, device_id={"band": band + step, "sect": sect}, device_id_type=MESH
            )

    def word_from(sem, ok):
        @pl.when(ok)
        def _():
            pl.semaphore_wait(sem, 1)

    def rcopy(src, dst, s, rs, **where):
        return pltpu.make_async_remote_copy(
            src_ref=src, dst_ref=dst, send_sem=s, recv_sem=rs, device_id=where, device_id_type=MESH
        )

    low_up = rcopy(
        r.low_h.at[mine, 0], r.low_halo.at[1], r.lo_s.at[0], r.lo_r.at[1], band=band - 1, sect=sect
    )
    low_dn = rcopy(
        r.low_h.at[mine, rows - 1], r.low_halo.at[0], r.lo_s.at[1], r.lo_r.at[0],
        band=band + 1, sect=sect,
    )

    def slots(m):
        on = [r.mask[m, y] for y in range(rows)]
        place_of = [0] + [None] * (rows - 2) + [1]
        row_of = [0, rows - 1] + [jnp.int32(0)] * (live - 2)
        hits = {}
        count = jnp.int32(0)
        for y in range(1, rows - 1):
            place_of[y] = jnp.where(on[y] > 0, jnp.minimum(count + 2, live - 1), 0)
            for p in range(2, live):
                hit = jnp.logical_and(on[y] > 0, count == p - 2)
                row_of[p] = jnp.where(hit, y, row_of[p])
                hits[p, y] = jnp.where(hit, 1, 0)
            count = count + on[y]
        return on, place_of, row_of, hits

    for ref in (r.m_l, r.m_r):
        zero = jnp.zeros((ref.shape[0], pad, br_w), F32)
        ref[:, :pad] = zero
        ref[:, pad + cols :] = zero
    for at in (0, rows + 1):
        r.joined[at] = jnp.zeros((cols, br_w), BF16)

    def taps(lhs, n, wref, d):
        mid = jnp.dot(lhs, wref[1], preferred_element_type=F32).reshape(n, cols, br_w)
        r.m_l[:n, pl.ds(pad, cols)] = jnp.dot(
            lhs, wref[0], preferred_element_type=F32
        ).reshape(n, cols, br_w)
        r.m_r[:n, pl.ds(pad, cols)] = jnp.dot(
            lhs, wref[2], preferred_element_type=F32
        ).reshape(n, cols, br_w)
        return mid + r.m_l[:n, pl.ds(pad - d, cols)] + r.m_r[:n, pl.ds(pad + d, cols)]

    def core_copy(t):
        if t < 4:
            src, dst = r.part_own.at[t, 0], r.crecv_own.at[t]
        else:
            src, dst = r.part_off.at[slot_of[t - 4], 0], r.crecv_off.at[slot_of[t - 4]]
        return rcopy(src, dst, r.c_s.at[0 if t < 4 else 1 + slot_of[t - 4]], r.c_r.at[t if t < 4 else 4 + slot_of[t - 4]], sect=peer)

    def run_of(t, g):
        return cuts[g]

    def x_copy(t, g, e, incoming=False):
        lo, n = run_of(t, g)
        at = g * 2 + t // 3 if t < 4 else (2 + slot_of[t - 4]) * n_cut + g
        send, recv, u = (
            (r.xsend_own, r.xrecv_own, t) if t < 4 else (r.xsend_off, r.xrecv_off, slot_of[t - 4])
        )
        other = lax.rem(xi + e, nx)
        slot = other if incoming else xi
        return rcopy(
            send.at[u, other, pl.ds(lo, n)], recv.at[u, slot, pl.ds(lo, n)],
            r.x_s.at[0 if t < 4 else 1 + slot_of[t - 4]], r.x_r.at[at, (e if incoming else nx - e) - 1],
            sect=other * 2 + core,
        )

    def x_arrived(g):
        for e in range(1, nx):
            whole = r.xrecv_own.at[pl.ds(0, 3), lax.rem(xi + e, nx), pl.ds(*cuts[g])]
            arrived(whole, r.x_r.at[g * 2, e - 1])

    def send_x(t, g):
        for e in range(1, nx):
            x_copy(t, g, e).start()

    def first(t, step):
        image = r.feat.at[0] if step == 0 else r.feat_own
        if t < 4:
            k = ORDER[t]
            row_of = facts[step][2]
            lhs = jnp.concatenate([image[row_of[p]] for p in range(live)], axis=0)
            if k:
                val = taps(lhs, live, r.wd.at[need.index((k, 1))], DILATIONS[k - 1])
            else:
                val = jnp.dot(lhs, r.w1[...], preferred_element_type=F32).reshape(live, cols, br_w)
            r.part_own[t, step] = val.astype(BF16)
        else:
            k, i, _ = off[t - 4]
            lhs = image[...].reshape(rows * cols, ch)
            val = taps(lhs, rows, r.wd.at[need.index((k, i))], DILATIONS[k - 1])
            r.part_off[slot_of[t - 4], step] = val.astype(BF16)

    def second(t):
        core_copy(t).wait_recv()
        for c in range(nx):
            cell = pl.ds(c * cs, cs)
            total = r.part_own[t, 1, :, cell].astype(F32) + r.crecv_own[t, :, cell].astype(F32)
            r.xsend_own[t, c] = total.astype(BF16)

            @pl.when(xi == c)
            def _(total=total):
                r.keep_own[t] = total

    def second_off(t, h):
        u = slot_of[t - 4]
        if h == 0:
            core_copy(t).wait_recv()
        elif h == 1:
            sel_copy(t).wait_recv()
        lo, n = cuts[h]
        for c in range(nx):
            cell = pl.ds(c * cs, cs)

            def row(y, cell=cell):
                return r.part_off[u, 1, y, cell].astype(F32) + r.crecv_off[u, y, cell].astype(F32)

            if h == 0:
                picked = [row(0), row(rows - 1)]
            else:
                inner = [row(y) for y in range(1, rows - 1)]
                picked = []
                for p in range(lo, lo + n):
                    total = jnp.zeros((cs, br_w), F32)
                    for y in range(1, rows - 1):
                        at = (p - 2) * (rows - 2) + y - 1
                        total = total + inner[y - 1] * r.sel_in[u, at : at + 1]
                    picked.append(total)
            for p, total in enumerate(picked):
                r.xsend_off[u, c, lo + p] = total.astype(BF16)

            @pl.when(xi == c)
            def _(picked=picked):
                for p, total in enumerate(picked):
                    r.keep_off[u, lo + p] = total

    def sends_to(t):
        k, i, hop = off[t - 4]
        return band + hop < nb if i == 0 else band - hop >= 0

    def gets_from(t):
        k, i, hop = off[t - 4]
        return band - hop >= 0 if i == 0 else band + hop < nb

    def sel_copy(t):
        k, i, hop = off[t - 4]
        return rcopy(
            r.sel_out, r.sel_in.at[slot_of[t - 4]], r.s_s.at[slot_of[t - 4]], r.s_r.at[slot_of[t - 4]],
            band=band - hop if i == 0 else band + hop, sect=sect,
        )

    def z_copy(t, h):
        k, i, hop = off[t - 4]
        run = pl.ds(*cuts[h])
        return rcopy(
            r.zsend.at[slot_of[t - 4], run], r.zrecv.at[slot_of[t - 4], run], r.z_s.at[slot_of[t - 4]], r.z_r.at[slot_of[t - 4], h],
            band=band + hop if i == 0 else band - hop, sect=sect,
        )

    def forward_off(t, h):
        run = pl.ds(*cuts[h])
        total = r.keep_off[slot_of[t - 4], run]
        for e in range(1, nx):
            x_copy(t, h, e, True).wait_recv()
            total = total + r.xrecv_off[slot_of[t - 4], lax.rem(xi + e, nx), run].astype(F32)
        r.zsend[slot_of[t - 4], run] = total.astype(BF16)
        z_copy(t, h).start()

    def for_off(fn, *rest):
        for t in range(4, 4 + n_off):
            @pl.when(sends_to(t))
            def _(t=t):
                fn(t, *rest)

    def pool_sect(e, incoming=False):
        other = lax.rem(sect + e, ns)
        slot = other if incoming else sect
        return rcopy(
            r.pool_s.at[sect], r.pool_s.at[slot], r.one_s.at[0], r.one_r.at[0], sect=other
        )

    def pool_band(e, incoming=False):
        other = lax.rem(band + e, nb)
        slot = other if incoming else band
        return rcopy(
            r.pool_b.at[band], r.pool_b.at[slot], r.one_s.at[1], r.one_r.at[1], band=other
        )

    def dot_f32(v, w):
        n = v.shape[0]
        high = v.astype(BF16).astype(F32)
        middle = (v - high).astype(BF16).astype(F32)
        terms = jnp.concatenate([high, middle, v - high - middle], axis=0).astype(BF16)
        p = jnp.dot(terms, w, preferred_element_type=F32)
        return p[:n] + p[n : 2 * n] + p[2 * n :]

    def all_of(ref, n):
        return ref.at[pl.ds(0, n)]

    def arrived(whole, sem):
        pltpu.make_async_copy(whole, whole, sem).wait()

    def pool():
        need_now("wpool")
        ones = jnp.ones((8, rows * cols), BF16)
        at = lax.broadcasted_iota(jnp.int32, (8, ch), 0)
        sums = jnp.zeros((8, ch), F32)
        for m, image in ((mine, r.feat_own), (theirs, r.feat.at[0])):
            part = jnp.dot(
                ones, image[...].reshape(rows * cols, ch), preferred_element_type=F32
            )
            sums = jnp.where(at == m, part, sums)
        r.pool_s[sect] = dot_f32(sums, r.wpool[...])[:mb]
        for e in range(1, ns):
            pool_sect(e).start()

    need_now("mask")
    facts = [slots(theirs), slots(mine)]
    on, place_of, row_of, hits = facts[1]

    for p in range(2, live):
        for y in range(1, rows - 1):
            at = (p - 2) * (rows - 2) + y - 1
            r.sel_out[at : at + 1] = jnp.full((1, br_w), hits[p, y].astype(F32))

    def own_half(t, step):
        with scope(f"first{t}{'ab'[step]}"):
            first(t, step)
        if step == 0:
            core_copy(t).start()

    def off_theirs(t):
        first(t, 0)
        core_copy(t).start()

    def off_send(t, h):
        second_off(t, h)
        send_x(t, h)

    with scope("w0"):
        need_now("theirs", "w1")
    free[:0] = range(3)
    fetch("wpool", (r.wpool_h, r.wpool), whole=r.wpool)
    fetch("taps", *[taps_of(*n) for n in need[:3]], whole=r.wd.at[pl.ds(0, 3)])
    fetch("low", (r.low_h.at[mine], r.low), whole=r.low)
    fetch("wr", (r.wr_h, r.wr), whole=r.wr)
    fetch("br", (r.br_h, r.br), whole=r.br)
    fetch("wml", (r.wm_h.at[:, :, pl.ds(br_w, lowp)], r.wml), whole=r.wml)
    fetch(
        "vec", (r.bm_h, r.vec.at[0]), (r.bpool_h, r.vec.at[1]), (r.bproj_h, r.vec.at[2]),
        whole=r.vec,
    )
    with scope("first0a"):
        first(0, 0)
    with scope("bar"):
        sides = jnp.minimum(band, 1) + jnp.minimum(nb - 1 - band, 1)
        pl.semaphore_wait(bar, (ns - 1) + sides)
    core_copy(0).start()
    for e in range(1, nx):
        pl.semaphore_signal(
            r.across, inc=1, device_id={"sect": lax.rem(sect + 2 * e, ns)}, device_id_type=MESH
        )
    pass_on(r.above, 1, band < 2)
    pass_on(r.below, -1, band + 2 >= nb)

    def tell(i, ok):
        for t in range(4, 4 + n_off):
            if off[t - 4][1] == i:
                @pl.when(jnp.logical_and(gets_from(t), ok))
                def _(t=t):
                    sel_copy(t).start()

    @pl.when(up_ok)
    def _():
        low_up.start()

    @pl.when(dn_ok)
    def _():
        low_dn.start()

    need_now("mine")
    own_half(0, 1)
    if n_off:
        need_now("off")
    with scope("offa"):
        for_off(off_theirs)
    free[:0] = [3, 4] if n_off else [3]
    fetch("wproj", (r.wproj_h, r.wproj), whole=r.wproj)
    fetch("bbr", (r.bbr_h, r.bbr), whole=r.bbr)
    fetch(
        "wmp",
        *[
            (r.wm_h.at[i, j, pl.ds(0, br_w)], r.wmp.at[j, pl.ds(i * br_w, br_w)])
            for i in range(3) for j in range(3)
        ],
        whole=r.wmp,
    )
    with scope("second0"):
        second(0)
    send_x(0, 0)
    with scope("p1"):
        word_from(r.above, band >= 2)
    pass_on(r.above, 1, band >= 2)
    tell(0, band >= 0)
    with scope("pool"):
        pool()
    with scope("p2"):
        word_from(r.below, jnp.logical_and(up_ok, band + 2 < nb))
    pass_on(r.below, -1, band + 2 < nb)
    tell(2, up_ok)
    with scope("offb"):
        for_off(first, 1)
    with scope("offs0"):
        for_off(off_send, 0)
    for g in range(1, n_cut):
        send_x(0, g)
    need_now("taps")
    own_half(1, 0)
    own_half(2, 0)
    with scope("p3"):
        word_from(r.below, jnp.logical_and(jnp.logical_not(up_ok), band + 2 < nb))
    tell(2, jnp.logical_not(up_ok))
    own_half(1, 1)
    with scope("second1"):
        second(1)
    for g in range(n_cut):
        send_x(1, g)
    own_half(3, 0)
    own_half(2, 1)
    with scope("poolb"):
        arrived(all_of(r.pool_s, ns - 1), r.one_r.at[0])
        total = r.pool_s[0]
        for s in range(1, ns):
            total = total + r.pool_s[s]
        r.pool_b[band] = total
    for e in range(1, nb):
        pool_band(e).start()
    with scope("second2"):
        second(2)
    own_half(3, 1)
    with scope("offs1"):
        for g in range(1, n_cut):
            for_off(off_send, g)
    send_x(2, 0)
    with scope("second3"):
        second(3)
    send_x(3, 0)
    for t in (2, 3):
        for g in range(1, n_cut):
            send_x(t, g)
    with scope("fwd0"):
        for_off(forward_off, 0)

    with scope("low"):
        need_now("low", "wr", "br", "wml", "vec")

        def reduced(v):
            return jax.nn.relu(
                lax.dot_general(
                    v, r.wr[...], (((1,), (1,)), ((), ())), preferred_element_type=F32
                )
                + r.br[...]
            ).astype(BF16)

        r.lowred[1 : rows + 1] = reduced(r.low[...].reshape(rows * cols, low_w)).reshape(
            rows, cols, lowp
        )
        for side, at, ok, copy in ((0, 0, up_ok, low_dn), (1, rows + 1, dn_ok, low_up)):
            @pl.when(ok)
            def _(side=side, at=at, copy=copy):
                copy.wait_recv()
                r.lowred[at] = reduced(r.low_halo[side])

            @pl.when(jnp.logical_not(ok))
            def _(at=at):
                r.lowred[at] = jnp.zeros((cols, lowp), BF16)

    def combine(mid, left, right, n):
        r.m_l[:n, pl.ds(pad, cols)] = left.reshape(n, cols, br_w)
        r.m_r[:n, pl.ds(pad, cols)] = right.reshape(n, cols, br_w)
        return (
            mid.reshape(n, cols, br_w)
            + r.m_l[:n, pl.ds(pad - 1, cols)]
            + r.m_r[:n, pl.ds(pad + 1, cols)]
        )

    with scope("lowconv"):
        terms = [None] * 3
        for i in range(3):
            lhs = jnp.concatenate([r.lowred[row_of[p] + i] for p in range(live)], axis=0)
            for j in range(3):
                term = jnp.dot(lhs, r.wml[i, j], preferred_element_type=F32)
                terms[j] = term if i == 0 else terms[j] + term
        r.lowacc[...] = combine(terms[1], terms[0], terms[2], live) + r.vec[0].reshape(1, 1, br_w)

    for g in range(1, n_cut):
        with scope(f"fwd{g}"):
            for_off(forward_off, g)

    need_now("wproj", "bbr")
    with scope("ctx"):
        if nb > 1:
            arrived(all_of(r.pool_b, nb - 1), r.one_r.at[1])
        total = r.pool_b[0]
        for b in range(1, nb):
            total = total + r.pool_b[b]
        pooled = jax.nn.relu(total / (nb * rows * cols) + r.vec[1])
        context = dot_f32(pooled, r.wproj[4 * br_w :])
        own = context[0:1]
        for m in range(1, mb):
            own = jnp.where(mine == m, context[m : m + 1], own)
        base = own + r.vec[2]

    def branch(t, g):
        lo, n = cuts[g]
        k = ORDER[t]
        with scope(f"x{t}{g}"):
            if t == 0:
                x_arrived(g)
            if t == 3:
                for e in range(1, nx):
                    x_copy(t, g, e, True).wait_recv()
        for u in range(4, 4 + n_off):
            if off[u - 4][0] == k:
                @pl.when(gets_from(u))
                def _(u=u):
                    with scope(f"z{g}"):
                        z_copy(u, g).wait_recv()
                    run = pl.ds(lo, n)
                    r.keep_own[t, run] = r.keep_own[t, run] + r.zrecv[slot_of[u - 4], run].astype(F32)
        total = r.keep_own[t, lo : lo + n]
        for e in range(1, nx):
            total = total + r.xrecv_own[t, lax.rem(xi + e, nx), lo : lo + n].astype(F32)
        total = jax.nn.relu(total + r.bbr[k : k + 1].reshape(1, 1, br_w)).astype(BF16)
        return jnp.dot(
            total.reshape(n * cs, br_w), r.wproj[k * br_w : (k + 1) * br_w],
            preferred_element_type=F32,
        )

    def gather_x(g, e, incoming=False):
        run = pl.ds(*cuts[g])
        other = lax.rem(xi + e, nx)
        slot = other if incoming else xi
        return rcopy(
            r.gath.at[xi, run], r.gath.at[slot, run],
            r.x_s.at[0], r.gx_r.at[g, (e if incoming else nx - e) - 1], sect=other * 2 + core,
        )

    def early(g):
        lo, n = cuts[g]
        acc = branch(0, g)
        for t in (1, 2):
            acc = acc + branch(t, g)
        r.acc[lo : lo + n] = (acc + base).reshape(n, cs, br_w)

    def project(g):
        lo, n = cuts[g]
        last = branch(3, g).reshape(n, cs, br_w)
        done = jax.nn.relu(r.acc[lo : lo + n] + last)
        for p in range(n):
            v = done[p]
            if lo + p < 2:
                v = v * on[(0, rows - 1)[lo + p]].astype(F32)
            r.gath[xi, lo + p] = v.astype(BF16)
        if g == 0:
            if nx > 1:
                pl.semaphore_wait(r.across, nx - 1)
            for e in reversed(range(nx)):
                for side, ok in ((0, dn_ok), (1, up_ok)):
                    @pl.when(ok)
                    def _(side=side, e=e):
                        halo_copy(side, e).start()
        for e in range(1, nx):
            gather_x(g, e).start()

    def halo_copy(side, e):
        other = lax.rem(xi + e, nx)
        return rcopy(
            r.gath.at[xi, 1 - side], r.halo.at[side, xi], r.lo_s.at[1 - side], r.h_r.at[side],
            band=band + 1 if side == 0 else band - 1, sect=other * 2 + core,
        )

    @pl.when(up_ok)
    def _():
        low_up.wait_send()

    @pl.when(dn_ok)
    def _():
        low_dn.wait_send()

    early(0)
    project(0)
    for g in range(1, n_cut):
        early(g)
    for g in range(1, n_cut):
        project(g)
    with scope("ga"):
        for e in range(1, nx):
            gather_x(0, e, True).wait_recv()
    for c in range(nx):
        for p, y in ((0, 0), (1, rows - 1)):
            r.joined[y + 1, pl.ds(c * cs, cs)] = r.gath[c, p]
    need_now("wmp")
    def merge_terms(rows_in, first_tap, taps_in):
        lhs = jnp.concatenate(
            [jnp.concatenate([r.joined[y] for y in ys], axis=0) for ys in rows_in], axis=1
        )
        tap = pl.ds(first_tap * br_w, taps_in * br_w)
        return [jnp.dot(lhs, r.wmp[j, tap], preferred_element_type=F32) for j in range(3)]

    for side, at, ok in ((0, 0, up_ok), (1, rows + 1, dn_ok)):
        @pl.when(ok)
        def _(side=side, at=at):
            with scope("hw"):
                arrived(r.halo.at[side], r.h_r.at[side])
            for c in range(nx):
                r.joined[at, pl.ds(c * cs, cs)] = r.halo[side, c]

    with scope("edge"):
        upper = merge_terms([[0], [1]], 0, 2)
        lower = merge_terms([[rows], [rows + 1]], 1, 2)
        left, mid, right = [jnp.concatenate(p, axis=0) for p in zip(upper, lower)]
        r.lowacc[:2] = r.lowacc[:2] + combine(mid, left, right, 2)
    def merged_copy(lo, n):
        run = pl.ds(lo, n)
        return rcopy(
            r.merged.at[run], r.merged_in.at[run], r.c_s.at[0], r.c_r.at[0], sect=peer
        )

    def finish(lo, n, terms):
        left, mid, right = terms
        total = combine(mid, left, right, n) + r.lowacc[lo : lo + n]
        r.merged[lo : lo + n] = jax.nn.relu(total).astype(BF16)
        merged_copy(lo, n).start()

    def gathered(g):
        with scope(f"gb{g}"):
            for e in range(1, nx):
                gather_x(g, e, True).wait_recv()

    def join(y, c, p):
        r.joined[y + 1, pl.ds(c * cs, cs)] = (
            r.gath[c, p].astype(F32) * on[y].astype(F32)
        ).astype(BF16)

    if n_cut > 1:
        gathered(1)
    for c in range(nx):
        join(1, c, min(2, live - 1))
    with scope("merge0"):
        finish(0, 1, merge_terms([[2]], 2, 1))
    for g in range(2, n_cut):
        gathered(g)
    with scope("join"):
        for y in range(2, rows - 1):
            for c in range(nx):
                join(y, c, place_of[y])
    if live > 2:
        with scope("merge1"):
            inner = range(2, live)
            finish(
                2, live - 2, merge_terms([[row_of[p] + i for p in inner] for i in range(3)], 0, 3)
            )
    with scope("merge2"):
        finish(1, 1, merge_terms([[rows - 1]], 0, 1))

    def spread(image, src, flags, places):
        for y in range(rows):
            r.out[image, y] = (src[places[y]].astype(F32) * flags[y].astype(F32)).astype(BF16)

    with scope("spread"):
        spread(mine, r.merged, on, place_of)
    with scope("ow"):
        arrived(r.merged, r.c_r.at[0])
    with scope("spread2"):
        spread(theirs, r.merged_in, facts[0][0], facts[0][1])

    def off_sent(t):
        u = slot_of[t - 4]
        core_copy(t).wait_send()
        if nx > 1:
            arrived(all_of(r.xsend_off.at[u], nx - 1), r.x_s.at[1 + u])
        arrived(r.zsend.at[u], r.z_s.at[u])

    for t in range(4, 4 + n_off):
        @pl.when(gets_from(t))
        def _(t=t):
            sel_copy(t).wait_send()
    for_off(off_sent)
    arrived(r.part_own.at[:, 0], r.c_s.at[0])
    if nx > 1:
        arrived(r.xsend_own.at[:, pl.ds(0, nx - 1)], r.x_s.at[0])
    arrived(all_of(r.pool_s, ns - 1), r.one_s.at[0])
    if nb > 1:
        arrived(all_of(r.pool_b, nb - 1), r.one_s.at[1])
    for side, ok in ((0, dn_ok), (1, up_ok)):
        @pl.when(ok)
        def _(side=side):
            arrived(r.halo.at[side], r.lo_s.at[1 - side])


def shards(
    features, low_level, land_mask, weight_one, weight_dilated, bias_branch, weight_pool,
    bias_pool, weight_project, bias_project, weight_reduce, bias_reduce, weight_merging,
    bias_merging,
):
    mb, rows, cols, ch = features.shape
    br_w = weight_project.shape[1]
    dec = weight_merging.shape[3]
    low_w, lowp = weight_reduce.shape
    nb, ns = lax.axis_size("band"), lax.axis_size("sect")
    nx = ns // 2
    cs = cols // nx
    assert mb == 2 and ns % 2 == 0 and rows > 2
    live = rows // LAND_BLOCK * LAND_MOST if rows % LAND_BLOCK == 0 else rows
    off = offsets(rows, nb)
    n_off = max(off_slots(off, nb), default=0) + 1
    assert dec == br_w
    n_cut = len(pieces(live))
    n_sel = -(-(live - 2) * (rows - 2) // 8) * 8
    pad = -(-max(DILATIONS) // 8) * 8
    vm, dma = pltpu.VMEM, pltpu.SemaphoreType.DMA
    dims = (mb, rows, cols, ch, br_w, live, nb, ns, low_w, lowp)
    args = dict(
        mask_h=land_mask, feat_h=features, low_h=low_level, w1_h=weight_one, wd_h=weight_dilated,
        bbr_h=bias_branch, wpool_h=weight_pool, bpool_h=bias_pool.reshape(1, -1),
        wproj_h=weight_project, bproj_h=bias_project.reshape(1, -1), wr_h=weight_reduce.T,
        br_h=bias_reduce.reshape(1, -1), wm_h=weight_merging, bm_h=bias_merging.reshape(1, -1),
    )
    scratch = dict(
        mask=pltpu.SMEM(land_mask.shape, jnp.int32),
        feat=vm((1, rows, cols, ch), BF16),
        feat_own=vm((rows, cols, ch), BF16),
        low=vm((rows, cols, low_w), BF16),
        low_halo=vm((2, cols, low_w), BF16),
        w1=vm(weight_one.shape, BF16),
        wpool=vm(weight_pool.shape, BF16),
        sel_out=vm((n_sel, br_w), F32),
        sel_in=vm((n_off, n_sel, br_w), F32),
        wd=vm((3 + len(off), 3, ch, br_w), BF16),
        wproj=vm(weight_project.shape, BF16),
        wmp=vm((3, 3 * br_w, dec), BF16),
        wml=vm((3, 3, lowp, dec), BF16),
        wr=vm((lowp, low_w), BF16),
        br=vm((1, lowp), F32),
        vec=vm((3, 1, br_w), F32),
        bbr=vm(bias_branch.shape, F32),
        m_l=vm((rows, cols + 2 * pad, br_w), F32),
        m_r=vm((rows, cols + 2 * pad, br_w), F32),
        part_off=vm((n_off, 2, rows, cols, br_w), BF16),
        crecv_off=vm((n_off, rows, cols, br_w), BF16),
        xsend_off=vm((n_off, nx, live, cs, br_w), BF16),
        xrecv_off=vm((n_off, nx, live, cs, br_w), BF16),
        zsend=vm((n_off, live, cs, br_w), BF16),
        zrecv=vm((n_off, live, cs, br_w), BF16),
        keep_off=vm((n_off, live, cs, br_w), F32),
        part_own=vm((5, 2, live, cols, br_w), BF16),
        crecv_own=vm((4, live, cols, br_w), BF16),
        xsend_own=vm((5, nx, live, cs, br_w), BF16),
        xrecv_own=vm((4, nx, live, cs, br_w), BF16),
        keep_own=vm((4, live, cs, br_w), F32),
        acc=vm((live, cs, br_w), F32),
        pool_s=vm((ns, mb, br_w), F32),
        pool_b=vm((nb, mb, br_w), F32),
        gath=vm((nx, live, cs, br_w), BF16),
        halo=vm((2, nx, cs, br_w), BF16),
        joined=vm((rows + 2, cols, br_w), BF16),
        lowred=vm((rows + 2, cols, lowp), BF16),
        lowacc=vm((live, cols, dec), F32),
        merged=vm((live, cols, dec), BF16),
        merged_in=vm((live, cols, dec), BF16),
        across=pltpu.SemaphoreType.REGULAR,
        above=pltpu.SemaphoreType.REGULAR,
        below=pltpu.SemaphoreType.REGULAR,
        loc_sem=dma((10,)),
        one_s=dma((2,)),
        one_r=dma((2,)),
        lo_s=dma((2,)),
        lo_r=dma((2,)),
        c_s=dma((1 + n_off,)),
        c_r=dma((4 + n_off,)),
        x_s=dma((1 + n_off,)),
        x_r=dma(((2 + n_off) * n_cut, max(nx - 1, 1))),
        s_s=dma((n_off,)),
        s_r=dma((n_off,)),
        z_s=dma((n_off,)),
        z_r=dma((n_off, n_cut)),
        gx_r=dma((n_cut, max(nx - 1, 1))),
        h_r=dma((2,)),
    )
    names = (*args, "out", *scratch)
    merged_map = pl.pallas_call(
        functools.partial(kernel, dims, names),
        out_shape=jax.ShapeDtypeStruct((mb, rows, cols, dec), BF16),
        in_specs=[pl.BlockSpec(memory_space=pltpu.HBM)] * len(args),
        out_specs=pl.BlockSpec(memory_space=pltpu.VMEM),
        scratch_shapes=list(scratch.values()),
        compiler_params=pltpu.CompilerParams(
            collective_id=0, has_side_effects=True, vmem_limit_bytes=48 * 1024 * 1024
        ),
    )(*[pltpu.with_memory_space_constraint(a, pltpu.HBM) for a in args.values()])
    return jnp.maximum(merged_map, jnp.zeros_like(merged_map))


def solution(mesh):
    in_specs = (
        P("grp", "band", None, "sect"),
        P("grp", "band", None, None),
        P("grp", "band"),
        P("sect", None),
        P(None, None, None, "sect", None),
        P(),
        P("sect", None),
        P(),
        P(),
        P(),
        P(),
        P(),
        P(),
        P(),
    )
    out_specs = P("grp", "band", None, None)
    return jax.shard_map(shards, mesh=mesh, in_specs=in_specs, out_specs=out_specs, check_vma=False)
```
